32 devices in a mesh: seq: 2 (over x), dp: 16 (over z, y, core).
Axes of the slice: x: 2, y: 2, z: 4, core: 2. Of those that a mesh axis runs over, the one named last changes fastest.
Arguments:
- tokens: bfloat16 [16, 1024, 768], P('dp', 'seq'), may hold values from -6 to 6
- timesteps: int32 [16], P('dp'), may hold values from 0 to 999
- starts: int32 [16, 2], P('dp'), may hold values from 0 to 768, as said below
- cotangent: bfloat16 [16, 1024, 768], P('dp', 'seq'), may hold values from -6 to 6
- ln1_gain: bfloat16 [768], P(('seq', 'dp')), may hold values from 0.099609375 to 1.8984375
- ln1_bias: bfloat16 [768], P(('seq', 'dp')), may hold values from -3 to 3
- w_qkv: bfloat16 [768, 2304], P(('seq', 'dp')), may hold values from -0.21875 to 0.21875
- bias_query: bfloat16 [768], P(('seq', 'dp')), may hold values from -3 to 3
- bias_value: bfloat16 [768], P(('seq', 'dp')), may hold values from -3 to 3
- w_out: bfloat16 [768, 768], P(('seq', 'dp')), may hold values from -3 to 3
- bias_out: bfloat16 [768], P(('seq', 'dp')), may hold values from -3 to 3
- ln2_gain: bfloat16 [768], P(('seq', 'dp')), may hold values from 0.099609375 to 1.8984375
- ln2_bias: bfloat16 [768], P(('seq', 'dp')), may hold values from -3 to 3
- w_up: bfloat16 [768, 3072], P(('seq', 'dp')), may hold values from -0.21875 to 0.21875
- bias_up: bfloat16 [3072], P(('seq', 'dp')), may hold values from -3 to 3
- w_down: bfloat16 [3072, 768], P(('seq', 'dp')), may hold values from -0.109375 to 0.109375
- bias_down: bfloat16 [768], P(('seq', 'dp')), may hold values from -3 to 3
- time_table: bfloat16 [1000, 768], P(None, ('seq', 'dp')), may hold values from -6 to 6
Outputs:
- block_out: bfloat16 [16, 1024, 768], P('dp', 'seq')
- grad_tokens: bfloat16 [16, 1024, 768], P('dp', 'seq')
- grad_ln1_gain: float32 [768], P(('seq', 'dp'))
- grad_ln1_bias: float32 [768], P(('seq', 'dp'))
- grad_w_qkv: float32 [768, 2304], P(('seq', 'dp'))
- grad_bias_query: float32 [768], P(('seq', 'dp'))
- grad_bias_value: float32 [768], P(('seq', 'dp'))
- grad_w_out: float32 [768, 768], P(('seq', 'dp'))
- grad_bias_out: float32 [768], P(('seq', 'dp'))
- grad_ln2_gain: float32 [768], P(('seq', 'dp'))
- grad_ln2_bias: float32 [768], P(('seq', 'dp'))
- grad_w_up: float32 [768, 3072], P(('seq', 'dp'))
- grad_bias_up: float32 [3072], P(('seq', 'dp'))
- grad_w_down: float32 [3072, 768], P(('seq', 'dp'))
- grad_bias_down: float32 [768], P(('seq', 'dp'))
- grad_time_table: float32 [1000, 768], P(None, ('seq', 'dp'))
The draws below stay inside these ranges and needn't reach their ends.
Inputs may be any that keep to these rules, and one draw needn't show every extreme that they name: The 2 pieces of a sequence do not intersect; piece k starts in positions k * 512 to (k + 1) * 512 - 256.
All inputs are finite; a program needn't handle non-finite values.
Results may differ from the reference program's by a relative error of at most 0.035.
Values may be sent and summed in bfloat16 or wider, within the bound.
No kernel may reach another device: no remote copies, remote signals or barrier semaphores. Data moves between devices by JAX's collectives and lax.ppermute only.
A program may use at most 192 MiB of HBM per device.

```python
import jax
import jax.numpy as jnp
from jax import lax

D = 768
HEADS = 12
HD = 64
FF = 3072
TSTEPS = 1000
LEN = 1024
PIC = 256
NPIC = 2
SEQS = 16


def draw_starts(key, part):
    region = LEN // NPIC
    offsets = jax.random.randint(key, (SEQS, NPIC), 0, region - PIC + 1)
    return (offsets + jnp.arange(NPIC, dtype=jnp.int32)[None, :] * region).astype(jnp.int32)


def place_ends(values, own_key, least, largest):
    longest = values.shape.index(max(values.shape))
    spots = []
    for shift in (0, 1):
        where = [jax.random.randint(jax.random.fold_in(own_key, axis), (), 0, length) for axis, length in enumerate(values.shape)]
        where[longest] = (where[longest] + shift) % values.shape[longest]
        spots.append(tuple(where))
    return values.at[spots[0]].set(least).at[spots[1]].set(largest)


def block_levels(rng, dims, pieces, low, largest):
    loudness = 1.0
    for dim, blocks in pieces:
        draws = jax.random.uniform(jax.random.fold_in(jax.random.fold_in(rng, 6), dim), (blocks,), jnp.float32, low / len(pieces), largest / len(pieces))
        loudness = loudness * jnp.repeat(jnp.exp(draws), dims[dim] // blocks).reshape((-1,) + (1,) * (len(dims) - 1 - dim))
    return loudness


def scatter_about(own_key, extent, width, most, pieces=(), kind=jnp.bfloat16):
    values = width * jax.random.normal(own_key, extent, jnp.float32)
    if pieces:
        values = values * block_levels(own_key, extent, pieces, -0.22, 0.18)
    return jnp.clip(values, -most, most).astype(kind)


def setup_inputs(seed: int = 0) -> dict:
    seeds = jax.random.split(jax.random.key(seed), 19)
    tokens = scatter_about(seeds[0], (SEQS, LEN, D), 1.0, 6.0, ((0, 16), (1, 2)))
    timesteps = place_ends(jax.random.randint(seeds[1], (SEQS,), 0, TSTEPS), jax.random.fold_in(seeds[1], 1), 0, TSTEPS - 1).astype(jnp.int32)
    starts = draw_starts(jax.random.fold_in(seeds[18], 71), 0)
    cotangent = scatter_about(seeds[3], (SEQS, LEN, D), 1.0, 6.0, ((0, 16), (1, 2)))
    ln1_gain = jnp.clip(1.0 + 0.18 * jax.random.normal(seeds[4], (D,), jnp.float32), 0.099609375, 1.8984375).astype(jnp.bfloat16)
    ln1_bias = scatter_about(seeds[5], (D,), 0.3, 3.0, ((0, 32),))
    w_qkv = scatter_about(seeds[6], (D, 3 * D), D ** -0.5, 0.21875, ((0, 32),))
    bias_query = scatter_about(seeds[7], (D,), 0.5, 3.0, ((0, 32),))
    bias_value = scatter_about(seeds[8], (D,), 0.5, 3.0, ((0, 32),))
    w_out = scatter_about(seeds[9], (D, D), 4 ** -0.5, 3.0, ((0, 32),))
    bias_out = scatter_about(seeds[10], (D,), 0.5, 3.0, ((0, 32),))
    ln2_gain = jnp.clip(1.0 + 0.18 * jax.random.normal(seeds[11], (D,), jnp.float32), 0.099609375, 1.8984375).astype(jnp.bfloat16)
    ln2_bias = scatter_about(seeds[12], (D,), 0.3, 3.0, ((0, 32),))
    w_up = scatter_about(seeds[13], (D, FF), D ** -0.5, 0.21875, ((0, 32),))
    bias_up = scatter_about(seeds[14], (FF,), 0.5, 3.0, ((0, 32),))
    w_down = scatter_about(seeds[15], (FF, D), FF ** -0.5, 0.109375, ((0, 32),))
    bias_down = scatter_about(seeds[16], (D,), 0.5, 3.0, ((0, 32),))
    time_table = scatter_about(seeds[17], (TSTEPS, D), 1.0, 6.0, ((1, 32),))
    return dict(tokens=tokens, timesteps=timesteps, starts=starts, cotangent=cotangent, ln1_gain=ln1_gain, ln1_bias=ln1_bias, w_qkv=w_qkv, bias_query=bias_query, bias_value=bias_value, w_out=w_out, bias_out=bias_out, ln2_gain=ln2_gain, ln2_bias=ln2_bias, w_up=w_up, bias_up=bias_up, w_down=w_down, bias_down=bias_down, time_table=time_table)


@jax.custom_vjp
def low(v):
    return lax.optimization_barrier(v.astype(jnp.bfloat16)).astype(jnp.float32)

@jax.custom_vjp
def low_back(v):
    return v

def low_keep(v):
    return (low(v), None)

def low_pass(kept, grad):
    return (grad,)

def back_keep(v):
    return (v, None)

def back_low(kept, grad):
    return (low(grad),)
low.defvjp(low_keep, low_pass)
low_back.defvjp(back_keep, back_low)
epsilon = 1e-05
highest = lax.Precision.HIGHEST

def layer_norm(values, gain, shift):
    average = lax.optimization_barrier(jnp.mean(values, axis=-1, keepdims=True))
    centred = values - average
    spread = lax.optimization_barrier(jnp.mean(centred * centred, axis=-1, keepdims=True))
    return centred * lax.rsqrt(spread + epsilon) * gain + shift

def piece_label(starts, places):
    inside = (places[None, None, :] >= starts[:, :, None]) & (places[None, None, :] < starts[:, :, None] + PIC)
    number = jnp.arange(1, NPIC + 1, dtype=jnp.int32)
    return lax.optimization_barrier(jnp.sum(inside.astype(jnp.int32) * number[None, :, None], axis=1))

def visible(starts):
    places = jnp.arange(LEN, dtype=jnp.int32)
    labels = piece_label(starts, places)
    causal = places[:, None] >= places[None, :]
    same = (labels[:, :, None] == labels[:, None, :]) & (labels[:, :, None] > 0)
    return causal[None] | same

def project(left, right):
    return jnp.einsum('gld,de->gle', left, right, precision=highest)

def block(inputs, embed, allowed, weights):
    gain_one, shift_one, qkv_w, query_b, value_b, out_w, out_b, gain_two, shift_two, up_w, up_b, down_w, down_b = weights
    group_size = inputs.shape[0]
    start_sum = inputs + embed[:, None, :]
    normed_one = low(layer_norm(start_sum, gain_one, shift_one))
    joined = project(normed_one, qkv_w)
    query = low(low_back(joined[..., :D] + query_b))
    keys = low(low_back(joined[..., D:2 * D]))
    values = low(low_back(joined[..., 2 * D:] + value_b))
    query = query.reshape(group_size, LEN, HEADS, HD)
    keys = keys.reshape(group_size, LEN, HEADS, HD)
    values = values.reshape(group_size, LEN, HEADS, HD)
    scores = low_back(HD ** (-0.5) * jnp.einsum('gqhe,gkhe->ghqk', query, keys, precision=highest))
    scores = jnp.where(allowed[:, None], scores, -1e+30)
    probs = jax.nn.softmax(scores, axis=-1)
    heads_out = jnp.einsum('ghqk,gkhe->gqhe', low(probs), values, precision=highest)
    heads_out = low(low_back(heads_out.reshape(group_size, LEN, D)))
    mid = start_sum + low_back(project(heads_out, out_w) + out_b)
    normed_two = low(layer_norm(mid, gain_two, shift_two))
    up_pre = low_back(project(normed_two, up_w) + up_b)
    act = low(jax.nn.gelu(up_pre))
    return mid + low_back(project(act, down_w) + down_b)

def reference(tokens, timesteps, starts, cotangent, ln1_gain, ln1_bias, w_qkv, bias_query, bias_value, w_out, bias_out, ln2_gain, ln2_bias, w_up, bias_up, w_down, bias_down, time_table):
    weights = tuple((item.astype(jnp.float32) for item in (ln1_gain, ln1_bias, w_qkv, bias_query, bias_value, w_out, bias_out, ln2_gain, ln2_bias, w_up, bias_up, w_down, bias_down)))
    table = time_table.astype(jnp.float32)
    group_size = 4
    seq_total = tokens.shape[0]
    group_count = seq_total // group_size
    tok_groups = tokens.astype(jnp.float32).reshape(group_count, group_size, LEN, D)
    cot_groups = cotangent.astype(jnp.float32).reshape(group_count, group_size, LEN, D)
    time_groups = timesteps.reshape(group_count, group_size)
    start_groups = starts.reshape(group_count, group_size, NPIC)

    def step(carry, inputs):
        table_acc, weight_acc = carry
        tok_part, time_part, start_part, cot_part = inputs
        allowed = visible(start_part)

        def forward(tok_value, table_value, weight_value):
            return block(tok_value, table_value[time_part], allowed, weight_value)
        result, pull = jax.vjp(forward, tok_part, table, weights)
        grad_tok, grad_table, grad_weights = pull(cot_part)
        new_weights = jax.tree.map(lambda left, right: left + right, weight_acc, grad_weights)
        return ((table_acc + grad_table, new_weights), (result.astype(jnp.bfloat16), grad_tok.astype(jnp.bfloat16)))
    start_carry = (jnp.zeros_like(table), jax.tree.map(jnp.zeros_like, weights))
    (table_grad, weight_grads), (outputs, tok_grads) = lax.scan(step, start_carry, (tok_groups, time_groups, start_groups, cot_groups))
    block_out = outputs.reshape(seq_total, LEN, D)
    grad_tokens = tok_grads.reshape(seq_total, LEN, D)
    return (block_out, grad_tokens, weight_grads[0], weight_grads[1], weight_grads[2], weight_grads[3], weight_grads[4], weight_grads[5], weight_grads[6], weight_grads[7], weight_grads[8], weight_grads[9], weight_grads[10], weight_grads[11], weight_grads[12], table_grad)
```

```python
import jax
import jax.numpy as jnp
from jax import lax
from jax.experimental import pallas as pl
from jax.experimental.pallas import tpu as pltpu
from jax.sharding import PartitionSpec as P

D = 768
HEADS = 12
HD = 64
TSTEPS = 1000
PIC = 256
NPIC = 2


epsilon = 1e-05


def layer_norm(values, gain, shift):
    average = jnp.mean(values, axis=-1, keepdims=True)
    centred = values - average
    spread = jnp.mean(centred * centred, axis=-1, keepdims=True)
    return centred * lax.rsqrt(spread + epsilon) * gain + shift


def piece_label(starts, places):
    inside = (places[None, None, :] >= starts[:, :, None]) & (
        places[None, None, :] < starts[:, :, None] + PIC
    )
    number = jnp.arange(1, NPIC + 1, dtype=jnp.int32)
    return jnp.sum(inside.astype(jnp.int32) * number[None, :, None], axis=1)


def visible_mask(starts, query_pos, key_pos):
    label_query = piece_label(starts, query_pos)
    label_key = piece_label(starts, key_pos)
    causal = query_pos[:, None] >= key_pos[None, :]
    return causal[None] | (label_query[:, :, None] == label_key[:, None, :]) & (
        label_query[:, :, None] > 0
    )


def dense(left, right):
    return jnp.dot(left, right, preferred_element_type=jnp.float32)


def dense_left(left, right):
    return lax.dot_general(
        left, right, (((0,), (0,)), ((), ())), preferred_element_type=jnp.float32
    )


def dense_right(left, right):
    return lax.dot_general(
        left, right, (((1,), (1,)), ((), ())), preferred_element_type=jnp.float32
    )


def head_slice(array, index):
    return lax.dynamic_slice_in_dim(array, index * HD, HD, 2)


def merge_heads(stacked):
    head_count, seq_count, row_count, head_size = stacked.shape
    return jnp.transpose(stacked, (1, 2, 0, 3)).reshape(
        seq_count, row_count, head_count * head_size
    )


def shards(
    tokens,
    timesteps,
    starts,
    cotangent,
    ln1_gain,
    ln1_bias,
    w_qkv,
    bias_query,
    bias_value,
    w_out,
    bias_out,
    ln2_gain,
    ln2_bias,
    w_up,
    bias_up,
    w_down,
    bias_down,
    time_table,
):
    gathered = (
        lax.all_gather(ln1_gain, ("seq", "dp"), axis=0, tiled=True),
        lax.all_gather(ln1_bias, ("seq", "dp"), axis=0, tiled=True),
        lax.all_gather(w_qkv, ("seq", "dp"), axis=0, tiled=True),
        lax.all_gather(bias_query, ("seq", "dp"), axis=0, tiled=True),
        lax.all_gather(bias_value, ("seq", "dp"), axis=0, tiled=True),
        lax.all_gather(w_out, ("seq", "dp"), axis=0, tiled=True),
        lax.all_gather(bias_out, ("seq", "dp"), axis=0, tiled=True),
        lax.all_gather(ln2_gain, ("seq", "dp"), axis=0, tiled=True),
        lax.all_gather(ln2_bias, ("seq", "dp"), axis=0, tiled=True),
        lax.all_gather(w_up, ("seq", "dp"), axis=0, tiled=True),
        lax.all_gather(bias_up, ("seq", "dp"), axis=0, tiled=True),
        lax.all_gather(w_down, ("seq", "dp"), axis=0, tiled=True),
        lax.all_gather(bias_down, ("seq", "dp"), axis=0, tiled=True),
        lax.all_gather(time_table, ("seq", "dp"), axis=1, tiled=True),
    )
    (
        gain_one,
        shift_one,
        qkv_full,
        query_shift,
        value_shift,
        out_full,
        out_shift,
        gain_two,
        shift_two,
        up_full,
        up_shift,
        down_full,
        down_shift,
        table_full,
    ) = gathered
    seq_count, row_count, model_width = tokens.shape
    flat_rows = seq_count * row_count
    scale = HD ** (-0.5)
    levels = jnp.arange(TSTEPS, dtype=jnp.int32)
    onehot = timesteps[:, None] == levels[None, :]
    embed = dense(onehot.astype(jnp.bfloat16), table_full)
    start_sum = (tokens.astype(jnp.float32) + embed[:, None, :]).reshape(flat_rows, model_width)
    norm_one, pull_one = jax.vjp(
        layer_norm, start_sum, gain_one.astype(jnp.float32), shift_one.astype(jnp.float32)
    )
    normed_one = norm_one.astype(jnp.bfloat16)
    joined = dense(normed_one, qkv_full)
    query = (
        (joined[:, :D] + query_shift.astype(jnp.float32))
        .astype(jnp.bfloat16)
        .reshape(seq_count, row_count, D)
    )
    keys = joined[:, D : 2 * D].astype(jnp.bfloat16).reshape(seq_count, row_count, D)
    values = (
        (joined[:, 2 * D :] + value_shift.astype(jnp.float32))
        .astype(jnp.bfloat16)
        .reshape(seq_count, row_count, D)
    )
    key_all, value_all = (
        lax.all_gather(keys, "seq", axis=1, tiled=True),
        lax.all_gather(values, "seq", axis=1, tiled=True),
    )
    full_len = key_all.shape[1]
    query_pos = lax.axis_index("seq") * row_count + jnp.arange(row_count, dtype=jnp.int32)
    every_pos = jnp.arange(full_len, dtype=jnp.int32)
    allowed = visible_mask(starts, query_pos, every_pos)

    def head_forward(index):
        query_head = head_slice(query, index)
        key_head = head_slice(key_all, index)
        value_head = head_slice(value_all, index)
        scores = scale * jnp.einsum(
            "sre,ske->srk", query_head, key_head, preferred_element_type=jnp.float32
        )
        scores = jnp.where(allowed, scores, -1e30)
        top = jnp.max(scores, axis=-1, keepdims=True)
        expo = jnp.exp(scores - top)
        total = jnp.sum(expo, axis=-1, keepdims=True)
        probs = expo / total
        result = jnp.einsum(
            "srk,ske->sre",
            probs.astype(jnp.bfloat16),
            value_head,
            preferred_element_type=jnp.float32,
        )
        return (result, top[..., 0] + jnp.log(total[..., 0]))

    head_out, log_total = lax.map(head_forward, jnp.arange(HEADS, dtype=jnp.int32))
    heads_out = merge_heads(head_out).astype(jnp.bfloat16).reshape(flat_rows, D)
    mid = start_sum + dense(heads_out, out_full) + out_shift.astype(jnp.float32)
    norm_two, pull_two = jax.vjp(
        layer_norm, mid, gain_two.astype(jnp.float32), shift_two.astype(jnp.float32)
    )
    normed_two = norm_two.astype(jnp.bfloat16)
    up_pre = dense(normed_two, up_full) + up_shift.astype(jnp.float32)
    act_value, pull_act = jax.vjp(jax.nn.gelu, up_pre)
    act = act_value.astype(jnp.bfloat16)
    block_out = (mid + dense(act, down_full) + down_shift.astype(jnp.float32)).astype(jnp.bfloat16)
    qkv_back, out_back, up_back, down_back = (
        lax.all_gather(w_qkv, ("seq", "dp"), axis=0, tiled=True),
        lax.all_gather(w_out, ("seq", "dp"), axis=0, tiled=True),
        lax.all_gather(w_up, ("seq", "dp"), axis=0, tiled=True),
        lax.all_gather(w_down, ("seq", "dp"), axis=0, tiled=True),
    )
    grad_mlp = cotangent.reshape(flat_rows, D)
    grad_down = dense_left(act, grad_mlp)
    grad_down_shift = jnp.sum(grad_mlp.astype(jnp.float32), axis=0)
    grad_act = dense_right(grad_mlp, down_back)
    (grad_up_pre,) = pull_act(grad_act)
    grad_up_low = grad_up_pre.astype(jnp.bfloat16)
    grad_up = dense_left(normed_two, grad_up_low)
    grad_up_shift = jnp.sum(grad_up_low.astype(jnp.float32), axis=0)
    grad_norm_two = dense_right(grad_up_low, up_back)
    grad_mid_norm, grad_gain_two, grad_shift_two = pull_two(grad_norm_two)
    grad_mid = cotangent.reshape(flat_rows, D).astype(jnp.float32) + grad_mid_norm
    grad_attn = grad_mid.astype(jnp.bfloat16)
    grad_out_w = dense_left(heads_out, grad_attn)
    grad_out_shift = jnp.sum(grad_attn.astype(jnp.float32), axis=0)
    grad_heads = (
        dense_right(grad_attn, out_back).astype(jnp.bfloat16).reshape(seq_count, row_count, D)
    )
    key_back, value_back = (
        lax.all_gather(keys, "seq", axis=1, tiled=True),
        lax.all_gather(values, "seq", axis=1, tiled=True),
    )

    def query_side(index, log_head):
        query_head = head_slice(query, index)
        key_head = head_slice(key_back, index)
        value_head = head_slice(value_back, index)
        grad_head = head_slice(grad_heads, index)
        scores = scale * jnp.einsum(
            "sre,ske->srk", query_head, key_head, preferred_element_type=jnp.float32
        )
        scores = jnp.where(allowed, scores, -1e30)
        probs = jnp.exp(scores - log_head[..., None])
        grad_probs = jnp.einsum(
            "sre,ske->srk", grad_head, value_head, preferred_element_type=jnp.float32
        )
        delta = jnp.sum(probs * grad_probs, axis=-1, keepdims=True)
        grad_scores = (probs * (grad_probs - delta)).astype(jnp.bfloat16)
        grad_query_head = scale * jnp.einsum(
            "srk,ske->sre", grad_scores, key_head, preferred_element_type=jnp.float32
        )
        return (probs, grad_scores, delta[..., 0], grad_query_head)

    def query_only(inputs):
        index, log_head = inputs
        probs, grad_scores, delta, grad_query_head = query_side(index, log_head)
        return (grad_query_head, delta)

    grad_query_heads, delta_heads = lax.map(
        query_only, (jnp.arange(HEADS, dtype=jnp.int32), log_total)
    )
    query_every, grad_every, log_every, delta_every = (
        lax.all_gather(query, "seq", axis=1, tiled=True),
        lax.all_gather(grad_heads, "seq", axis=1, tiled=True),
        lax.all_gather(log_total.astype(jnp.bfloat16), "seq", axis=2, tiled=True).astype(
            log_total.dtype
        ),
        lax.all_gather(delta_heads.astype(jnp.bfloat16), "seq", axis=2, tiled=True).astype(
            delta_heads.dtype
        ),
    )
    key_allowed = visible_mask(starts, every_pos, query_pos)

    def key_side(inputs):
        index, log_head, delta_head = inputs
        query_head = head_slice(query_every, index)
        grad_head = head_slice(grad_every, index)
        key_head = head_slice(keys, index)
        value_head = head_slice(values, index)
        scores = scale * jnp.einsum(
            "sqe,ske->sqk", query_head, key_head, preferred_element_type=jnp.float32
        )
        scores = jnp.where(key_allowed, scores, -1e30)
        probs = jnp.exp(scores - log_head[..., None])
        grad_probs = jnp.einsum(
            "sqe,ske->sqk", grad_head, value_head, preferred_element_type=jnp.float32
        )
        grad_scores = (probs * (grad_probs - delta_head[..., None])).astype(jnp.bfloat16)
        grad_key_head = scale * jnp.einsum(
            "sqk,sqe->ske", grad_scores, query_head, preferred_element_type=jnp.float32
        )
        grad_value_head = jnp.einsum(
            "sqk,sqe->ske",
            probs.astype(jnp.bfloat16),
            grad_head,
            preferred_element_type=jnp.float32,
        )
        return (grad_key_head, grad_value_head)

    grad_key_heads, grad_value_heads = lax.map(
        key_side, (jnp.arange(HEADS, dtype=jnp.int32), log_every, delta_every)
    )
    grad_key_own = merge_heads(grad_key_heads)
    grad_value_own = merge_heads(grad_value_heads)
    grad_query_low = merge_heads(grad_query_heads).astype(jnp.bfloat16).reshape(flat_rows, D)
    grad_key_low = grad_key_own.astype(jnp.bfloat16).reshape(flat_rows, D)
    grad_value_low = grad_value_own.astype(jnp.bfloat16).reshape(flat_rows, D)
    grad_joined = jnp.concatenate([grad_query_low, grad_key_low, grad_value_low], axis=1)
    grad_qkv = dense_left(normed_one, grad_joined)
    grad_query_shift = jnp.sum(grad_query_low.astype(jnp.float32), axis=0)
    grad_value_shift = jnp.sum(grad_value_low.astype(jnp.float32), axis=0)
    grad_norm_one = dense_right(grad_joined, qkv_back)
    grad_start_norm, grad_gain_one, grad_shift_one = pull_one(grad_norm_one)
    grad_start = grad_mid + grad_start_norm
    grad_tokens = grad_start.astype(jnp.bfloat16).reshape(seq_count, row_count, D)
    seq_sums = jnp.sum(grad_start.reshape(seq_count, row_count, D), axis=1)
    every_sums, every_times = (
        lax.all_gather(seq_sums, ("seq", "dp"), axis=0, tiled=True),
        lax.all_gather(timesteps, ("seq", "dp"), axis=0, tiled=True),
    )
    own_width = D // lax.axis_size(("seq", "dp"))
    own_sums = lax.dynamic_slice_in_dim(
        every_sums, lax.axis_index(("seq", "dp")) * own_width, own_width, 1
    )
    every_onehot = (every_times[None, :] == levels[:, None]).astype(jnp.float32)
    grad_table = jnp.dot(every_onehot, own_sums, precision=lax.Precision.HIGHEST)
    summed = (
        lax.psum_scatter(grad_gain_one, ("seq", "dp"), scatter_dimension=0, tiled=True),
        lax.psum_scatter(grad_shift_one, ("seq", "dp"), scatter_dimension=0, tiled=True),
        lax.psum_scatter(grad_qkv, ("seq", "dp"), scatter_dimension=0, tiled=True),
        lax.psum_scatter(grad_query_shift, ("seq", "dp"), scatter_dimension=0, tiled=True),
        lax.psum_scatter(grad_value_shift, ("seq", "dp"), scatter_dimension=0, tiled=True),
        lax.psum_scatter(grad_out_w, ("seq", "dp"), scatter_dimension=0, tiled=True),
        lax.psum_scatter(grad_out_shift, ("seq", "dp"), scatter_dimension=0, tiled=True),
        lax.psum_scatter(grad_gain_two, ("seq", "dp"), scatter_dimension=0, tiled=True),
        lax.psum_scatter(grad_shift_two, ("seq", "dp"), scatter_dimension=0, tiled=True),
        lax.psum_scatter(grad_up, ("seq", "dp"), scatter_dimension=0, tiled=True),
        lax.psum_scatter(grad_up_shift, ("seq", "dp"), scatter_dimension=0, tiled=True),
        lax.psum_scatter(grad_down, ("seq", "dp"), scatter_dimension=0, tiled=True),
        lax.psum_scatter(grad_down_shift, ("seq", "dp"), scatter_dimension=0, tiled=True),
    )
    return (
        block_out.reshape(seq_count, row_count, D),
        grad_tokens,
        summed[0],
        summed[1],
        summed[2],
        summed[3],
        summed[4],
        summed[5],
        summed[6],
        summed[7],
        summed[8],
        summed[9],
        summed[10],
        summed[11],
        summed[12],
        grad_table,
    )


AXES = ("seq", "dp")
CORE, Y, Z0, Z1, X = 1, 2, 4, 8, 16
DEVICES = 32
QUARTER = 256
ROWS = 512
LEN = 1024


def trade(array, mask):
    return lax.ppermute(array, AXES, [(i, i ^ mask) for i in range(DEVICES)])


def join(bit, own, other, axis):
    return jnp.where(
        bit == 0,
        jnp.concatenate([own, other], axis=axis),
        jnp.concatenate([other, own], axis=axis),
    )


def spot():
    x = lax.axis_index("seq")
    dp = lax.axis_index("dp")
    return x, dp >> 2, (dp >> 1) & 1, dp & 1


def hop_pairs(first):
    pairs = []
    for base in range(0, 16, 2):
        if first:
            moves = (((0, 0), (0, 1)), ((0, 1), (1, 0)), ((1, 0), (0, 0)))
        else:
            moves = (((1, 0), (0, 1)), ((1, 1), (1, 0)), ((0, 1), (1, 1)))
        for (sx, sc), (tx, tc) in moves:
            pairs.append((sx * 16 + base + sc, tx * 16 + base + tc))
    return pairs


def swap_in(array):
    x, _, _, core = spot()
    first_corner = (x == 0) & (core == 0)
    last_corner = (x == 1) & (core == 1)
    front, back = array[:QUARTER], array[QUARTER:]
    one = lax.ppermute(jnp.where(first_corner, back, front), AXES, hop_pairs(True))
    two = lax.ppermute(jnp.where(last_corner, front, back), AXES, hop_pairs(False))
    low = jnp.where(first_corner, front, jnp.where(last_corner, two, one))
    high = jnp.where(first_corner, one, jnp.where(last_corner, back, two))
    return jnp.concatenate([low, high], axis=0)


def swap_out(array):
    x, _, _, core = spot()
    first_corner = (x == 0) & (core == 0)
    last_corner = (x == 1) & (core == 1)
    low, high = array[:QUARTER], array[QUARTER:]
    one = lax.ppermute(
        jnp.where(first_corner, high, low), AXES, [(t, s) for s, t in hop_pairs(True)]
    )
    two = lax.ppermute(
        jnp.where(last_corner, low, high), AXES, [(t, s) for s, t in hop_pairs(False)]
    )
    front = jnp.where(first_corner, low, jnp.where(last_corner, two, one))
    back = jnp.where(first_corner, one, jnp.where(last_corner, high, two))
    return jnp.concatenate([front, back], axis=0)


def gather_small(row):
    own = row[None]
    fours = jnp.concatenate([own] + [trade(own, m) for m in (Z0, Z1, Z0 | Z1)], axis=0)
    every = jnp.concatenate(
        [fours] + [trade(fours, m) for m in (Y, X, X | Y)], axis=0
    )
    every = jnp.concatenate([every, trade(every, CORE)], axis=0)
    masks = [
        c | xy | z
        for c in (0, CORE)
        for xy in (0, Y, X, X | Y)
        for z in (0, Z0, Z1, Z0 | Z1)
    ]
    x, z, y, core = spot()
    me = x * 16 + z * 4 + y * 2 + core
    owner = jnp.array(masks, jnp.int32) ^ me
    return every, owner


def in_order(every, owner):
    pick = (jnp.arange(DEVICES, dtype=jnp.int32)[:, None] == owner[None, :]).astype(every.dtype)
    return jnp.dot(pick, every, preferred_element_type=jnp.float32).astype(every.dtype)


def scatter_small(rows):
    x, z, y, core = spot()

    def part(array, bit):
        keep = lax.dynamic_index_in_dim(array, bit, 0, keepdims=False)
        send = lax.dynamic_index_in_dim(array, 1 - bit, 0, keepdims=False)
        return keep, send

    cube = rows.reshape(2, 4, 2, 2, rows.shape[1])
    keep, send = part(jnp.moveaxis(cube, 3, 0), core)
    cube = keep + trade(send, CORE)
    cube = jnp.moveaxis(cube, 1, 2).reshape(4, 4, -1)
    place = x * 2 + y
    pick = lambda array, index: lax.dynamic_index_in_dim(array, index, 0, keepdims=False)
    total = pick(cube, place)
    for mask, jump in ((Y, 1), (X, 2), (X | Y, 3)):
        total = total + trade(pick(cube, place ^ jump), mask)
    final = pick(total, z)
    for mask, jump in ((Z0, 1), (Z1, 2), (Z0 | Z1, 3)):
        final = final + trade(pick(total, z ^ jump), mask)
    return final


def gather_blocks(block, last):
    x, z, y, _ = spot()
    one, two, three = (trade(block, m) for m in (Z0, Z1, Z0 | Z1))
    pair = join(z & 1, block[None], one[None], 0)
    other = join(z & 1, two[None], three[None], 0)
    fours = join(z >> 1, pair, other, 0)
    if last == "x":
        fours = join(y, fours[:, None], trade(fours, Y)[:, None], 1)
        return join(x, fours[None], trade(fours, X)[None], 0)
    fours = join(x, fours[None], trade(fours, X)[None], 0)
    return join(y, fours[:, :, None], trade(fours, Y)[:, :, None], 2)


def scatter_blocks(blocks, first):
    x, z, y, _ = spot()

    def fold(array, bit, axis, mask):
        keep = lax.dynamic_index_in_dim(array, bit, axis, keepdims=False)
        send = lax.dynamic_index_in_dim(array, 1 - bit, axis, keepdims=False)
        got = trade(send, mask)
        return (keep.astype(jnp.float32) + got.astype(jnp.float32)).astype(array.dtype)

    if first == "x":
        fours = fold(fold(blocks, x, 0, X), y, 1, Y)
    else:
        fours = fold(fold(blocks, y, 2, Y), x, 0, X)
    pick = lambda index: lax.dynamic_index_in_dim(fours, index, 0, keepdims=False)
    total = pick(z).astype(jnp.float32)
    for mask, jump in ((Z0, 1), (Z1, 2), (Z0 | Z1, 3)):
        total = total + trade(pick(z ^ jump), mask).astype(jnp.float32)
    return total


def inside_piece(place, start):
    return (place >= start) & (place < start + PIC)


def fill_bias(scalars, low_bias, high_bias):
    core, first, second = scalars[0], scalars[1], scalars[2]

    def fill(ref, chunk, key_start, query_start):
        shape = (QUARTER, QUARTER)
        key = key_start + lax.broadcasted_iota(jnp.int32, shape, 0)
        query = query_start + lax.broadcasted_iota(jnp.int32, shape, 1)
        seen = (
            (key <= query)
            | (inside_piece(key, first) & inside_piece(query, first))
            | (inside_piece(key, second) & inside_piece(query, second))
        )
        ref[pl.ds(chunk * QUARTER, QUARTER), :] = jnp.where(seen, 0.0, -1e30)

    mine, theirs = core * QUARTER, (1 - core) * QUARTER
    fill(low_bias, 0, mine, mine)
    fill(low_bias, 1, theirs, mine)
    half = 2 * QUARTER
    fill(high_bias, 0, mine, half + mine)
    fill(high_bias, 1, half + mine, half + mine)
    fill(high_bias, 2, theirs, half + mine)
    fill(high_bias, 3, half + theirs, half + mine)


def head_lanes(array, head):
    lane = lax.broadcasted_iota(jnp.int32, array.shape, 1)
    return jnp.where((lane >= HD) == (head == 1), array, jnp.zeros_like(array))


def dot_nt(left, right):
    return lax.dot_general(
        left, right, (((1,), (1,)), ((), ())), preferred_element_type=jnp.float32
    )


def dot_nn(left, right):
    return lax.dot_general(
        left, right, (((1,), (0,)), ((), ())), preferred_element_type=jnp.float32
    )


def forward_kernel(scalars, q, k_own, k_other, v_own, v_other, out, lse, low_bias, high_bias):
    @pl.when(pl.program_id(0) == 0)
    def _():
        fill_bias(scalars, low_bias, high_bias)

    scale = HD ** (-0.5)
    key_high = jnp.concatenate([k_own[...], k_other[...]], axis=0)
    value_high = jnp.concatenate([v_own[...], v_other[...]], axis=0)
    key_low = jnp.concatenate([k_own[:QUARTER], k_other[:QUARTER]], axis=0)
    value_low = jnp.concatenate([v_own[:QUARTER], v_other[:QUARTER]], axis=0)
    value_high_t, value_low_t = value_high.T, value_low.T
    for part, (key, value_t, bias) in enumerate(
        ((key_low, value_low_t, low_bias), (key_high, value_high_t, high_bias))
    ):
        rows = pl.ds(part * QUARTER, QUARTER)
        query = q[rows, :] * jnp.bfloat16(scale)
        tops = []
        for head in range(2):
            scores = dot_nt(key, head_lanes(query, head)) + bias[...]
            top = jnp.max(scores, axis=0, keepdims=True)
            expo = jnp.exp(scores - top)
            total = jnp.sum(expo, axis=0, keepdims=True)
            mixed = dot_nn(
                value_t[head * HD : (head + 1) * HD], expo.astype(jnp.bfloat16)
            )
            tops.append(mixed / total)
            lse[0, pl.ds(head, 1), rows] = top + jnp.log(total)
        both = jnp.concatenate(tops, axis=0)
        out[rows, :] = both.T.astype(jnp.bfloat16)


def backward_kernel(
    scalars, q, grad, lse, k_own, k_other, v_own, v_other,
    dq, dk_own, dk_other, dv_own, dv_other, low_bias, high_bias,
):
    @pl.when(pl.program_id(0) == 0)
    def _():
        fill_bias(scalars, low_bias, high_bias)

    scale = HD ** (-0.5)
    key_high = jnp.concatenate([k_own[...], k_other[...]], axis=0)
    value_high = jnp.concatenate([v_own[...], v_other[...]], axis=0)
    key_low = jnp.concatenate([k_own[:QUARTER], k_other[:QUARTER]], axis=0)
    value_low = jnp.concatenate([v_own[:QUARTER], v_other[:QUARTER]], axis=0)
    key_high_t, key_low_t = key_high.T, key_low.T
    sums = []
    for part, (key, key_t, value, bias) in enumerate(
        ((key_low, key_low_t, value_low, low_bias), (key_high, key_high_t, value_high, high_bias))
    ):
        rows = pl.ds(part * QUARTER, QUARTER)
        query = q[rows, :] * jnp.bfloat16(scale)
        grad_out = grad[rows, :]
        grad_query, grad_key, grad_value = [], 0.0, 0.0
        for head in range(2):
            query_head = head_lanes(query, head)
            grad_head = head_lanes(grad_out, head)
            scores = dot_nt(key, query_head) + bias[...]
            probs = jnp.exp(scores - lse[0, pl.ds(head, 1), rows])
            grad_probs = dot_nt(value, grad_head)
            delta = jnp.sum(probs * grad_probs, axis=0, keepdims=True)
            grad_scores = (probs * (grad_probs - delta)).astype(jnp.bfloat16)
            grad_value += dot_nn(probs.astype(jnp.bfloat16), grad_head)
            grad_key += dot_nn(grad_scores, query_head)
            grad_query.append(
                dot_nn(key_t[head * HD : (head + 1) * HD], grad_scores) * scale
            )
        dq[rows, :] = jnp.concatenate(grad_query, axis=0).T.astype(jnp.bfloat16)
        sums.append((grad_key, grad_value))
    (key_l, value_l), (key_h, value_h) = sums
    for own, other, low, high in (
        (dk_own, dk_other, key_l, key_h),
        (dv_own, dv_other, value_l, value_h),
    ):
        own[:QUARTER] = (low[:QUARTER] + high[:QUARTER]).astype(jnp.bfloat16)
        own[QUARTER:] = high[QUARTER : 2 * QUARTER].astype(jnp.bfloat16)
        other[:QUARTER] = (low[QUARTER:] + high[2 * QUARTER : 3 * QUARTER]).astype(jnp.bfloat16)
        other[QUARTER:] = high[3 * QUARTER :].astype(jnp.bfloat16)


def pair_block():
    return pl.BlockSpec((ROWS, 2 * HD), lambda i, s: (0, i))


def lse_block():
    return pl.BlockSpec((1, 2, ROWS), lambda i, s: (i, 0, 0))


def bias_scratch():
    return [
        pltpu.VMEM((2 * QUARTER, QUARTER), jnp.float32),
        pltpu.VMEM((4 * QUARTER, QUARTER), jnp.float32),
    ]


def attend(scalars, q, k_own, k_other, v_own, v_other):
    return pl.pallas_call(
        forward_kernel,
        grid_spec=pltpu.PrefetchScalarGridSpec(
            num_scalar_prefetch=1,
            grid=(HEADS // 2,),
            in_specs=[pair_block()] * 5,
            out_specs=[pair_block(), lse_block()],
            scratch_shapes=bias_scratch(),
        ),
        out_shape=[
            jax.ShapeDtypeStruct((ROWS, D), jnp.bfloat16),
            jax.ShapeDtypeStruct((HEADS // 2, 2, ROWS), jnp.float32),
        ],
        cost_estimate=pl.CostEstimate(flops=10**10, bytes_accessed=5 * 10**6, transcendentals=5 * 10**6),
        compiler_params=pltpu.CompilerParams(vmem_limit_bytes=32 * 2**20),
        name="attend",
    )(scalars, q, k_own, k_other, v_own, v_other)


def attend_back(scalars, q, grad, lse, k_own, k_other, v_own, v_other):
    return pl.pallas_call(
        backward_kernel,
        grid_spec=pltpu.PrefetchScalarGridSpec(
            num_scalar_prefetch=1,
            grid=(HEADS // 2,),
            in_specs=[pair_block()] * 2 + [lse_block()] + [pair_block()] * 4,
            out_specs=[pair_block()] * 5,
            scratch_shapes=bias_scratch(),
        ),
        out_shape=[jax.ShapeDtypeStruct((ROWS, D), jnp.bfloat16)] * 5,
        cost_estimate=pl.CostEstimate(flops=2 * 10**10, bytes_accessed=8 * 10**6, transcendentals=5 * 10**6),
        compiler_params=pltpu.CompilerParams(vmem_limit_bytes=32 * 2**20),
        name="attend_back",
    )(scalars, q, grad, lse, k_own, k_other, v_own, v_other)


def norm_parts(values):
    average = jnp.mean(values, axis=-1, keepdims=True)
    centred = values - average
    rate = lax.rsqrt(jnp.mean(centred * centred, axis=-1, keepdims=True) + epsilon)
    return centred * rate, rate


def norm_back(grad, normal, rate, gain):
    scaled = grad * gain
    return rate * (
        scaled
        - jnp.mean(scaled, axis=-1, keepdims=True)
        - normal * jnp.mean(scaled * normal, axis=-1, keepdims=True)
    )


GELU = 0.7978845608028654


def gelu_both(v):
    inner = jnp.tanh(GELU * (v + 0.044715 * v * v * v))
    slope = 0.5 * (1 + inner) + 0.5 * v * (1 - inner * inner) * GELU * (
        1 + 3 * 0.044715 * v * v
    )
    return 0.5 * v * (1 + inner), slope


def core_halves(array, core):
    half = array.shape[1] // 2
    keep = lax.dynamic_slice_in_dim(array, core * half, half, 1)
    send = lax.dynamic_slice_in_dim(array, (1 - core) * half, half, 1)
    return keep, send


def quick_shards(
    tokens, timesteps, starts, cotangent, ln1_gain, ln1_bias, w_qkv, bias_query,
    bias_value, w_out, bias_out, ln2_gain, ln2_bias, w_up, bias_up, w_down,
    bias_down, time_table,
):
    x, z, y, core = spot()
    f32 = jnp.float32
    low = jnp.bfloat16

    def chip_half(shard):
        rows = join(core, shard, trade(shard, CORE), 0)
        return lax.dynamic_slice_in_dim(rows, core * (shard.shape[1] // 2), shard.shape[1] // 2, 1)

    qkv_half, out_half, up_half = chip_half(w_qkv), chip_half(w_out), chip_half(w_up)
    first_a = gather_blocks(qkv_half[:, :640], "x").reshape(D, -1)
    first_b = gather_blocks(jnp.concatenate([qkv_half[:, 640:], out_half], axis=1), "y").reshape(D, -1)
    up_a = gather_blocks(up_half[:, :768], "x").reshape(D, -1)
    up_b = gather_blocks(up_half[:, 768:], "y").reshape(D, -1)
    down_a = gather_blocks(w_down[:, :384], "x").reshape(16, 96, -1)
    down_b = gather_blocks(w_down[:, 384:], "y").reshape(16, 96, -1)

    first_a2, first_b2 = trade(first_a, CORE), trade(first_b, CORE)
    qkv_full = join(
        core,
        jnp.concatenate([first_a, first_b[:, :512]], axis=1),
        jnp.concatenate([first_a2, first_b2[:, :512]], axis=1),
        1,
    )
    out_full = join(core, first_b[:, 512:], first_b2[:, 512:], 1)
    up_full = join(
        core,
        jnp.concatenate([up_a, up_b], axis=1),
        jnp.concatenate([trade(up_a, CORE), trade(up_b, CORE)], axis=1),
        1,
    )
    down_full = join(
        core,
        jnp.concatenate([down_a, down_b], axis=2)[:, None],
        jnp.concatenate([trade(down_a, CORE), trade(down_b, CORE)], axis=2)[:, None],
        1,
    ).reshape(4 * D, D)

    notes, owner = gather_small(jnp.concatenate([timesteps, starts[0]]))
    order = (jnp.arange(DEVICES, dtype=jnp.int32)[:, None] == owner[None, :]).astype(jnp.int32)
    notes = jnp.sum(order[:, :, None] * notes[None], axis=1)
    every_times = notes[:16, 0]
    levels = jnp.arange(TSTEPS, dtype=jnp.int32)
    rows_of = dense((every_times[:, None] == levels[None, :]).astype(low), time_table).astype(low)
    vectors = (ln1_gain, ln1_bias, bias_query, bias_value, bias_out, ln2_gain, ln2_bias, bias_down)
    every, owner = gather_small(
        jnp.concatenate(vectors + (bias_up, rows_of.reshape(-1)))
    )
    every = in_order(every, owner)
    wide = lambda k: every[:, 24 * k : 24 * k + 24].reshape(D).astype(f32)
    gain_one, shift_one, query_shift, value_shift, out_shift, gain_two, shift_two, down_shift = (
        wide(k) for k in range(8)
    )
    up_shift = every[:, 192:288].reshape(4 * D).astype(f32)
    sequence = ((lax.axis_index("dp") >> 1) << 1) | x
    embed = lax.dynamic_slice_in_dim(every, 288 + 24 * sequence, 24, 1).reshape(D).astype(f32)
    own_starts = lax.dynamic_slice_in_dim(notes, sequence, 1, 0)[0, 1:]
    scalars = jnp.concatenate([core[None].astype(jnp.int32), own_starts])

    start_sum = swap_in(tokens[0]).astype(f32) + embed
    normal_one, rate_one = norm_parts(start_sum)
    normed_one = (normal_one * gain_one + shift_one).astype(low)
    joined = dense(normed_one, qkv_full)
    query = (joined[:, :D] + query_shift).astype(low)
    keys = joined[:, D : 2 * D].astype(low)
    values = (joined[:, 2 * D :] + value_shift).astype(low)
    keys_other, values_other = trade(keys, CORE), trade(values, CORE)
    heads_out, lse = attend(scalars, query, keys, keys_other, values, values_other)

    cot = swap_in(cotangent[0])
    mid = start_sum + dense(heads_out, out_full) + out_shift
    normal_two, rate_two = norm_parts(mid)
    normed_two = (normal_two * gain_two + shift_two).astype(low)
    up_pre = dense(normed_two, up_full) + up_shift
    act_wide, slope = gelu_both(up_pre)
    act = act_wide.astype(low)

    def split_rows(grad):
        cube = grad.reshape(16, 2, 96, D)
        keep = lax.dynamic_index_in_dim(cube, core, 1, keepdims=False)
        send = lax.dynamic_index_in_dim(cube, 1 - core, 1, keepdims=False)
        return (keep.astype(f32) + trade(send, CORE).astype(f32)).astype(low)

    def split_columns(grad):
        keep, send = core_halves(grad, core)
        return (keep.astype(f32) + trade(send, CORE).astype(f32)).astype(low)

    def cube_of(array):
        return array.reshape(2, 4, 2, -1, array.shape[-1])

    def settle(block):
        keep = lax.dynamic_slice_in_dim(block, core * 24, 24, 0)
        send = lax.dynamic_slice_in_dim(block, (1 - core) * 24, 24, 0)
        return join(core, keep, trade(send, CORE), 1)

    down_sum = split_rows(dense_left(act, cot).astype(low))
    grad_down = jnp.concatenate(
        [
            scatter_blocks(cube_of(down_sum[:, :, :384]), "x"),
            scatter_blocks(cube_of(down_sum[:, :, 384:]), "y"),
        ],
        axis=1,
    )
    block_out = swap_out((mid + dense(act, down_full) + down_shift).astype(low))
    grad_up_low = (dense_right(cot, down_full) * slope).astype(low)
    up_sum = split_columns(dense_left(normed_two, grad_up_low).astype(low))
    grad_up = settle(
        jnp.concatenate(
            [
                scatter_blocks(cube_of(up_sum[:, :768]), "x"),
                scatter_blocks(cube_of(up_sum[:, 768:]), "y"),
            ],
            axis=1,
        )
    )
    grad_norm_two = dense_right(grad_up_low, up_full)
    grad_mid = cot.astype(f32) + norm_back(grad_norm_two, normal_two, rate_two, gain_two)
    grad_attn = grad_mid.astype(low)
    out_sum = split_columns(dense_left(heads_out, grad_attn).astype(low))
    grad_out_w = settle(scatter_blocks(cube_of(out_sum), "y"))
    grad_heads = dense_right(grad_attn, out_full).astype(low)
    dq, dk, dk_other, dv, dv_other = attend_back(
        scalars, query, grad_heads, lse, keys, keys_other, values, values_other
    )
    dk = (dk.astype(f32) + trade(dk_other, CORE).astype(f32)).astype(low)
    dv = (dv.astype(f32) + trade(dv_other, CORE).astype(f32)).astype(low)
    grad_joined = jnp.concatenate([dq, dk, dv], axis=1)
    qkv_sum = split_columns(dense_left(normed_one, grad_joined).astype(low))
    grad_qkv = settle(
        jnp.concatenate(
            [
                scatter_blocks(cube_of(qkv_sum[:, :640]), "x"),
                scatter_blocks(cube_of(qkv_sum[:, 640:]), "y"),
            ],
            axis=1,
        )
    )
    grad_norm_one = dense_right(grad_joined, qkv_full)
    grad_start = grad_mid + norm_back(grad_norm_one, normal_one, rate_one, gain_one)
    grad_tokens = swap_out(grad_start.astype(low))

    down_total = lambda array: jnp.sum(array.astype(f32), axis=0)
    sums = (
        down_total(grad_norm_one * normal_one),
        down_total(grad_norm_one),
        down_total(dq),
        down_total(dv),
        down_total(grad_attn),
        down_total(grad_norm_two * normal_two),
        down_total(grad_norm_two),
        down_total(cot),
    )
    own_sum = jnp.sum(grad_start, axis=0).reshape(DEVICES, 1, 24)
    ours = (jnp.arange(16, dtype=jnp.int32) == sequence).astype(f32)[None, :, None]
    packed = jnp.concatenate(
        [v.reshape(DEVICES, 24) for v in sums]
        + [down_total(grad_up_low).reshape(DEVICES, 96), (own_sum * ours).reshape(DEVICES, 384)],
        axis=1,
    )
    final = scatter_small(packed)
    vec = lambda k: final[24 * k : 24 * k + 24]
    hit = (every_times[None, :] == levels[:, None]).astype(f32)
    grad_table = jnp.dot(hit, final[288:].reshape(16, 24), precision=lax.Precision.HIGHEST)
    return (
        block_out[None],
        grad_tokens[None],
        vec(0),
        vec(1),
        grad_qkv,
        vec(2),
        vec(3),
        grad_out_w,
        vec(4),
        vec(5),
        vec(6),
        grad_up,
        final[192:288],
        grad_down,
        vec(7),
        grad_table,
    )


def solution(mesh):
    quick = mesh.shape["seq"] == 2 and mesh.shape["dp"] == 16
    return jax.shard_map(
        quick_shards if quick else shards,
        mesh=mesh,
        in_specs=(
            P("dp", "seq", None),
            P("dp"),
            P("dp", None),
            P("dp", "seq", None),
            P(("seq", "dp")),
            P(("seq", "dp")),
            P(("seq", "dp"), None),
            P(("seq", "dp")),
            P(("seq", "dp")),
            P(("seq", "dp"), None),
            P(("seq", "dp")),
            P(("seq", "dp")),
            P(("seq", "dp")),
            P(("seq", "dp"), None),
            P(("seq", "dp")),
            P(("seq", "dp"), None),
            P(("seq", "dp")),
            P(None, ("seq", "dp")),
        ),
        out_specs=(
            P("dp", "seq", None),
            P("dp", "seq", None),
            P(("seq", "dp")),
            P(("seq", "dp")),
            P(("seq", "dp"), None),
            P(("seq", "dp")),
            P(("seq", "dp")),
            P(("seq", "dp"), None),
            P(("seq", "dp")),
            P(("seq", "dp")),
            P(("seq", "dp")),
            P(("seq", "dp"), None),
            P(("seq", "dp")),
            P(("seq", "dp"), None),
            P(("seq", "dp")),
            P(None, ("seq", "dp")),
        ),
        check_vma=False,
    )
```

```python
import jax
import jax.numpy as jnp
from jax import lax
from jax.experimental import pallas as pl
from jax.experimental.pallas import tpu as pltpu
from jax.sharding import PartitionSpec as P

D = 768
HEADS = 12
HD = 64
TSTEPS = 1000
PIC = 256
NPIC = 2


epsilon = 1e-05


def layer_norm(values, gain, shift):
    average = jnp.mean(values, axis=-1, keepdims=True)
    centred = values - average
    spread = jnp.mean(centred * centred, axis=-1, keepdims=True)
    return centred * lax.rsqrt(spread + epsilon) * gain + shift


def piece_label(starts, places):
    inside = (places[None, None, :] >= starts[:, :, None]) & (
        places[None, None, :] < starts[:, :, None] + PIC
    )
    number = jnp.arange(1, NPIC + 1, dtype=jnp.int32)
    return jnp.sum(inside.astype(jnp.int32) * number[None, :, None], axis=1)


def visible_mask(starts, query_pos, key_pos):
    label_query = piece_label(starts, query_pos)
    label_key = piece_label(starts, key_pos)
    causal = query_pos[:, None] >= key_pos[None, :]
    return causal[None] | (label_query[:, :, None] == label_key[:, None, :]) & (
        label_query[:, :, None] > 0
    )


def dense(left, right):
    return jnp.dot(left, right, preferred_element_type=jnp.float32)


def dense_left(left, right):
    return lax.dot_general(
        left, right, (((0,), (0,)), ((), ())), preferred_element_type=jnp.float32
    )


def dense_right(left, right):
    return lax.dot_general(
        left, right, (((1,), (1,)), ((), ())), preferred_element_type=jnp.float32
    )


def head_slice(array, index):
    return lax.dynamic_slice_in_dim(array, index * HD, HD, 2)


def merge_heads(stacked):
    head_count, seq_count, row_count, head_size = stacked.shape
    return jnp.transpose(stacked, (1, 2, 0, 3)).reshape(
        seq_count, row_count, head_count * head_size
    )


def shards(
    tokens,
    timesteps,
    starts,
    cotangent,
    ln1_gain,
    ln1_bias,
    w_qkv,
    bias_query,
    bias_value,
    w_out,
    bias_out,
    ln2_gain,
    ln2_bias,
    w_up,
    bias_up,
    w_down,
    bias_down,
    time_table,
):
    gathered = (
        lax.all_gather(ln1_gain, ("seq", "dp"), axis=0, tiled=True),
        lax.all_gather(ln1_bias, ("seq", "dp"), axis=0, tiled=True),
        lax.all_gather(w_qkv, ("seq", "dp"), axis=0, tiled=True),
        lax.all_gather(bias_query, ("seq", "dp"), axis=0, tiled=True),
        lax.all_gather(bias_value, ("seq", "dp"), axis=0, tiled=True),
        lax.all_gather(w_out, ("seq", "dp"), axis=0, tiled=True),
        lax.all_gather(bias_out, ("seq", "dp"), axis=0, tiled=True),
        lax.all_gather(ln2_gain, ("seq", "dp"), axis=0, tiled=True),
        lax.all_gather(ln2_bias, ("seq", "dp"), axis=0, tiled=True),
        lax.all_gather(w_up, ("seq", "dp"), axis=0, tiled=True),
        lax.all_gather(bias_up, ("seq", "dp"), axis=0, tiled=True),
        lax.all_gather(w_down, ("seq", "dp"), axis=0, tiled=True),
        lax.all_gather(bias_down, ("seq", "dp"), axis=0, tiled=True),
        lax.all_gather(time_table, ("seq", "dp"), axis=1, tiled=True),
    )
    (
        gain_one,
        shift_one,
        qkv_full,
        query_shift,
        value_shift,
        out_full,
        out_shift,
        gain_two,
        shift_two,
        up_full,
        up_shift,
        down_full,
        down_shift,
        table_full,
    ) = gathered
    seq_count, row_count, model_width = tokens.shape
    flat_rows = seq_count * row_count
    scale = HD ** (-0.5)
    levels = jnp.arange(TSTEPS, dtype=jnp.int32)
    onehot = timesteps[:, None] == levels[None, :]
    embed = dense(onehot.astype(jnp.bfloat16), table_full)
    start_sum = (tokens.astype(jnp.float32) + embed[:, None, :]).reshape(flat_rows, model_width)
    norm_one, pull_one = jax.vjp(
        layer_norm, start_sum, gain_one.astype(jnp.float32), shift_one.astype(jnp.float32)
    )
    normed_one = norm_one.astype(jnp.bfloat16)
    joined = dense(normed_one, qkv_full)
    query = (
        (joined[:, :D] + query_shift.astype(jnp.float32))
        .astype(jnp.bfloat16)
        .reshape(seq_count, row_count, D)
    )
    keys = joined[:, D : 2 * D].astype(jnp.bfloat16).reshape(seq_count, row_count, D)
    values = (
        (joined[:, 2 * D :] + value_shift.astype(jnp.float32))
        .astype(jnp.bfloat16)
        .reshape(seq_count, row_count, D)
    )
    key_all, value_all = (
        lax.all_gather(keys, "seq", axis=1, tiled=True),
        lax.all_gather(values, "seq", axis=1, tiled=True),
    )
    full_len = key_all.shape[1]
    query_pos = lax.axis_index("seq") * row_count + jnp.arange(row_count, dtype=jnp.int32)
    every_pos = jnp.arange(full_len, dtype=jnp.int32)
    allowed = visible_mask(starts, query_pos, every_pos)

    def head_forward(index):
        query_head = head_slice(query, index)
        key_head = head_slice(key_all, index)
        value_head = head_slice(value_all, index)
        scores = scale * jnp.einsum(
            "sre,ske->srk", query_head, key_head, preferred_element_type=jnp.float32
        )
        scores = jnp.where(allowed, scores, -1e30)
        top = jnp.max(scores, axis=-1, keepdims=True)
        expo = jnp.exp(scores - top)
        total = jnp.sum(expo, axis=-1, keepdims=True)
        probs = expo / total
        result = jnp.einsum(
            "srk,ske->sre",
            probs.astype(jnp.bfloat16),
            value_head,
            preferred_element_type=jnp.float32,
        )
        return (result, top[..., 0] + jnp.log(total[..., 0]))

    head_out, log_total = lax.map(head_forward, jnp.arange(HEADS, dtype=jnp.int32))
    heads_out = merge_heads(head_out).astype(jnp.bfloat16).reshape(flat_rows, D)
    mid = start_sum + dense(heads_out, out_full) + out_shift.astype(jnp.float32)
    norm_two, pull_two = jax.vjp(
        layer_norm, mid, gain_two.astype(jnp.float32), shift_two.astype(jnp.float32)
    )
    normed_two = norm_two.astype(jnp.bfloat16)
    up_pre = dense(normed_two, up_full) + up_shift.astype(jnp.float32)
    act_value, pull_act = jax.vjp(jax.nn.gelu, up_pre)
    act = act_value.astype(jnp.bfloat16)
    block_out = (mid + dense(act, down_full) + down_shift.astype(jnp.float32)).astype(jnp.bfloat16)
    qkv_back, out_back, up_back, down_back = (
        lax.all_gather(w_qkv, ("seq", "dp"), axis=0, tiled=True),
        lax.all_gather(w_out, ("seq", "dp"), axis=0, tiled=True),
        lax.all_gather(w_up, ("seq", "dp"), axis=0, tiled=True),
        lax.all_gather(w_down, ("seq", "dp"), axis=0, tiled=True),
    )
    grad_mlp = cotangent.reshape(flat_rows, D)
    grad_down = dense_left(act, grad_mlp)
    grad_down_shift = jnp.sum(grad_mlp.astype(jnp.float32), axis=0)
    grad_act = dense_right(grad_mlp, down_back)
    (grad_up_pre,) = pull_act(grad_act)
    grad_up_low = grad_up_pre.astype(jnp.bfloat16)
    grad_up = dense_left(normed_two, grad_up_low)
    grad_up_shift = jnp.sum(grad_up_low.astype(jnp.float32), axis=0)
    grad_norm_two = dense_right(grad_up_low, up_back)
    grad_mid_norm, grad_gain_two, grad_shift_two = pull_two(grad_norm_two)
    grad_mid = cotangent.reshape(flat_rows, D).astype(jnp.float32) + grad_mid_norm
    grad_attn = grad_mid.astype(jnp.bfloat16)
    grad_out_w = dense_left(heads_out, grad_attn)
    grad_out_shift = jnp.sum(grad_attn.astype(jnp.float32), axis=0)
    grad_heads = (
        dense_right(grad_attn, out_back).astype(jnp.bfloat16).reshape(seq_count, row_count, D)
    )
    key_back, value_back = (
        lax.all_gather(keys, "seq", axis=1, tiled=True),
        lax.all_gather(values, "seq", axis=1, tiled=True),
    )

    def query_side(index, log_head):
        query_head = head_slice(query, index)
        key_head = head_slice(key_back, index)
        value_head = head_slice(value_back, index)
        grad_head = head_slice(grad_heads, index)
        scores = scale * jnp.einsum(
            "sre,ske->srk", query_head, key_head, preferred_element_type=jnp.float32
        )
        scores = jnp.where(allowed, scores, -1e30)
        probs = jnp.exp(scores - log_head[..., None])
        grad_probs = jnp.einsum(
            "sre,ske->srk", grad_head, value_head, preferred_element_type=jnp.float32
        )
        delta = jnp.sum(probs * grad_probs, axis=-1, keepdims=True)
        grad_scores = (probs * (grad_probs - delta)).astype(jnp.bfloat16)
        grad_query_head = scale * jnp.einsum(
            "srk,ske->sre", grad_scores, key_head, preferred_element_type=jnp.float32
        )
        return (probs, grad_scores, delta[..., 0], grad_query_head)

    def query_only(inputs):
        index, log_head = inputs
        probs, grad_scores, delta, grad_query_head = query_side(index, log_head)
        return (grad_query_head, delta)

    grad_query_heads, delta_heads = lax.map(
        query_only, (jnp.arange(HEADS, dtype=jnp.int32), log_total)
    )
    query_every, grad_every, log_every, delta_every = (
        lax.all_gather(query, "seq", axis=1, tiled=True),
        lax.all_gather(grad_heads, "seq", axis=1, tiled=True),
        lax.all_gather(log_total.astype(jnp.bfloat16), "seq", axis=2, tiled=True).astype(
            log_total.dtype
        ),
        lax.all_gather(delta_heads.astype(jnp.bfloat16), "seq", axis=2, tiled=True).astype(
            delta_heads.dtype
        ),
    )
    key_allowed = visible_mask(starts, every_pos, query_pos)

    def key_side(inputs):
        index, log_head, delta_head = inputs
        query_head = head_slice(query_every, index)
        grad_head = head_slice(grad_every, index)
        key_head = head_slice(keys, index)
        value_head = head_slice(values, index)
        scores = scale * jnp.einsum(
            "sqe,ske->sqk", query_head, key_head, preferred_element_type=jnp.float32
        )
        scores = jnp.where(key_allowed, scores, -1e30)
        probs = jnp.exp(scores - log_head[..., None])
        grad_probs = jnp.einsum(
            "sqe,ske->sqk", grad_head, value_head, preferred_element_type=jnp.float32
        )
        grad_scores = (probs * (grad_probs - delta_head[..., None])).astype(jnp.bfloat16)
        grad_key_head = scale * jnp.einsum(
            "sqk,sqe->ske", grad_scores, query_head, preferred_element_type=jnp.float32
        )
        grad_value_head = jnp.einsum(
            "sqk,sqe->ske",
            probs.astype(jnp.bfloat16),
            grad_head,
            preferred_element_type=jnp.float32,
        )
        return (grad_key_head, grad_value_head)

    grad_key_heads, grad_value_heads = lax.map(
        key_side, (jnp.arange(HEADS, dtype=jnp.int32), log_every, delta_every)
    )
    grad_key_own = merge_heads(grad_key_heads)
    grad_value_own = merge_heads(grad_value_heads)
    grad_query_low = merge_heads(grad_query_heads).astype(jnp.bfloat16).reshape(flat_rows, D)
    grad_key_low = grad_key_own.astype(jnp.bfloat16).reshape(flat_rows, D)
    grad_value_low = grad_value_own.astype(jnp.bfloat16).reshape(flat_rows, D)
    grad_joined = jnp.concatenate([grad_query_low, grad_key_low, grad_value_low], axis=1)
    grad_qkv = dense_left(normed_one, grad_joined)
    grad_query_shift = jnp.sum(grad_query_low.astype(jnp.float32), axis=0)
    grad_value_shift = jnp.sum(grad_value_low.astype(jnp.float32), axis=0)
    grad_norm_one = dense_right(grad_joined, qkv_back)
    grad_start_norm, grad_gain_one, grad_shift_one = pull_one(grad_norm_one)
    grad_start = grad_mid + grad_start_norm
    grad_tokens = grad_start.astype(jnp.bfloat16).reshape(seq_count, row_count, D)
    seq_sums = jnp.sum(grad_start.reshape(seq_count, row_count, D), axis=1)
    every_sums, every_times = (
        lax.all_gather(seq_sums, ("seq", "dp"), axis=0, tiled=True),
        lax.all_gather(timesteps, ("seq", "dp"), axis=0, tiled=True),
    )
    own_width = D // lax.axis_size(("seq", "dp"))
    own_sums = lax.dynamic_slice_in_dim(
        every_sums, lax.axis_index(("seq", "dp")) * own_width, own_width, 1
    )
    every_onehot = (every_times[None, :] == levels[:, None]).astype(jnp.float32)
    grad_table = jnp.dot(every_onehot, own_sums, precision=lax.Precision.HIGHEST)
    summed = (
        lax.psum_scatter(grad_gain_one, ("seq", "dp"), scatter_dimension=0, tiled=True),
        lax.psum_scatter(grad_shift_one, ("seq", "dp"), scatter_dimension=0, tiled=True),
        lax.psum_scatter(grad_qkv, ("seq", "dp"), scatter_dimension=0, tiled=True),
        lax.psum_scatter(grad_query_shift, ("seq", "dp"), scatter_dimension=0, tiled=True),
        lax.psum_scatter(grad_value_shift, ("seq", "dp"), scatter_dimension=0, tiled=True),
        lax.psum_scatter(grad_out_w, ("seq", "dp"), scatter_dimension=0, tiled=True),
        lax.psum_scatter(grad_out_shift, ("seq", "dp"), scatter_dimension=0, tiled=True),
        lax.psum_scatter(grad_gain_two, ("seq", "dp"), scatter_dimension=0, tiled=True),
        lax.psum_scatter(grad_shift_two, ("seq", "dp"), scatter_dimension=0, tiled=True),
        lax.psum_scatter(grad_up, ("seq", "dp"), scatter_dimension=0, tiled=True),
        lax.psum_scatter(grad_up_shift, ("seq", "dp"), scatter_dimension=0, tiled=True),
        lax.psum_scatter(grad_down, ("seq", "dp"), scatter_dimension=0, tiled=True),
        lax.psum_scatter(grad_down_shift, ("seq", "dp"), scatter_dimension=0, tiled=True),
    )
    return (
        block_out.reshape(seq_count, row_count, D),
        grad_tokens,
        summed[0],
        summed[1],
        summed[2],
        summed[3],
        summed[4],
        summed[5],
        summed[6],
        summed[7],
        summed[8],
        summed[9],
        summed[10],
        summed[11],
        summed[12],
        grad_table,
    )


AXES = ("seq", "dp")
CORE, Y, Z0, Z1, X = 1, 2, 4, 8, 16
STAGES = (CORE, Y, X, Z0, Z1)
DEVICES = 32
QUARTER = 256
ROWS = 512
FF = 3072
TILE = 256
WIDE = 384
MIB = 2**20
F32 = jnp.float32
LOW = jnp.bfloat16

Z_MASKS = (0, Z0, Z1, Z0 | Z1)
X_LAST = tuple((xy | z) >> 1 for xy in (0, Y, X, X | Y) for z in Z_MASKS)
Y_LAST = tuple((xy | z) >> 1 for xy in (0, X, Y, X | Y) for z in Z_MASKS)


def trade(array, mask):
    return lax.ppermute(array, AXES, [(i, i ^ mask) for i in range(DEVICES)])


def join(bit, own, other, axis):
    return jnp.where(
        bit == 0,
        jnp.concatenate([own, other], axis=axis),
        jnp.concatenate([other, own], axis=axis),
    )


def spot():
    x = lax.axis_index("seq")
    dp = lax.axis_index("dp")
    return x, dp >> 2, (dp >> 1) & 1, dp & 1


def hop_pairs(first):
    pairs = []
    for base in range(0, 16, 2):
        if first:
            moves = (((0, 0), (0, 1)), ((0, 1), (1, 0)), ((1, 0), (0, 0)))
        else:
            moves = (((1, 0), (0, 1)), ((1, 1), (1, 0)), ((0, 1), (1, 1)))
        for (sx, sc), (tx, tc) in moves:
            pairs.append((sx * 16 + base + sc, tx * 16 + base + tc))
    return pairs


def swap_in(array):
    x, _, _, core = spot()
    first_corner = (x == 0) & (core == 0)
    last_corner = (x == 1) & (core == 1)
    front, back = array[:QUARTER], array[QUARTER:]
    one = lax.ppermute(jnp.where(first_corner, back, front), AXES, hop_pairs(True))
    two = lax.ppermute(jnp.where(last_corner, front, back), AXES, hop_pairs(False))
    low = jnp.where(first_corner, front, jnp.where(last_corner, two, one))
    high = jnp.where(first_corner, one, jnp.where(last_corner, back, two))
    return jnp.concatenate([low, high], axis=0)


def swap_out(array):
    x, _, _, core = spot()
    first_corner = (x == 0) & (core == 0)
    last_corner = (x == 1) & (core == 1)
    low, high = array[:QUARTER], array[QUARTER:]
    one = lax.ppermute(
        jnp.where(first_corner, high, low), AXES, [(t, s) for s, t in hop_pairs(True)]
    )
    two = lax.ppermute(
        jnp.where(last_corner, low, high), AXES, [(t, s) for s, t in hop_pairs(False)]
    )
    front = jnp.where(first_corner, low, jnp.where(last_corner, two, one))
    back = jnp.where(first_corner, one, jnp.where(last_corner, high, two))
    return jnp.concatenate([front, back], axis=0)


def small_masks():
    masks = [0]
    for stage in STAGES:
        masks = masks + [mask | stage for mask in masks]
    return masks


def gather_small(row):
    every = row[None]
    for stage in STAGES:
        every = jnp.concatenate([every, trade(every, stage)], axis=0)
    return every


def pick_matrix(me, dtype):
    owner = jnp.array(small_masks(), jnp.int32) ^ me
    return (jnp.arange(DEVICES, dtype=jnp.int32)[:, None] == owner[None, :]).astype(dtype)


def scatter_small(rows):
    for stage in reversed(STAGES):
        half = rows.shape[0] // 2
        rows = rows[:half] + trade(rows[half:], stage)
    return rows[0]


def gather_z(block):
    return jnp.stack([block] + [trade(block, mask) for mask in Z_MASKS[1:]], axis=0)


def gather_two(blocks, first, second):
    blocks = jnp.concatenate([blocks, trade(blocks, first)], axis=0)
    return jnp.concatenate([blocks, trade(blocks, second)], axis=0)


def gather_direct(blocks):
    return jnp.concatenate([blocks] + [trade(blocks, m) for m in (Y, X, X | Y)], axis=0)


def add_low(left, right):
    return (left.astype(F32) + right.astype(F32)).astype(LOW)


def scatter_two(keep, got, n, first):
    cube = lambda array: array.reshape(2, 4, 2, -1, n)
    keep, got = cube(keep), cube(got)
    if first == "x":
        away = add_low(keep[1], got[1])
        half = add_low(add_low(keep[0], got[0]), trade(away, X))
        return add_low(half[:, 0], trade(half[:, 1], Y))
    away = add_low(keep[:, :, 1], got[:, :, 1])
    half = add_low(add_low(keep[:, :, 0], got[:, :, 0]), trade(away, Y))
    return add_low(half[0], trade(half[1], X))


def scatter_direct(keep, got, n):
    cube = lambda array: array.reshape(2, 4, 2, -1, n)
    keep, got = cube(keep), cube(got)
    total = keep[0, :, 0].astype(F32) + got[0, :, 0].astype(F32)
    for mask, a, b in ((Y, 0, 1), (X, 1, 0), (X | Y, 1, 1)):
        total = total + trade(add_low(keep[a, :, b], got[a, :, b]), mask).astype(F32)
    return total.astype(LOW)


def scatter_z(fours):
    total = fours[0].astype(F32)
    for place, mask in enumerate(Z_MASKS[1:], 1):
        total = total + trade(fours[place], mask).astype(F32)
    return total


def settle(block, core):
    keep = lax.dynamic_slice_in_dim(block, core * 24, 24, 0)
    send = lax.dynamic_slice_in_dim(block, (1 - core) * 24, 24, 0)
    return join(core, keep, trade(send, CORE), 1)


def dot_nt(left, right):
    return lax.dot_general(
        left, right, (((1,), (1,)), ((), ())), preferred_element_type=F32
    )


def dot_nn(left, right):
    return lax.dot_general(
        left, right, (((1,), (0,)), ((), ())), preferred_element_type=F32
    )


def inside_piece(place, start):
    return (place >= start) & (place < start + PIC)


def fill_bias(scalars, low_bias, high_bias):
    core, first, second = scalars[1], scalars[3], scalars[4]

    def fill(ref, chunk, key_start, query_start):
        shape = (QUARTER, QUARTER)
        key = key_start + lax.broadcasted_iota(jnp.int32, shape, 0)
        query = query_start + lax.broadcasted_iota(jnp.int32, shape, 1)
        seen = (
            (key <= query)
            | (inside_piece(key, first) & inside_piece(query, first))
            | (inside_piece(key, second) & inside_piece(query, second))
        )
        ref[pl.ds(chunk * QUARTER, QUARTER), :] = jnp.where(seen, 0.0, -1e30)

    mine, theirs = core * QUARTER, (1 - core) * QUARTER
    fill(low_bias, 0, mine, mine)
    fill(low_bias, 1, theirs, mine)
    half = 2 * QUARTER
    fill(high_bias, 0, mine, half + mine)
    fill(high_bias, 1, half + mine, half + mine)
    fill(high_bias, 2, theirs, half + mine)
    fill(high_bias, 3, half + theirs, half + mine)


def head_lanes(array, head):
    lane = lax.broadcasted_iota(jnp.int32, array.shape, 1)
    return jnp.where((lane >= HD) == (head == 1), array, jnp.zeros_like(array))


def key_sets(own, other):
    high = jnp.concatenate([own[...], other[...]], axis=0)
    low = jnp.concatenate([own[:QUARTER], other[:QUARTER]], axis=0)
    return low, high


def forward_kernel(scalars, q, k_own, k_other, v_own, v_other, out, lse, low_bias, high_bias):
    @pl.when(pl.program_id(0) == 0)
    def _():
        fill_bias(scalars, low_bias, high_bias)

    scale = HD ** (-0.5)
    keys, values = key_sets(k_own, k_other), key_sets(v_own, v_other)
    for part, bias in enumerate((low_bias, high_bias)):
        key, value_t = keys[part], values[part].T
        rows = pl.ds(part * QUARTER, QUARTER)
        query = q[rows, :] * jnp.bfloat16(scale)
        tops = []
        for head in range(2):
            scores = dot_nt(key, head_lanes(query, head)) + bias[...]
            top = jnp.max(scores, axis=0, keepdims=True)
            expo = jnp.exp(scores - top)
            total = jnp.sum(expo, axis=0, keepdims=True)
            mixed = dot_nn(value_t[head * HD : (head + 1) * HD], expo.astype(LOW))
            tops.append(mixed / total)
            lse[0, pl.ds(head, 1), rows] = top + jnp.log(total)
        both = jnp.concatenate(tops, axis=0)
        out[rows, :] = both.T.astype(LOW)


def backward_kernel(
    scalars, q, grad, lse, k_own, k_other, v_own, v_other,
    dq, own, other, low_bias, high_bias,
):
    @pl.when(pl.program_id(0) == 0)
    def _():
        fill_bias(scalars, low_bias, high_bias)

    scale = HD ** (-0.5)
    keys, values = key_sets(k_own, k_other), key_sets(v_own, v_other)
    sums = []
    for part, bias in enumerate((low_bias, high_bias)):
        key, value = keys[part], values[part]
        key_t = key.T
        rows = pl.ds(part * QUARTER, QUARTER)
        query = q[rows, :] * jnp.bfloat16(scale)
        grad_out = grad[rows, :]
        grad_query, grad_key, grad_value = [], 0.0, 0.0
        for head in range(2):
            query_head = head_lanes(query, head)
            grad_head = head_lanes(grad_out, head)
            scores = dot_nt(key, query_head) + bias[...]
            probs = jnp.exp(scores - lse[0, pl.ds(head, 1), rows])
            grad_probs = dot_nt(value, grad_head)
            delta = jnp.sum(probs * grad_probs, axis=0, keepdims=True)
            grad_scores = (probs * (grad_probs - delta)).astype(LOW)
            grad_value += dot_nn(probs.astype(LOW), grad_head)
            grad_key += dot_nn(grad_scores, query_head)
            grad_query.append(
                dot_nn(key_t[head * HD : (head + 1) * HD], grad_scores) * scale
            )
        dq[rows, :] = jnp.concatenate(grad_query, axis=0).T.astype(LOW)
        sums.append((grad_key, grad_value))
    for which in range(2):
        low, high = sums[0][which], sums[1][which]
        own[which, :QUARTER] = (low[:QUARTER] + high[:QUARTER]).astype(LOW)
        own[which, QUARTER:] = high[QUARTER : 2 * QUARTER].astype(LOW)
        other[which, :QUARTER] = (low[QUARTER:] + high[2 * QUARTER : 3 * QUARTER]).astype(LOW)
        other[which, QUARTER:] = high[3 * QUARTER :].astype(LOW)


PAIRS = HEADS // 2


def pair_block(skip=0):
    return pl.BlockSpec((ROWS, 2 * HD), lambda i, s: (0, i + skip))


def lse_block():
    return pl.BlockSpec((1, 2, ROWS), lambda i, s: (i, 0, 0))


def bias_scratch():
    return [
        pltpu.VMEM((2 * QUARTER, QUARTER), F32),
        pltpu.VMEM((4 * QUARTER, QUARTER), F32),
    ]


def cost(flops, size):
    return pl.CostEstimate(flops=flops, bytes_accessed=size, transcendentals=0)


def array(shape, dtype=LOW):
    return jax.ShapeDtypeStruct(shape, dtype)


def attend(scalars, q, kv, kv_other):
    return pl.pallas_call(
        forward_kernel,
        grid_spec=pltpu.PrefetchScalarGridSpec(
            num_scalar_prefetch=1,
            grid=(PAIRS,),
            in_specs=[pair_block(), pair_block(), pair_block(), pair_block(PAIRS), pair_block(PAIRS)],
            out_specs=[pair_block(), lse_block()],
            scratch_shapes=bias_scratch(),
        ),
        out_shape=[array((ROWS, D)), array((PAIRS, 2, ROWS), F32)],
        cost_estimate=cost(10**10, 5 * 10**6),
        compiler_params=pltpu.CompilerParams(vmem_limit_bytes=32 * MIB),
        name="attend",
    )(scalars, q, kv, kv_other, kv, kv_other)


def attend_back(scalars, q, grad, lse, kv, kv_other):
    both = pl.BlockSpec((2, ROWS, 2 * HD), lambda i, s: (0, 0, i))
    return pl.pallas_call(
        backward_kernel,
        grid_spec=pltpu.PrefetchScalarGridSpec(
            num_scalar_prefetch=1,
            grid=(PAIRS,),
            in_specs=[pair_block()] * 2
            + [lse_block(), pair_block(), pair_block(), pair_block(PAIRS), pair_block(PAIRS)],
            out_specs=[pair_block(), both, both],
            scratch_shapes=bias_scratch(),
        ),
        out_shape=[array((ROWS, D)), array((2, ROWS, D)), array((2, ROWS, D))],
        cost_estimate=cost(2 * 10**10, 8 * 10**6),
        compiler_params=pltpu.CompilerParams(vmem_limit_bytes=32 * MIB),
        name="attend_back",
    )(scalars, q, grad, lse, kv, kv_other, kv, kv_other)


def fetch(jobs, sems):
    copies = [pltpu.make_async_copy(s, d, sems.at[i]) for i, (s, d) in enumerate(jobs)]
    for copy in copies:
        copy.start()
    return copies


def wait(copies):
    for copy in copies:
        copy.wait()


def column_jobs(scalars, source, other, target, masks, start, width):
    chip, core = scalars[0], scalars[1]
    jobs = []
    for blocks, side in ((source, core), (other, 1 - core)):
        columns = pl.ds(pl.multiple_of(side * width, 128), width)
        for j, mask in enumerate(masks):
            rows = pl.ds(pl.multiple_of((chip ^ mask) * 48, 16), 48)
            jobs.append((blocks.at[j, :, pl.ds(start, width)], target.at[rows, columns]))
    return jobs


def down_jobs(scalars, source, other, target):
    chip, core = scalars[0], scalars[1]
    jobs = []
    for blocks, side in ((source, core), (other, 1 - core)):
        for j, mask in enumerate(Y_LAST):
            for half in range(2):
                first = pl.multiple_of((chip ^ mask) * 192 + side * 96 + half * 48, 16)
                jobs.append((blocks.at[j, :, pl.ds(half * D, D)], target.at[pl.ds(first, 48), :]))
    return jobs


CHUNK = 128


def by_rows(body):
    @pl.loop(0, ROWS // CHUNK)
    def _(step):
        body(pl.ds(pl.multiple_of(step * CHUNK, CHUNK), CHUNK))


def norm_parts(values):
    average = jnp.mean(values, axis=-1, keepdims=True)
    centred = values - average
    rate = lax.rsqrt(jnp.mean(centred * centred, axis=-1, keepdims=True) + epsilon)
    return centred * rate, rate


def norm_back(grad, normal, rate, gain):
    scaled = grad * gain
    return rate * (
        scaled
        - jnp.mean(scaled, axis=-1, keepdims=True)
        - normal * jnp.mean(scaled * normal, axis=-1, keepdims=True)
    )


def full(shape):
    return pl.BlockSpec(shape, lambda i, s: (0,) * len(shape))


def anywhere():
    return pl.BlockSpec(memory_space=pl.ANY)


def embed_row(scalars, vec):
    return vec[pl.ds(12 + scalars[2], 1), :]


def project_kernel(scalars, tok, vec, blocks, other, normed, q, kv, weight, sems):
    step = pl.program_id(0)

    @pl.when(step == 0)
    def _():
        copies = fetch(column_jobs(scalars, blocks, other, weight, X_LAST, 0, 1152), sems)

        def rows_of(rows):
            normal, _ = norm_parts(tok[rows, :].astype(F32) + embed_row(scalars, vec))
            normed[rows, :] = (normal * vec[0:1, :] + vec[1:2, :]).astype(LOW)

        by_rows(rows_of)
        wait(copies)

    columns = pl.ds(pl.multiple_of(step * TILE, TILE), TILE)
    result = dot_nn(normed[...], weight[:, columns])

    @pl.when(step < 3)
    def _():
        q[...] = (result + vec[2:3, columns]).astype(LOW)

    @pl.when((step >= 3) & (step < 6))
    def _():
        kv[...] = result.astype(LOW)

    @pl.when(step >= 6)
    def _():
        side = pl.ds(pl.multiple_of(step * TILE - 2 * D, TILE), TILE)
        kv[...] = (result + vec[3:4, side]).astype(LOW)


def project(scalars, tok, vec, blocks, other):
    return pl.pallas_call(
        project_kernel,
        grid_spec=pltpu.PrefetchScalarGridSpec(
            num_scalar_prefetch=1,
            grid=(9,),
            in_specs=[full((ROWS, D)), full((28, D)), anywhere(), anywhere()],
            out_specs=[
                full((ROWS, D)),
                pl.BlockSpec((ROWS, TILE), lambda i, s: (0, jnp.minimum(i, 2))),
                pl.BlockSpec((ROWS, TILE), lambda i, s: (0, jnp.maximum(i - 3, 0))),
            ],
            scratch_shapes=[pltpu.VMEM((D, 3 * D), LOW), pltpu.SemaphoreType.DMA((32,))],
        ),
        out_shape=[array((ROWS, D)), array((ROWS, D)), array((ROWS, 2 * D))],
        cost_estimate=cost(2 * 10**9, 8 * 10**6),
        compiler_params=pltpu.CompilerParams(vmem_limit_bytes=32 * MIB),
        name="project",
    )(scalars, tok, vec, blocks, other)


GELU = 0.7978845608028654


def mlp_up_kernel(
    scalars, heads, tok, vec, up_bias, blocks, other, mid, normed, act, slope,
    w_up, w_out, sems,
):
    step = pl.program_id(0)

    @pl.when(step == 0)
    def _():
        jobs = column_jobs(scalars, blocks, other, w_out, X_LAST, 1536, 384)
        jobs += column_jobs(scalars, blocks, other, w_up, X_LAST, 0, 1536)
        copies = fetch(jobs, sems)
        wait(copies)
        mid[...] = dot_nn(heads[...], w_out[...])

        def rows_of(rows):
            total = tok[rows, :].astype(F32) + embed_row(scalars, vec) + mid[rows, :] + vec[4:5, :]
            mid[rows, :] = total
            normal, _ = norm_parts(total)
            normed[rows, :] = (normal * vec[5:6, :] + vec[6:7, :]).astype(LOW)

        by_rows(rows_of)

    columns = pl.ds(pl.multiple_of(step * TILE, TILE), TILE)
    v = dot_nn(normed[...], w_up[:, columns]) + up_bias[...]
    square = v * v
    inner = jnp.tanh(GELU * v * (1 + 0.044715 * square))
    half = 0.5 * (1 + inner)
    act[...] = (v * half).astype(LOW)
    slope[...] = (
        half + 0.5 * GELU * v * (1 - inner * inner) * (1 + 3 * 0.044715 * square)
    ).astype(LOW)


def mlp_up(scalars, heads, tok, vec, up_bias, blocks, other):
    tile = pl.BlockSpec((ROWS, TILE), lambda i, s: (0, i))
    return pl.pallas_call(
        mlp_up_kernel,
        grid_spec=pltpu.PrefetchScalarGridSpec(
            num_scalar_prefetch=1,
            grid=(FF // TILE,),
            in_specs=[
                full((ROWS, D)), full((ROWS, D)), full((28, D)),
                pl.BlockSpec((1, TILE), lambda i, s: (0, i)),
                anywhere(), anywhere(),
            ],
            out_specs=[full((ROWS, D)), full((ROWS, D)), tile, tile],
            scratch_shapes=[
                pltpu.VMEM((D, FF), LOW), pltpu.VMEM((D, D), LOW), pltpu.SemaphoreType.DMA((64,)),
            ],
        ),
        out_shape=[array((ROWS, D), F32), array((ROWS, D)), array((ROWS, FF)), array((ROWS, FF))],
        cost_estimate=cost(4 * 10**9, 16 * 10**6),
        compiler_params=pltpu.CompilerParams(vmem_limit_bytes=40 * MIB),
        name="mlp_up",
    )(scalars, heads, tok, vec, up_bias, blocks, other)


def down_grad_kernel(scalars, act, cot, send, keep):
    chip, core = scalars[0], scalars[1]
    result = lax.dot_general(
        act[...], cot[...], (((0,), (0,)), ((), ())), preferred_element_type=F32
    )
    for index in range(2):
        place = (pl.program_id(0) * 2 + index) ^ chip
        rows = pl.ds(pl.multiple_of(place * 96, 16), 96)
        first = result[index * 192 : index * 192 + 96].astype(LOW)
        second = result[index * 192 + 96 : index * 192 + 192].astype(LOW)
        keep[rows, :] = jnp.where(core == 0, first, second)
        send[rows, :] = jnp.where(core == 0, second, first)


def down_grad(scalars, act, cot):
    return pl.pallas_call(
        down_grad_kernel,
        grid_spec=pltpu.PrefetchScalarGridSpec(
            num_scalar_prefetch=1,
            grid=(8,),
            in_specs=[pl.BlockSpec((ROWS, WIDE), lambda i, s: (0, i)), full((ROWS, D))],
            out_specs=[full((FF // 2, D))] * 2,
        ),
        out_shape=[array((FF // 2, D))] * 2,
        cost_estimate=cost(3 * 10**9, 9 * 10**6),
        compiler_params=pltpu.CompilerParams(vmem_limit_bytes=32 * MIB),
        name="down_grad",
    )(scalars, act, cot)


def mlp_down_kernel(
    scalars, act, slope, mid, cot, vec, blocks, other, out, grad_up, bias_sum, weight, total, sems
):
    step = pl.program_id(0)

    @pl.when(step == 0)
    def _():
        copies = fetch(down_jobs(scalars, blocks, other, weight), sems)
        wait(copies)
        total[...] = mid[...] + vec[7:8, :]

    rows = pl.ds(pl.multiple_of(step * TILE, TILE), TILE)
    part = weight[rows, :]
    total[...] += dot_nn(act[...], part)
    grad = (dot_nt(cot[...], part) * slope[...].astype(F32)).astype(LOW)
    grad_up[...] = grad
    bias_sum[...] = jnp.sum(grad.astype(F32), axis=0, keepdims=True)

    @pl.when(step == FF // TILE - 1)
    def _():
        out[...] = total[...].astype(LOW)


def mlp_down(scalars, act, slope, mid, cot, vec, blocks, other):
    tile = pl.BlockSpec((ROWS, TILE), lambda i, s: (0, i))
    return pl.pallas_call(
        mlp_down_kernel,
        grid_spec=pltpu.PrefetchScalarGridSpec(
            num_scalar_prefetch=1,
            grid=(FF // TILE,),
            in_specs=[
                tile, tile, full((ROWS, D)), full((ROWS, D)), full((28, D)), anywhere(), anywhere(),
            ],
            out_specs=[full((ROWS, D)), tile, pl.BlockSpec((1, TILE), lambda i, s: (0, i))],
            scratch_shapes=[
                pltpu.VMEM((FF, D), LOW), pltpu.VMEM((ROWS, D), F32), pltpu.SemaphoreType.DMA((64,)),
            ],
        ),
        out_shape=[array((ROWS, D)), array((ROWS, FF)), array((1, FF), F32)],
        cost_estimate=cost(6 * 10**9, 16 * 10**6),
        compiler_params=pltpu.CompilerParams(vmem_limit_bytes=40 * MIB),
        name="mlp_down",
    )(scalars, act, slope, mid, cot, vec, blocks, other)


def mlp_back_kernel(
    scalars, grad_up, mid, cot, vec, blocks, other, grad_mid, grad_attn, grad_heads, sums,
    w_up, w_out, total, sems,
):
    step = pl.program_id(0)

    @pl.when(step == 0)
    def _():
        jobs = column_jobs(scalars, blocks, other, w_out, X_LAST, 1536, 384)
        jobs += column_jobs(scalars, blocks, other, w_up, X_LAST, 0, 1536)
        copies = fetch(jobs, sems)
        wait(copies)
        total[...] = jnp.zeros_like(total)

    columns = pl.ds(pl.multiple_of(step * TILE, TILE), TILE)
    total[...] += dot_nt(grad_up[...], w_up[:, columns])

    @pl.when(step == FF // TILE - 1)
    def _():
        sums[...] = jnp.zeros_like(sums)

        def rows_of(rows):
            normal, rate = norm_parts(mid[rows, :])
            grad = total[rows, :]
            outer = cot[rows, :].astype(F32)
            back = outer + norm_back(grad, normal, rate, vec[5:6, :])
            grad_mid[rows, :] = back
            low = back.astype(LOW)
            grad_attn[rows, :] = low
            sums[0:1, :] += jnp.sum(grad * normal, axis=0, keepdims=True)
            sums[1:2, :] += jnp.sum(grad, axis=0, keepdims=True)
            sums[2:3, :] += jnp.sum(low.astype(F32), axis=0, keepdims=True)
            sums[3:4, :] += jnp.sum(outer, axis=0, keepdims=True)

        by_rows(rows_of)
        grad_heads[...] = dot_nt(grad_attn[...], w_out[...]).astype(LOW)


def mlp_back(scalars, grad_up, mid, cot, vec, blocks, other):
    return pl.pallas_call(
        mlp_back_kernel,
        grid_spec=pltpu.PrefetchScalarGridSpec(
            num_scalar_prefetch=1,
            grid=(FF // TILE,),
            in_specs=[
                pl.BlockSpec((ROWS, TILE), lambda i, s: (0, i)),
                full((ROWS, D)), full((ROWS, D)), full((28, D)), anywhere(), anywhere(),
            ],
            out_specs=[full((ROWS, D))] * 3 + [full((8, D))],
            scratch_shapes=[
                pltpu.VMEM((D, FF), LOW), pltpu.VMEM((D, D), LOW), pltpu.VMEM((ROWS, D), F32),
                pltpu.SemaphoreType.DMA((64,)),
            ],
        ),
        out_shape=[array((ROWS, D), F32), array((ROWS, D)), array((ROWS, D)), array((8, D), F32)],
        cost_estimate=cost(4 * 10**9, 14 * 10**6),
        compiler_params=pltpu.CompilerParams(vmem_limit_bytes=40 * MIB),
        name="mlp_back",
    )(scalars, grad_up, mid, cot, vec, blocks, other)


def place_rows(result, target, chip):
    for index in range(16):
        rows = pl.ds(pl.multiple_of((index ^ chip) * 48, 16), 48)
        target[rows, :] = result[index * 48 : index * 48 + 48].astype(LOW)


def weight_grad_kernel(tiles, lefts, scalars, *refs):
    left_refs, right_refs = refs[: len(lefts)], refs[len(lefts) : 2 * len(lefts)]
    send, keep = refs[2 * len(lefts) : 2 * len(lefts) + 2]
    flipped = refs[2 * len(lefts) + 2 :]
    step = pl.program_id(0)
    chip = scalars[0]

    @pl.when(step == 0)
    def _():
        for left, flip in zip(left_refs, flipped):
            flip[...] = left[...].T

    local = jnp.where(step < tiles, step, step - tiles)
    for which, (first, last) in enumerate(lefts):

        @pl.when((local >= first) & (local < last))
        def _(which=which):
            result = dot_nn(flipped[which][...], right_refs[which][...])

            @pl.when(step < tiles)
            def _():
                place_rows(result, send, chip)

            @pl.when(step >= tiles)
            def _():
                place_rows(result, keep, chip)


def weight_grad(scalars, tiles, parts, name):
    def right_block(first, count):
        def index(i, s):
            local = jnp.clip(jnp.where(i < tiles, i, i - tiles) - first, 0, count - 1)
            side = jnp.where(i < tiles, 1 - s[1], s[1])
            return (0, side * count + local)

        return pl.BlockSpec((ROWS, WIDE), index)

    lefts = tuple((first, first + count) for _, _, first, count in parts)
    return pl.pallas_call(
        lambda *refs: weight_grad_kernel(tiles, lefts, *refs),
        grid_spec=pltpu.PrefetchScalarGridSpec(
            num_scalar_prefetch=1,
            grid=(2 * tiles,),
            in_specs=[full((ROWS, D))] * len(parts)
            + [right_block(first, count) for _, _, first, count in parts],
            out_specs=[
                pl.BlockSpec((D, WIDE), lambda i, s: (0, jnp.minimum(i, tiles - 1))),
                pl.BlockSpec((D, WIDE), lambda i, s: (0, jnp.maximum(i - tiles, 0))),
            ],
            scratch_shapes=[pltpu.VMEM((D, ROWS), LOW)] * len(parts),
        ),
        out_shape=[array((D, tiles * WIDE))] * 2,
        cost_estimate=cost(tiles * 6 * 10**8, 10 * 10**6),
        compiler_params=pltpu.CompilerParams(vmem_limit_bytes=32 * MIB),
        name=name,
    )(scalars, *[p[0] for p in parts], *[p[1] for p in parts])


def project_back_kernel(
    scalars, joined, tok, grad_mid, vec, blocks, other, out, sums, column_sums,
    weight, total, sems,
):
    step = pl.program_id(0)

    @pl.when(step == 0)
    def _():
        copies = fetch(column_jobs(scalars, blocks, other, weight, X_LAST, 0, 1152), sems)
        wait(copies)
        total[...] = jnp.zeros_like(total)

    columns = pl.ds(pl.multiple_of(step * TILE, TILE), TILE)
    total[...] += dot_nt(joined[...], weight[:, columns])
    column_sums[...] = jnp.sum(joined[...].astype(F32), axis=0, keepdims=True)

    @pl.when(step == 8)
    def _():
        sums[...] = jnp.zeros_like(sums)

        def rows_of(rows):
            normal, rate = norm_parts(tok[rows, :].astype(F32) + embed_row(scalars, vec))
            grad = total[rows, :]
            back = grad_mid[rows, :] + norm_back(grad, normal, rate, vec[0:1, :])
            out[rows, :] = back.astype(LOW)
            sums[0:1, :] += jnp.sum(grad * normal, axis=0, keepdims=True)
            sums[1:2, :] += jnp.sum(grad, axis=0, keepdims=True)
            sums[2:3, :] += jnp.sum(back, axis=0, keepdims=True)

        by_rows(rows_of)


def project_back(scalars, joined, tok, grad_mid, vec, blocks, other):
    return pl.pallas_call(
        project_back_kernel,
        grid_spec=pltpu.PrefetchScalarGridSpec(
            num_scalar_prefetch=1,
            grid=(9,),
            in_specs=[
                pl.BlockSpec((ROWS, TILE), lambda i, s: (0, i)),
                full((ROWS, D)), full((ROWS, D)), full((28, D)), anywhere(), anywhere(),
            ],
            out_specs=[
                full((ROWS, D)), full((8, D)), pl.BlockSpec((1, TILE), lambda i, s: (0, i)),
            ],
            scratch_shapes=[
                pltpu.VMEM((D, 3 * D), LOW), pltpu.VMEM((ROWS, D), F32), pltpu.SemaphoreType.DMA((32,)),
            ],
        ),
        out_shape=[array((ROWS, D)), array((8, D), F32), array((1, 3 * D), F32)],
        cost_estimate=cost(3 * 10**9, 12 * 10**6),
        compiler_params=pltpu.CompilerParams(vmem_limit_bytes=40 * MIB),
        name="project_back",
    )(scalars, joined, tok, grad_mid, vec, blocks, other)


def quick_shards(
    tokens, timesteps, starts, cotangent, ln1_gain, ln1_bias, w_qkv, bias_query,
    bias_value, w_out, bias_out, ln2_gain, ln2_bias, w_up, bias_up, w_down,
    bias_down, time_table,
):
    x, z, y, core = spot()
    chip = x * 8 + z * 2 + y
    me = chip * 2 + core
    sequence = ((lax.axis_index("dp") >> 1) << 1) | x

    notes = gather_small(jnp.concatenate([timesteps, starts[0]]))
    tokens_here = swap_in(tokens[0])

    shards_here = jnp.concatenate([w_qkv, w_up, w_out], axis=1)
    pair = join(core, shards_here, trade(shards_here, CORE), 0)
    half = lambda start, width: lax.dynamic_slice_in_dim(pair, start + core * width, width, 1)
    qkv_own = gather_direct(gather_z(half(0, 1152)))
    qkv_other = trade(qkv_own, CORE)
    rest = gather_z(
        jnp.concatenate(
            [half(2304, 1536), half(5376, 384), w_down[:48], w_down[48:]], axis=1
        )
    )
    up_own = gather_two(rest[:, :, :1920], Y, X)
    up_other = trade(up_own, CORE)
    down_own = gather_two(rest[:, :, 1920:], X, Y)
    down_other = trade(down_own, CORE)

    picks = pick_matrix(me, jnp.int32)
    notes = jnp.sum(picks[:, :, None] * notes[None], axis=1)
    every_times = notes[:16, 0]
    levels = jnp.arange(TSTEPS, dtype=jnp.int32)
    rows_of = dense((every_times[:, None] == levels[None, :]).astype(LOW), time_table).astype(LOW)
    vectors = (ln1_gain, ln1_bias, bias_query, bias_value, bias_out, ln2_gain, ln2_bias, bias_down)
    every = gather_small(jnp.concatenate(vectors + (bias_up, rows_of.reshape(-1))))
    every = dense(picks.astype(LOW), every)
    up_bias = every[:, 192:288].reshape(1, FF)
    vec = jnp.transpose(every.reshape(DEVICES, 28, 24), (1, 0, 2)).reshape(28, D)
    own_starts = lax.dynamic_slice_in_dim(notes, sequence, 1, 0)[0, 1:]
    scalars = jnp.concatenate([jnp.stack([chip, core, sequence]).astype(jnp.int32), own_starts])

    normed_one, query, kv = project(scalars, tokens_here, vec, qkv_own, qkv_other)
    kv_other = trade(kv, CORE)
    cot = swap_in(cotangent[0])
    heads_out, lse = attend(scalars, query, kv, kv_other)
    mid, normed_two, act, slope = mlp_up(
        scalars, heads_out, tokens_here, vec, up_bias, up_own, up_other
    )

    send, keep = down_grad(scalars, act, cot)
    grad_down = scatter_z(scatter_two(keep, trade(send, CORE), D, "x"))

    out, grad_up_low, up_sums = mlp_down(
        scalars, act, slope, mid, cot, vec, down_own, down_other
    )
    block_out = swap_out(out)
    grad_mid, grad_attn, grad_heads, mid_sums = mlp_back(
        scalars, grad_up_low, mid, cot, vec, up_own, up_other
    )
    send, keep = weight_grad(
        scalars, 5, ((normed_two, grad_up_low, 0, 4), (heads_out, grad_attn, 4, 1)), "up_grad"
    )
    grad_up_out = scatter_z(scatter_two(keep, trade(send, CORE), 1920, "y"))
    grad_up = settle(grad_up_out[:, :1536], core)
    grad_out_w = settle(grad_up_out[:, 1536:], core)

    dq, own, other = attend_back(scalars, query, grad_heads, lse, kv, kv_other)
    both = add_low(own, trade(other, CORE))
    joined = jnp.concatenate([dq, both[0], both[1]], axis=1)
    send, keep = weight_grad(scalars, 3, ((normed_one, joined, 0, 3),), "qkv_grad")
    grad_qkv = settle(scatter_z(scatter_direct(keep, trade(send, CORE), 1152)), core)
    grad_start, start_sums, joined_sums = project_back(
        scalars, joined, tokens_here, grad_mid, vec, qkv_own, qkv_other
    )
    grad_tokens = swap_out(grad_start)

    rows = jnp.concatenate(
        [start_sums[0:2], joined_sums[:, :D], joined_sums[:, 2 * D :], mid_sums[2:3],
         mid_sums[0:2], mid_sums[3:4]],
        axis=0,
    )
    ours = (jnp.arange(16, dtype=jnp.int32) == sequence).astype(F32)[:, None]
    tall = jnp.concatenate([rows, ours * start_sums[2:3]], axis=0)
    tall = jnp.transpose(tall.reshape(24, DEVICES, 24), (1, 0, 2)).reshape(DEVICES, 576)
    packed = jnp.concatenate([tall, up_sums.reshape(DEVICES, 96)], axis=1)
    packed = jnp.dot(picks.astype(F32).T, packed, precision=lax.Precision.HIGHEST)
    final = scatter_small(packed)
    vector = lambda k: final[24 * k : 24 * k + 24]
    hit = (every_times[None, :] == levels[:, None]).astype(F32)
    grad_table = jnp.dot(hit, final[192:576].reshape(16, 24), precision=lax.Precision.HIGHEST)
    return (
        block_out[None],
        grad_tokens[None],
        vector(0),
        vector(1),
        grad_qkv,
        vector(2),
        vector(3),
        grad_out_w,
        vector(4),
        vector(5),
        vector(6),
        grad_up,
        final[576:],
        grad_down,
        vector(7),
        grad_table,
    )


def solution(mesh):
    quick = mesh.shape["seq"] == 2 and mesh.shape["dp"] == 16
    return jax.shard_map(
        quick_shards if quick else shards,
        mesh=mesh,
        in_specs=(
            P("dp", "seq", None),
            P("dp"),
            P("dp", None),
            P("dp", "seq", None),
            P(("seq", "dp")),
            P(("seq", "dp")),
            P(("seq", "dp"), None),
            P(("seq", "dp")),
            P(("seq", "dp")),
            P(("seq", "dp"), None),
            P(("seq", "dp")),
            P(("seq", "dp")),
            P(("seq", "dp")),
            P(("seq", "dp"), None),
            P(("seq", "dp")),
            P(("seq", "dp"), None),
            P(("seq", "dp")),
            P(None, ("seq", "dp")),
        ),
        out_specs=(
            P("dp", "seq", None),
            P("dp", "seq", None),
            P(("seq", "dp")),
            P(("seq", "dp")),
            P(("seq", "dp"), None),
            P(("seq", "dp")),
            P(("seq", "dp")),
            P(("seq", "dp"), None),
            P(("seq", "dp")),
            P(("seq", "dp")),
            P(("seq", "dp")),
            P(("seq", "dp"), None),
            P(("seq", "dp")),
            P(("seq", "dp"), None),
            P(("seq", "dp")),
            P(None, ("seq", "dp")),
        ),
        check_vma=False,
    )
```

```python
import jax
import jax.numpy as jnp
from jax import lax
from jax.experimental import pallas as pl
from jax.experimental.pallas import tpu as pltpu
from jax.sharding import PartitionSpec as P


D = 768
HEADS = 12
HD = 64
TSTEPS = 1000
PIC = 256
NPIC = 2


epsilon = 1e-05


def layer_norm(values, gain, shift):
    average = jnp.mean(values, axis=-1, keepdims=True)
    centred = values - average
    spread = jnp.mean(centred * centred, axis=-1, keepdims=True)
    return centred * lax.rsqrt(spread + epsilon) * gain + shift


def piece_label(starts, places):
    inside = (places[None, None, :] >= starts[:, :, None]) & (
        places[None, None, :] < starts[:, :, None] + PIC
    )
    number = jnp.arange(1, NPIC + 1, dtype=jnp.int32)
    return jnp.sum(inside.astype(jnp.int32) * number[None, :, None], axis=1)


def visible_mask(starts, query_pos, key_pos):
    label_query = piece_label(starts, query_pos)
    label_key = piece_label(starts, key_pos)
    causal = query_pos[:, None] >= key_pos[None, :]
    return causal[None] | (label_query[:, :, None] == label_key[:, None, :]) & (
        label_query[:, :, None] > 0
    )


def dense(left, right):
    return jnp.dot(left, right, preferred_element_type=jnp.float32)


def dense_left(left, right):
    return lax.dot_general(
        left, right, (((0,), (0,)), ((), ())), preferred_element_type=jnp.float32
    )


def dense_right(left, right):
    return lax.dot_general(
        left, right, (((1,), (1,)), ((), ())), preferred_element_type=jnp.float32
    )


def head_slice(array, index):
    return lax.dynamic_slice_in_dim(array, index * HD, HD, 2)


def merge_heads(stacked):
    head_count, seq_count, row_count, head_size = stacked.shape
    return jnp.transpose(stacked, (1, 2, 0, 3)).reshape(
        seq_count, row_count, head_count * head_size
    )


def shards(
    tokens,
    timesteps,
    starts,
    cotangent,
    ln1_gain,
    ln1_bias,
    w_qkv,
    bias_query,
    bias_value,
    w_out,
    bias_out,
    ln2_gain,
    ln2_bias,
    w_up,
    bias_up,
    w_down,
    bias_down,
    time_table,
):
    gathered = (
        lax.all_gather(ln1_gain, ("seq", "dp"), axis=0, tiled=True),
        lax.all_gather(ln1_bias, ("seq", "dp"), axis=0, tiled=True),
        lax.all_gather(w_qkv, ("seq", "dp"), axis=0, tiled=True),
        lax.all_gather(bias_query, ("seq", "dp"), axis=0, tiled=True),
        lax.all_gather(bias_value, ("seq", "dp"), axis=0, tiled=True),
        lax.all_gather(w_out, ("seq", "dp"), axis=0, tiled=True),
        lax.all_gather(bias_out, ("seq", "dp"), axis=0, tiled=True),
        lax.all_gather(ln2_gain, ("seq", "dp"), axis=0, tiled=True),
        lax.all_gather(ln2_bias, ("seq", "dp"), axis=0, tiled=True),
        lax.all_gather(w_up, ("seq", "dp"), axis=0, tiled=True),
        lax.all_gather(bias_up, ("seq", "dp"), axis=0, tiled=True),
        lax.all_gather(w_down, ("seq", "dp"), axis=0, tiled=True),
        lax.all_gather(bias_down, ("seq", "dp"), axis=0, tiled=True),
        lax.all_gather(time_table, ("seq", "dp"), axis=1, tiled=True),
    )
    (
        gain_one,
        shift_one,
        qkv_full,
        query_shift,
        value_shift,
        out_full,
        out_shift,
        gain_two,
        shift_two,
        up_full,
        up_shift,
        down_full,
        down_shift,
        table_full,
    ) = gathered
    seq_count, row_count, model_width = tokens.shape
    flat_rows = seq_count * row_count
    scale = HD ** (-0.5)
    levels = jnp.arange(TSTEPS, dtype=jnp.int32)
    onehot = timesteps[:, None] == levels[None, :]
    embed = dense(onehot.astype(jnp.bfloat16), table_full)
    start_sum = (tokens.astype(jnp.float32) + embed[:, None, :]).reshape(flat_rows, model_width)
    norm_one, pull_one = jax.vjp(
        layer_norm, start_sum, gain_one.astype(jnp.float32), shift_one.astype(jnp.float32)
    )
    normed_one = norm_one.astype(jnp.bfloat16)
    joined = dense(normed_one, qkv_full)
    query = (
        (joined[:, :D] + query_shift.astype(jnp.float32))
        .astype(jnp.bfloat16)
        .reshape(seq_count, row_count, D)
    )
    keys = joined[:, D : 2 * D].astype(jnp.bfloat16).reshape(seq_count, row_count, D)
    values = (
        (joined[:, 2 * D :] + value_shift.astype(jnp.float32))
        .astype(jnp.bfloat16)
        .reshape(seq_count, row_count, D)
    )
    key_all, value_all = (
        lax.all_gather(keys, "seq", axis=1, tiled=True),
        lax.all_gather(values, "seq", axis=1, tiled=True),
    )
    full_len = key_all.shape[1]
    query_pos = lax.axis_index("seq") * row_count + jnp.arange(row_count, dtype=jnp.int32)
    every_pos = jnp.arange(full_len, dtype=jnp.int32)
    allowed = visible_mask(starts, query_pos, every_pos)

    def head_forward(index):
        query_head = head_slice(query, index)
        key_head = head_slice(key_all, index)
        value_head = head_slice(value_all, index)
        scores = scale * jnp.einsum(
            "sre,ske->srk", query_head, key_head, preferred_element_type=jnp.float32
        )
        scores = jnp.where(allowed, scores, -1e30)
        top = jnp.max(scores, axis=-1, keepdims=True)
        expo = jnp.exp(scores - top)
        total = jnp.sum(expo, axis=-1, keepdims=True)
        probs = expo / total
        result = jnp.einsum(
            "srk,ske->sre",
            probs.astype(jnp.bfloat16),
            value_head,
            preferred_element_type=jnp.float32,
        )
        return (result, top[..., 0] + jnp.log(total[..., 0]))

    head_out, log_total = lax.map(head_forward, jnp.arange(HEADS, dtype=jnp.int32))
    heads_out = merge_heads(head_out).astype(jnp.bfloat16).reshape(flat_rows, D)
    mid = start_sum + dense(heads_out, out_full) + out_shift.astype(jnp.float32)
    norm_two, pull_two = jax.vjp(
        layer_norm, mid, gain_two.astype(jnp.float32), shift_two.astype(jnp.float32)
    )
    normed_two = norm_two.astype(jnp.bfloat16)
    up_pre = dense(normed_two, up_full) + up_shift.astype(jnp.float32)
    act_value, pull_act = jax.vjp(jax.nn.gelu, up_pre)
    act = act_value.astype(jnp.bfloat16)
    block_out = (mid + dense(act, down_full) + down_shift.astype(jnp.float32)).astype(jnp.bfloat16)
    qkv_back, out_back, up_back, down_back = (
        lax.all_gather(w_qkv, ("seq", "dp"), axis=0, tiled=True),
        lax.all_gather(w_out, ("seq", "dp"), axis=0, tiled=True),
        lax.all_gather(w_up, ("seq", "dp"), axis=0, tiled=True),
        lax.all_gather(w_down, ("seq", "dp"), axis=0, tiled=True),
    )
    grad_mlp = cotangent.reshape(flat_rows, D)
    grad_down = dense_left(act, grad_mlp)
    grad_down_shift = jnp.sum(grad_mlp.astype(jnp.float32), axis=0)
    grad_act = dense_right(grad_mlp, down_back)
    (grad_up_pre,) = pull_act(grad_act)
    grad_up_low = grad_up_pre.astype(jnp.bfloat16)
    grad_up = dense_left(normed_two, grad_up_low)
    grad_up_shift = jnp.sum(grad_up_low.astype(jnp.float32), axis=0)
    grad_norm_two = dense_right(grad_up_low, up_back)
    grad_mid_norm, grad_gain_two, grad_shift_two = pull_two(grad_norm_two)
    grad_mid = cotangent.reshape(flat_rows, D).astype(jnp.float32) + grad_mid_norm
    grad_attn = grad_mid.astype(jnp.bfloat16)
    grad_out_w = dense_left(heads_out, grad_attn)
    grad_out_shift = jnp.sum(grad_attn.astype(jnp.float32), axis=0)
    grad_heads = (
        dense_right(grad_attn, out_back).astype(jnp.bfloat16).reshape(seq_count, row_count, D)
    )
    key_back, value_back = (
        lax.all_gather(keys, "seq", axis=1, tiled=True),
        lax.all_gather(values, "seq", axis=1, tiled=True),
    )

    def query_side(index, log_head):
        query_head = head_slice(query, index)
        key_head = head_slice(key_back, index)
        value_head = head_slice(value_back, index)
        grad_head = head_slice(grad_heads, index)
        scores = scale * jnp.einsum(
            "sre,ske->srk", query_head, key_head, preferred_element_type=jnp.float32
        )
        scores = jnp.where(allowed, scores, -1e30)
        probs = jnp.exp(scores - log_head[..., None])
        grad_probs = jnp.einsum(
            "sre,ske->srk", grad_head, value_head, preferred_element_type=jnp.float32
        )
        delta = jnp.sum(probs * grad_probs, axis=-1, keepdims=True)
        grad_scores = (probs * (grad_probs - delta)).astype(jnp.bfloat16)
        grad_query_head = scale * jnp.einsum(
            "srk,ske->sre", grad_scores, key_head, preferred_element_type=jnp.float32
        )
        return (probs, grad_scores, delta[..., 0], grad_query_head)

    def query_only(inputs):
        index, log_head = inputs
        _, _, delta, grad_query_head = query_side(index, log_head)
        return (grad_query_head, delta)

    grad_query_heads, delta_heads = lax.map(
        query_only, (jnp.arange(HEADS, dtype=jnp.int32), log_total)
    )
    query_every, grad_every, log_every, delta_every = (
        lax.all_gather(query, "seq", axis=1, tiled=True),
        lax.all_gather(grad_heads, "seq", axis=1, tiled=True),
        lax.all_gather(log_total.astype(jnp.bfloat16), "seq", axis=2, tiled=True).astype(
            log_total.dtype
        ),
        lax.all_gather(delta_heads.astype(jnp.bfloat16), "seq", axis=2, tiled=True).astype(
            delta_heads.dtype
        ),
    )
    key_allowed = visible_mask(starts, every_pos, query_pos)

    def key_side(inputs):
        index, log_head, delta_head = inputs
        query_head = head_slice(query_every, index)
        grad_head = head_slice(grad_every, index)
        key_head = head_slice(keys, index)
        value_head = head_slice(values, index)
        scores = scale * jnp.einsum(
            "sqe,ske->sqk", query_head, key_head, preferred_element_type=jnp.float32
        )
        scores = jnp.where(key_allowed, scores, -1e30)
        probs = jnp.exp(scores - log_head[..., None])
        grad_probs = jnp.einsum(
            "sqe,ske->sqk", grad_head, value_head, preferred_element_type=jnp.float32
        )
        grad_scores = (probs * (grad_probs - delta_head[..., None])).astype(jnp.bfloat16)
        grad_key_head = scale * jnp.einsum(
            "sqk,sqe->ske", grad_scores, query_head, preferred_element_type=jnp.float32
        )
        grad_value_head = jnp.einsum(
            "sqk,sqe->ske",
            probs.astype(jnp.bfloat16),
            grad_head,
            preferred_element_type=jnp.float32,
        )
        return (grad_key_head, grad_value_head)

    grad_key_heads, grad_value_heads = lax.map(
        key_side, (jnp.arange(HEADS, dtype=jnp.int32), log_every, delta_every)
    )
    grad_key_own = merge_heads(grad_key_heads)
    grad_value_own = merge_heads(grad_value_heads)
    grad_query_low = merge_heads(grad_query_heads).astype(jnp.bfloat16).reshape(flat_rows, D)
    grad_key_low = grad_key_own.astype(jnp.bfloat16).reshape(flat_rows, D)
    grad_value_low = grad_value_own.astype(jnp.bfloat16).reshape(flat_rows, D)
    grad_joined = jnp.concatenate([grad_query_low, grad_key_low, grad_value_low], axis=1)
    grad_qkv = dense_left(normed_one, grad_joined)
    grad_query_shift = jnp.sum(grad_query_low.astype(jnp.float32), axis=0)
    grad_value_shift = jnp.sum(grad_value_low.astype(jnp.float32), axis=0)
    grad_norm_one = dense_right(grad_joined, qkv_back)
    grad_start_norm, grad_gain_one, grad_shift_one = pull_one(grad_norm_one)
    grad_start = grad_mid + grad_start_norm
    grad_tokens = grad_start.astype(jnp.bfloat16).reshape(seq_count, row_count, D)
    seq_sums = jnp.sum(grad_start.reshape(seq_count, row_count, D), axis=1)
    every_sums, every_times = (
        lax.all_gather(seq_sums, ("seq", "dp"), axis=0, tiled=True),
        lax.all_gather(timesteps, ("seq", "dp"), axis=0, tiled=True),
    )
    own_width = D // lax.axis_size(("seq", "dp"))
    own_sums = lax.dynamic_slice_in_dim(
        every_sums, lax.axis_index(("seq", "dp")) * own_width, own_width, 1
    )
    every_onehot = (every_times[None, :] == levels[:, None]).astype(jnp.float32)
    grad_table = jnp.dot(every_onehot, own_sums, precision=lax.Precision.HIGHEST)
    summed = (
        lax.psum_scatter(grad_gain_one, ("seq", "dp"), scatter_dimension=0, tiled=True),
        lax.psum_scatter(grad_shift_one, ("seq", "dp"), scatter_dimension=0, tiled=True),
        lax.psum_scatter(grad_qkv, ("seq", "dp"), scatter_dimension=0, tiled=True),
        lax.psum_scatter(grad_query_shift, ("seq", "dp"), scatter_dimension=0, tiled=True),
        lax.psum_scatter(grad_value_shift, ("seq", "dp"), scatter_dimension=0, tiled=True),
        lax.psum_scatter(grad_out_w, ("seq", "dp"), scatter_dimension=0, tiled=True),
        lax.psum_scatter(grad_out_shift, ("seq", "dp"), scatter_dimension=0, tiled=True),
        lax.psum_scatter(grad_gain_two, ("seq", "dp"), scatter_dimension=0, tiled=True),
        lax.psum_scatter(grad_shift_two, ("seq", "dp"), scatter_dimension=0, tiled=True),
        lax.psum_scatter(grad_up, ("seq", "dp"), scatter_dimension=0, tiled=True),
        lax.psum_scatter(grad_up_shift, ("seq", "dp"), scatter_dimension=0, tiled=True),
        lax.psum_scatter(grad_down, ("seq", "dp"), scatter_dimension=0, tiled=True),
        lax.psum_scatter(grad_down_shift, ("seq", "dp"), scatter_dimension=0, tiled=True),
    )
    return (
        block_out.reshape(seq_count, row_count, D),
        grad_tokens,
        summed[0],
        summed[1],
        summed[2],
        summed[3],
        summed[4],
        summed[5],
        summed[6],
        summed[7],
        summed[8],
        summed[9],
        summed[10],
        summed[11],
        summed[12],
        grad_table,
    )


AXES = ("seq", "dp")
CORE, Y, Z0, Z1, X = 1, 2, 4, 8, 16
DEVICES = 32
QUARTER = 256
ROWS = 512
FF = 3072
TILE = 768
WIDE = 384
MIB = 2**20
F32 = jnp.float32
LOW = jnp.bfloat16

Z_MASKS = (0, Z0, Z1, Z0 | Z1)
X_LAST = tuple((xy | z) >> 1 for xy in (0, Y, X, X | Y) for z in Z_MASKS)
Y_LAST = tuple((xy | z) >> 1 for xy in (0, X, Y, X | Y) for z in Z_MASKS)


def send(array, pairs):
    return lax.ppermute(array, AXES, pairs)


def trade(array, mask):
    return send(array, [(i, i ^ mask) for i in range(DEVICES)])


def exchange(array):
    return lax.all_to_all(array, AXES, 0, 0, tiled=True)


def join(bit, own, other, axis):
    return jnp.where(
        bit == 0,
        jnp.concatenate([own, other], axis=axis),
        jnp.concatenate([other, own], axis=axis),
    )


def spot():
    x = lax.axis_index("seq")
    dp = lax.axis_index("dp")
    return x, dp >> 2, (dp >> 1) & 1, dp & 1


def hop_pairs(first):
    pairs = []
    for base in range(0, 16, 2):
        if first:
            moves = (((0, 0), (0, 1)), ((0, 1), (1, 0)), ((1, 0), (0, 0)))
        else:
            moves = (((1, 0), (0, 1)), ((1, 1), (1, 0)), ((0, 1), (1, 1)))
        for (sx, sc), (tx, tc) in moves:
            pairs.append((sx * 16 + base + sc, tx * 16 + base + tc))
    return pairs


def corners():
    x, _, _, core = spot()
    return (x == 0) & (core == 0), (x == 1) & (core == 1)


def swap_in(array):
    first, last = corners()
    front, back = array[:QUARTER], array[QUARTER:]
    one = send(jnp.where(first, back, front), hop_pairs(True))
    two = send(jnp.where(last, front, back), hop_pairs(False))
    low = jnp.where(first, front, jnp.where(last, two, one))
    high = jnp.where(first, one, jnp.where(last, back, two))
    return jnp.concatenate([low, high], axis=0)


def swap_out(array):
    first, last = corners()
    low, high = array[:QUARTER], array[QUARTER:]
    back_pairs = lambda which: [(t, s) for s, t in hop_pairs(which)]
    one = send(jnp.where(first, high, low), back_pairs(True))
    two = send(jnp.where(last, low, high), back_pairs(False))
    front = jnp.where(first, low, jnp.where(last, two, one))
    back = jnp.where(first, one, jnp.where(last, high, two))
    return jnp.concatenate([front, back], axis=0)


def gather_z(block):
    got = [trade(block, mask) for mask in Z_MASKS[1:]]
    return jnp.stack([block] + got, axis=0)


def gather_z_two(block):
    return grow(grow(block[None], Z0), Z1)


def grow(blocks, mask):
    return jnp.concatenate([blocks, trade(blocks, mask)], axis=0)


def gather_direct(blocks):
    got = [trade(blocks, m) for m in (Y, X, X | Y)]
    return jnp.concatenate([blocks] + got, axis=0)


def add_low(left, right):
    return (left.astype(F32) + right.astype(F32)).astype(LOW)


def scatter_two(keep, got, x_first):
    n = keep.shape[-1]
    cube = lambda array: array.reshape(2, 4, 2, -1, n)
    keep, got = cube(keep), cube(got)
    if x_first:
        away = trade(add_low(keep[1], got[1]), X)
        half = add_low(add_low(keep[0], got[0]), away)
        return add_low(half[:, 0], trade(half[:, 1], Y))
    away = trade(add_low(keep[:, :, 1], got[:, :, 1]), Y)
    half = add_low(add_low(keep[:, :, 0], got[:, :, 0]), away)
    return add_low(half[0], trade(half[1], X))


def scatter_direct(keep, got):
    n = keep.shape[-1]
    cube = lambda array: array.reshape(2, 4, 2, -1, n)
    keep, got = cube(keep), cube(got)
    total = keep[0, :, 0].astype(F32) + got[0, :, 0].astype(F32)
    for mask, a, b in ((Y, 0, 1), (X, 1, 0), (X | Y, 1, 1)):
        away = trade(add_low(keep[a, :, b], got[a, :, b]), mask)
        total = total + away.astype(F32)
    return total.astype(LOW)


def scatter_z(fours):
    total = fours[0].astype(F32)
    for place, mask in enumerate(Z_MASKS[1:], 1):
        total = total + trade(fours[place], mask).astype(F32)
    return total


def scatter_z_two(fours):
    half = add_low(fours[:2], trade(fours[2:], Z1))
    return half[0].astype(F32) + trade(half[1], Z0).astype(F32)


def settle(block, core):
    keep = lax.dynamic_slice_in_dim(block, core * 24, 24, 0)
    away = lax.dynamic_slice_in_dim(block, (1 - core) * 24, 24, 0)
    return keep, trade(away, CORE)


def dot_nt(left, right):
    return lax.dot_general(
        left, right, (((1,), (1,)), ((), ())), preferred_element_type=F32
    )


def dot_nn(left, right):
    return lax.dot_general(
        left, right, (((1,), (0,)), ((), ())), preferred_element_type=F32
    )


def inside_piece(place, start):
    return (place >= start) & (place < start + PIC)


def fill_bias(scalars, low_bias, high_bias):
    core, first, second = scalars[1], scalars[3], scalars[4]

    def fill(ref, chunk, key_start, query_start):
        shape = (QUARTER, QUARTER)
        key = key_start + lax.broadcasted_iota(jnp.int32, shape, 0)
        query = query_start + lax.broadcasted_iota(jnp.int32, shape, 1)
        seen = (
            (key <= query)
            | (inside_piece(key, first) & inside_piece(query, first))
            | (inside_piece(key, second) & inside_piece(query, second))
        )
        ref[pl.ds(chunk * QUARTER, QUARTER), :] = jnp.where(seen, 0.0, -1e30)

    mine, theirs = core * QUARTER, (1 - core) * QUARTER
    fill(low_bias, 0, mine, mine)
    fill(low_bias, 1, theirs, mine)
    half = 2 * QUARTER
    fill(high_bias, 0, mine, half + mine)
    fill(high_bias, 1, half + mine, half + mine)
    fill(high_bias, 2, theirs, half + mine)
    fill(high_bias, 3, half + theirs, half + mine)


def head_lanes(array, head):
    lane = lax.broadcasted_iota(jnp.int32, array.shape, 1)
    return jnp.where((lane >= HD) == (head == 1), array, jnp.zeros_like(array))


def key_sets(own, other):
    high = jnp.concatenate([own[...], other[...]], axis=0)
    low = jnp.concatenate([own[:QUARTER], other[:QUARTER]], axis=0)
    return low, high


def forward_kernel(scalars, q, k_own, k_other, v_own, v_other, out, lse, low_bias, high_bias):
    @pl.when(pl.program_id(0) == 0)
    def _():
        fill_bias(scalars, low_bias, high_bias)

    scale = HD ** (-0.5)
    keys, values = key_sets(k_own, k_other), key_sets(v_own, v_other)
    for part, bias in enumerate((low_bias, high_bias)):
        key, value_t = keys[part], values[part].T
        rows = pl.ds(part * QUARTER, QUARTER)
        query = q[rows, :] * jnp.bfloat16(scale)
        tops = []
        for head in range(2):
            scores = dot_nt(key, head_lanes(query, head)) + bias[...]
            top = jnp.max(scores, axis=0, keepdims=True)
            expo = jnp.exp(scores - top)
            total = jnp.sum(expo, axis=0, keepdims=True)
            mixed = dot_nn(value_t[head * HD : (head + 1) * HD], expo.astype(LOW))
            tops.append(mixed / total)
            lse[0, pl.ds(head, 1), rows] = top + jnp.log(total)
        both = jnp.concatenate(tops, axis=0)
        out[rows, :] = both.T.astype(LOW)


def backward_kernel(
    scalars, q, grad, lse, k_own, k_other, v_own, v_other,
    dq, own, other, low_bias, high_bias,
):
    @pl.when(pl.program_id(0) == 0)
    def _():
        fill_bias(scalars, low_bias, high_bias)

    scale = HD ** (-0.5)
    keys, values = key_sets(k_own, k_other), key_sets(v_own, v_other)
    sums = []
    for part, bias in enumerate((low_bias, high_bias)):
        key, value = keys[part], values[part]
        key_t = key.T
        rows = pl.ds(part * QUARTER, QUARTER)
        query = q[rows, :] * jnp.bfloat16(scale)
        grad_out = grad[rows, :]
        grad_query, grad_key, grad_value = [], 0.0, 0.0
        for head in range(2):
            query_head = head_lanes(query, head)
            grad_head = head_lanes(grad_out, head)
            scores = dot_nt(key, query_head) + bias[...]
            probs = jnp.exp(scores - lse[0, pl.ds(head, 1), rows])
            grad_probs = dot_nt(value, grad_head)
            delta = jnp.sum(probs * grad_probs, axis=0, keepdims=True)
            grad_scores = (probs * (grad_probs - delta)).astype(LOW)
            grad_value += dot_nn(probs.astype(LOW), grad_head)
            grad_key += dot_nn(grad_scores, query_head)
            grad_query.append(
                dot_nn(key_t[head * HD : (head + 1) * HD], grad_scores) * scale
            )
        dq[rows, :] = jnp.concatenate(grad_query, axis=0).T.astype(LOW)
        sums.append((grad_key, grad_value))
    for which in range(2):
        low, high = sums[0][which], sums[1][which]
        own[which, :QUARTER] = (low[:QUARTER] + high[:QUARTER]).astype(LOW)
        own[which, QUARTER:] = high[QUARTER : 2 * QUARTER].astype(LOW)
        other[which, :QUARTER] = (low[QUARTER:] + high[2 * QUARTER : 3 * QUARTER]).astype(LOW)
        other[which, QUARTER:] = high[3 * QUARTER :].astype(LOW)


PAIRS = HEADS // 2


PART = 2


def pair_block(skip=0):
    return pl.BlockSpec((ROWS, 2 * HD), lambda i, s: (0, i + skip))


def lse_block():
    return pl.BlockSpec((1, 2, ROWS), lambda i, s: (i, 0, 0))


def bias_scratch():
    return [
        pltpu.VMEM((2 * QUARTER, QUARTER), F32),
        pltpu.VMEM((4 * QUARTER, QUARTER), F32),
    ]


def cost(flops, size):
    return pl.CostEstimate(flops=flops, bytes_accessed=size, transcendentals=0)


def array(shape, dtype=LOW):
    return jax.ShapeDtypeStruct(shape, dtype)


def attend(scalars, q, kv, kv_other, part):
    skip = part * PART
    block = pair_block(skip)
    value = pair_block(skip + PAIRS)
    return pl.pallas_call(
        forward_kernel,
        grid_spec=pltpu.PrefetchScalarGridSpec(
            num_scalar_prefetch=1,
            grid=(PART,),
            in_specs=[block, block, block, value, value],
            out_specs=[pair_block(), lse_block()],
            scratch_shapes=bias_scratch(),
        ),
        out_shape=[array((ROWS, PART * 2 * HD)), array((PART, 2, ROWS), F32)],
        cost_estimate=cost(10**9, 2 * 10**6),
        compiler_params=pltpu.CompilerParams(vmem_limit_bytes=16 * MIB),
    )(scalars, q, kv, kv_other, kv, kv_other)


def attend_back(scalars, q, grad, lse, kv, kv_other):
    both = pl.BlockSpec((2, ROWS, 2 * HD), lambda i, s: (0, 0, i))
    return pl.pallas_call(
        backward_kernel,
        grid_spec=pltpu.PrefetchScalarGridSpec(
            num_scalar_prefetch=1,
            grid=(PAIRS,),
            in_specs=[pair_block()] * 2
            + [lse_block(), pair_block(), pair_block(), pair_block(PAIRS), pair_block(PAIRS)],
            out_specs=[pair_block(), both, both],
            scratch_shapes=bias_scratch(),
        ),
        out_shape=[array((ROWS, D)), array((2, ROWS, D)), array((2, ROWS, D))],
        cost_estimate=cost(2 * 10**10, 8 * 10**6),
        compiler_params=pltpu.CompilerParams(vmem_limit_bytes=18 * MIB),
        name="attend_back",
    )(scalars, q, grad, lse, kv, kv_other, kv, kv_other)


def fetch(jobs, sems):
    copies = [pltpu.make_async_copy(s, d, sems.at[i]) for i, (s, d) in enumerate(jobs)]
    for copy in copies:
        copy.start()
    return copies


def wait(copies):
    for copy in copies:
        copy.wait()


def column_jobs(scalars, source, other, target, masks, start, width, half, skip=0):
    chip, core = scalars[0], scalars[1]
    jobs = []
    for blocks, side in ((source, core), (other, 1 - core)):
        columns = pl.ds(pl.multiple_of(side * half + skip, 128), width)
        for j, mask in enumerate(masks):
            rows = pl.ds(pl.multiple_of((chip ^ mask) * 48, 16), 48)
            jobs.append((blocks.at[j, :, pl.ds(start, width)], target.at[rows, columns]))
    return jobs


UP_A = 1024


def up_jobs(scalars, pieces, w_up, w_out):
    a, b, a2, b2 = pieces
    jobs = column_jobs(scalars, b, b2, w_out, Y_LAST, 1536 - UP_A, 384, 384)
    jobs += column_jobs(scalars, a, a2, w_up, X_LAST, 0, UP_A, 1536)
    return jobs + column_jobs(scalars, b, b2, w_up, Y_LAST, 0, 1536 - UP_A, 1536, UP_A)


def down_jobs(scalars, pieces, target):
    chip, core = scalars[0], scalars[1]
    a, b, a2, b2 = pieces
    jobs = []
    for blocks, side, masks, half in (
        (a, core, X_LAST, 0), (b, core, Y_LAST, 1), (a2, 1 - core, X_LAST, 0), (b2, 1 - core, Y_LAST, 1)
    ):
        for j, mask in enumerate(masks):
            first = pl.multiple_of((chip ^ mask) * 192 + side * 96, 16)
            jobs.append((blocks.at[j], target.at[pl.ds(first, 96), pl.ds(half * 384, 384)]))
    return jobs


CHUNK = 128


def by_rows(body):
    @pl.loop(0, ROWS // CHUNK)
    def _(step):
        body(pl.ds(pl.multiple_of(step * CHUNK, CHUNK), CHUNK))


def norm_parts(values):
    average = jnp.mean(values, axis=-1, keepdims=True)
    centred = values - average
    rate = lax.rsqrt(jnp.mean(centred * centred, axis=-1, keepdims=True) + epsilon)
    return centred * rate, rate


def norm_back(grad, normal, rate, gain):
    scaled = grad * gain
    return rate * (
        scaled
        - jnp.mean(scaled, axis=-1, keepdims=True)
        - normal * jnp.mean(scaled * normal, axis=-1, keepdims=True)
    )


def full(shape):
    return pl.BlockSpec(shape, lambda i, s: (0,) * len(shape))


def anywhere():
    return pl.BlockSpec(memory_space=pl.ANY)


def spread(shape):
    column = lax.broadcasted_iota(jnp.int32, shape, len(shape) - 1)
    return column, column - column // 24 * 24


def project_kernel(scalars, tok, owned, blocks, other, vec, normed, q, kv, weight, sems):
    step = pl.program_id(0)

    @pl.when(step == 0)
    def _():
        copies = fetch(column_jobs(scalars, blocks, other, weight, X_LAST, 0, 1152, 1152), sems)
        _, inner = spread((24, D))
        place = (inner == lax.broadcasted_iota(jnp.int32, (24, D), 0)).astype(LOW)
        wide = dot_nn(owned[...].reshape(DEVICES * 16, 24), place).reshape(DEVICES, 16, D)
        column, _ = spread((DEVICES, 16, D))
        mine = column // 24 == lax.broadcasted_iota(jnp.int32, (DEVICES, 16, D), 0)
        vec[...] = jnp.sum(jnp.where(mine, wide, 0.0), axis=0)

        def rows_of(rows):
            normal, _ = norm_parts(tok[rows, :].astype(F32) + vec[12:13, :])
            normed[rows, :] = (normal * vec[0:1, :] + vec[1:2, :]).astype(LOW)

        by_rows(rows_of)
        wait(copies)

    columns = pl.ds(pl.multiple_of(step * D, D), D)
    result = dot_nn(normed[...], weight[:, columns])

    @pl.when(step < 1)
    def _():
        q[...] = (result + vec[2:3, :]).astype(LOW)

    @pl.when(step == 1)
    def _():
        kv[...] = result.astype(LOW)

    @pl.when(step == 2)
    def _():
        kv[...] = (result + vec[3:4, :]).astype(LOW)


def project(scalars, tok, owned, blocks, other):
    return pl.pallas_call(
        project_kernel,
        grid_spec=pltpu.PrefetchScalarGridSpec(
            num_scalar_prefetch=1,
            grid=(3,),
            in_specs=[full((ROWS, D)), full((DEVICES, 16, 24)), anywhere(), anywhere()],
            out_specs=[
                full((16, D)),
                full((ROWS, D)),
                full((ROWS, D)),
                pl.BlockSpec((ROWS, D), lambda i, s: (0, jnp.maximum(i - 1, 0))),
            ],
            scratch_shapes=[pltpu.VMEM((D, 3 * D), LOW), pltpu.SemaphoreType.DMA((32,))],
        ),
        out_shape=[array((16, D), F32), array((ROWS, D)), array((ROWS, D)), array((ROWS, 2 * D))],
        cost_estimate=cost(2 * 10**9, 8 * 10**6),
        compiler_params=pltpu.CompilerParams(vmem_limit_bytes=18 * MIB),
        name="project",
    )(scalars, tok, owned, blocks, other)


GELU = 0.7978845608028654


def mlp_up_kernel(
    scalars, heads, tok, vec, up_bias, a, b, a2, b2, mid, normed, act, slope,
    w_up, w_out, sems,
):
    step = pl.program_id(0)

    @pl.when(step == 0)
    def _():
        copies = fetch(up_jobs(scalars, (a, b, a2, b2), w_up, w_out), sems)
        wait(copies[:32])
        mid[...] = dot_nn(heads[...], w_out[...])

        def rows_of(rows):
            total = tok[rows, :].astype(F32) + vec[12:13, :] + mid[rows, :] + vec[4:5, :]
            mid[rows, :] = total
            normal, _ = norm_parts(total)
            normed[rows, :] = (normal * vec[5:6, :] + vec[6:7, :]).astype(LOW)

        by_rows(rows_of)
        wait(copies[32:])

    columns = pl.ds(pl.multiple_of(step * TILE, TILE), TILE)
    v = dot_nn(normed[...], w_up[:, columns]) + up_bias[...]
    square = v * v
    inner = jnp.tanh(GELU * v * (1 + 0.044715 * square))
    half = 0.5 * (1 + inner)
    act[...] = (v * half).astype(LOW)
    slope[...] = (
        half + 0.5 * GELU * v * (1 - inner * inner) * (1 + 3 * 0.044715 * square)
    ).astype(LOW)


def mlp_up(scalars, heads, tok, vec, up_bias, pieces):
    tile = pl.BlockSpec((ROWS, TILE), lambda i, s: (0, i))
    return pl.pallas_call(
        mlp_up_kernel,
        grid_spec=pltpu.PrefetchScalarGridSpec(
            num_scalar_prefetch=1,
            grid=(FF // TILE,),
            in_specs=[
                full((ROWS, D)), full((ROWS, D)), full((16, D)),
                pl.BlockSpec((1, TILE), lambda i, s: (0, i)),
            ] + [anywhere()] * 4,
            out_specs=[full((ROWS, D)), full((ROWS, D)), tile, tile],
            scratch_shapes=[
                pltpu.VMEM((D, FF), LOW), pltpu.VMEM((D, D), LOW), pltpu.SemaphoreType.DMA((96,)),
            ],
        ),
        out_shape=[array((ROWS, D), F32), array((ROWS, D)), array((ROWS, FF)), array((ROWS, FF))],
        cost_estimate=cost(4 * 10**9, 16 * 10**6),
        compiler_params=pltpu.CompilerParams(vmem_limit_bytes=24 * MIB),
        name="mlp_up",
    )(scalars, heads, tok, vec, up_bias, *pieces)


def down_grad_kernel(scalars, act, cot, send, keep):
    chip, core = scalars[0], scalars[1]
    result = lax.dot_general(
        act[...], cot[...], (((0,), (0,)), ((), ())), preferred_element_type=F32
    )
    for index in range(2):
        place = (pl.program_id(0) * 2 + index) ^ chip
        rows = pl.ds(pl.multiple_of(place * 96, 16), 96)
        first = result[index * 192 : index * 192 + 96].astype(LOW)
        second = result[index * 192 + 96 : index * 192 + 192].astype(LOW)
        keep[rows, :] = jnp.where(core == 0, first, second)
        send[rows, :] = jnp.where(core == 0, second, first)


def down_grad(scalars, act, cot):
    return pl.pallas_call(
        down_grad_kernel,
        grid_spec=pltpu.PrefetchScalarGridSpec(
            num_scalar_prefetch=1,
            grid=(8,),
            in_specs=[pl.BlockSpec((ROWS, WIDE), lambda i, s: (0, i)), full((ROWS, D))],
            out_specs=[full((FF // 2, D))] * 2,
        ),
        out_shape=[array((FF // 2, D))] * 2,
        cost_estimate=cost(3 * 10**9, 9 * 10**6),
        compiler_params=pltpu.CompilerParams(vmem_limit_bytes=16 * MIB),
        name="down_grad",
    )(scalars, act, cot)


TILES = FF // TILE


def mlp_mid_kernel(
    scalars, act, slope, mid, cot, vec, da, db, da2, db2, ua, ub, ua2, ub2,
    out, grad_up, bias_sum, grad_mid, grad_attn, grad_heads, sums,
    w_down, w_up, w_out, held, total, down_sems, up_sems,
):
    step = pl.program_id(0)
    down = lambda: [
        pltpu.make_async_copy(s, d, down_sems.at[i])
        for i, (s, d) in enumerate(down_jobs(scalars, (da, db, da2, db2), w_down))
    ]
    up = lambda: [
        pltpu.make_async_copy(s, d, up_sems.at[i])
        for i, (s, d) in enumerate(up_jobs(scalars, (ua, ub, ua2, ub2), w_up, w_out))
    ]

    @pl.when(step == 0)
    def _():
        copies = down()
        for copy in copies + up():
            copy.start()
        total[...] = mid[...] + vec[7:8, :]
        wait(copies)

    @pl.when(step < TILES)
    def _():
        rows = pl.ds(pl.multiple_of(step * TILE, TILE), TILE)
        part = w_down[rows, :]
        total[...] += dot_nn(act[...], part)
        grad = (dot_nt(cot[...], part) * slope[...].astype(F32)).astype(LOW)
        grad_up[...] = grad
        held[step] = grad
        bias_sum[...] = jnp.sum(grad.astype(F32), axis=0, keepdims=True)

    @pl.when(step == TILES)
    def _():
        out[...] = total[...].astype(LOW)
        total[...] = jnp.zeros_like(total)
        wait(up())

    @pl.when(step >= TILES)
    def _():
        local = step - TILES
        columns = pl.ds(pl.multiple_of(local * TILE, TILE), TILE)
        total[...] += dot_nt(held[local], w_up[:, columns])

    @pl.when(step == 2 * TILES - 1)
    def _():
        sums[...] = jnp.zeros_like(sums)

        def rows_of(rows):
            normal, rate = norm_parts(mid[rows, :])
            grad = total[rows, :]
            outer = cot[rows, :].astype(F32)
            back = outer + norm_back(grad, normal, rate, vec[5:6, :])
            grad_mid[rows, :] = back
            low = back.astype(LOW)
            grad_attn[rows, :] = low
            sums[0:1, :] += jnp.sum(grad * normal, axis=0, keepdims=True)
            sums[1:2, :] += jnp.sum(grad, axis=0, keepdims=True)
            sums[2:3, :] += jnp.sum(low.astype(F32), axis=0, keepdims=True)
            sums[3:4, :] += jnp.sum(outer, axis=0, keepdims=True)

        by_rows(rows_of)
        grad_heads[...] = dot_nt(grad_attn[...], w_out[...]).astype(LOW)


def mlp_mid(scalars, act, slope, mid, cot, vec, down_pieces, up_pieces):
    index = lambda i, s: (0, jnp.minimum(i, TILES - 1))
    tile = pl.BlockSpec((ROWS, TILE), index)
    return pl.pallas_call(
        mlp_mid_kernel,
        grid_spec=pltpu.PrefetchScalarGridSpec(
            num_scalar_prefetch=1,
            grid=(2 * TILES,),
            in_specs=[tile, tile, full((ROWS, D)), full((ROWS, D)), full((16, D))]
            + [anywhere()] * 8,
            out_specs=[full((ROWS, D)), tile, pl.BlockSpec((1, TILE), index)]
            + [full((ROWS, D))] * 3
            + [full((8, D))],
            scratch_shapes=[
                pltpu.VMEM((FF, D), LOW), pltpu.VMEM((D, FF), LOW), pltpu.VMEM((D, D), LOW),
                pltpu.VMEM((TILES, ROWS, TILE), LOW), pltpu.VMEM((ROWS, D), F32),
                pltpu.SemaphoreType.DMA((64,)), pltpu.SemaphoreType.DMA((96,)),
            ],
        ),
        out_shape=[
            array((ROWS, D)), array((ROWS, FF)), array((1, FF), F32), array((ROWS, D), F32),
            array((ROWS, D)), array((ROWS, D)), array((8, D), F32),
        ],
        cost_estimate=cost(10**10, 30 * 10**6),
        compiler_params=pltpu.CompilerParams(vmem_limit_bytes=38 * MIB),
        name="mlp_mid",
    )(scalars, act, slope, mid, cot, vec, *down_pieces, *up_pieces)


def place_rows(result, target, chip):
    for index in range(16):
        rows = pl.ds(pl.multiple_of((index ^ chip) * 48, 16), 48)
        target[rows, :] = result[index * 48 : index * 48 + 48].astype(LOW)


def weight_grad_kernel(tiles, lefts, scalars, *refs):
    left_refs, right_refs = refs[: len(lefts)], refs[len(lefts) : 2 * len(lefts)]
    send, keep = refs[2 * len(lefts) : 2 * len(lefts) + 2]
    flipped = refs[2 * len(lefts) + 2 :]
    step = pl.program_id(0)
    chip = scalars[0]

    @pl.when(step == 0)
    def _():
        for left, flip in zip(left_refs, flipped):
            flip[...] = left[...].T

    local = jnp.where(step < tiles, step, step - tiles)
    for which, (first, last) in enumerate(lefts):

        @pl.when((local >= first) & (local < last))
        def _(which=which):
            result = dot_nn(flipped[which][...], right_refs[which][...])

            @pl.when(step < tiles)
            def _():
                place_rows(result, send, chip)

            @pl.when(step >= tiles)
            def _():
                place_rows(result, keep, chip)


def weight_grad(scalars, tiles, parts):
    def right_block(first, count):
        def index(i, s):
            local = jnp.clip(jnp.where(i < tiles, i, i - tiles) - first, 0, count - 1)
            side = jnp.where(i < tiles, 1 - s[1], s[1])
            return (0, side * count + local)

        return pl.BlockSpec((ROWS, WIDE), index)

    lefts = tuple((first, first + count) for _, _, first, count in parts)
    return pl.pallas_call(
        lambda *refs: weight_grad_kernel(tiles, lefts, *refs),
        grid_spec=pltpu.PrefetchScalarGridSpec(
            num_scalar_prefetch=1,
            grid=(2 * tiles,),
            in_specs=[full((ROWS, D))] * len(parts)
            + [right_block(first, count) for _, _, first, count in parts],
            out_specs=[
                pl.BlockSpec((D, WIDE), lambda i, s: (0, jnp.minimum(i, tiles - 1))),
                pl.BlockSpec((D, WIDE), lambda i, s: (0, jnp.maximum(i - tiles, 0))),
            ],
            scratch_shapes=[pltpu.VMEM((D, ROWS), LOW)] * len(parts),
        ),
        out_shape=[array((D, tiles * WIDE))] * 2,
        cost_estimate=cost(tiles * 6 * 10**8, 10 * 10**6),
        compiler_params=pltpu.CompilerParams(vmem_limit_bytes=18 * MIB),
    )(scalars, *[p[0] for p in parts], *[p[1] for p in parts])


def project_back_kernel(
    scalars, joined, tok, grad_mid, vec, mid_sums, up_sums, blocks, other, out, payload,
    weight, total, sums, column_sums, sems,
):
    step = pl.program_id(0)

    @pl.when(step == 0)
    def _():
        copies = fetch(column_jobs(scalars, blocks, other, weight, X_LAST, 0, 1152, 1152), sems)
        total[...] = jnp.zeros_like(total)
        wait(copies)

    columns = pl.ds(pl.multiple_of(step * D, D), D)
    total[...] += dot_nt(joined[...], weight[:, columns])
    column_sums[:, columns] = jnp.sum(joined[...].astype(F32), axis=0, keepdims=True)

    @pl.when(step == 2)
    def _():
        sums[...] = jnp.zeros_like(sums)

        def rows_of(rows):
            normal, rate = norm_parts(tok[rows, :].astype(F32) + vec[12:13, :])
            grad = total[rows, :]
            back = grad_mid[rows, :] + norm_back(grad, normal, rate, vec[0:1, :])
            out[rows, :] = back.astype(LOW)
            sums[0:1, :] += jnp.sum(grad * normal, axis=0, keepdims=True)
            sums[1:2, :] += jnp.sum(grad, axis=0, keepdims=True)
            sums[12:13, :] += jnp.sum(back, axis=0, keepdims=True)

        by_rows(rows_of)
        sums[2:3, :] = column_sums[:, :D]
        sums[3:4, :] = column_sums[:, 2 * D :]
        sums[4:5, :] = mid_sums[2:3, :]
        sums[5:7, :] = mid_sums[0:2, :]
        sums[7:8, :] = mid_sums[3:4, :]
        _, inner = spread((24, D))
        place = (inner == lax.broadcasted_iota(jnp.int32, (24, D), 0)).astype(F32)
        column, _ = spread((DEVICES, 16, D))
        mine = column // 24 == lax.broadcasted_iota(jnp.int32, (DEVICES, 16, D), 0)
        wide = jnp.where(mine, sums[...][None], 0.0).reshape(DEVICES * 16, D)
        narrow = lax.dot_general(
            wide, place, (((1,), (1,)), ((), ())),
            precision=lax.Precision.HIGHEST, preferred_element_type=F32,
        )
        payload[...] = narrow.reshape(DEVICES, 16, 24)
        payload[:, 8:12, :] = up_sums[...]


def project_back(scalars, joined, tok, grad_mid, vec, mid_sums, up_sums, blocks, other):
    return pl.pallas_call(
        project_back_kernel,
        grid_spec=pltpu.PrefetchScalarGridSpec(
            num_scalar_prefetch=1,
            grid=(3,),
            in_specs=[
                pl.BlockSpec((ROWS, D), lambda i, s: (0, i)),
                full((ROWS, D)), full((ROWS, D)), full((16, D)), full((8, D)),
                full((DEVICES, 4, 24)), anywhere(), anywhere(),
            ],
            out_specs=[full((ROWS, D)), full((DEVICES, 16, 24))],
            scratch_shapes=[
                pltpu.VMEM((D, 3 * D), LOW), pltpu.VMEM((ROWS, D), F32), pltpu.VMEM((16, D), F32),
                pltpu.VMEM((1, 3 * D), F32), pltpu.SemaphoreType.DMA((32,)),
            ],
        ),
        out_shape=[array((ROWS, D)), array((DEVICES, 16, 24), F32)],
        cost_estimate=cost(3 * 10**9, 12 * 10**6),
        compiler_params=pltpu.CompilerParams(vmem_limit_bytes=26 * MIB),
        name="project_back",
    )(scalars, joined, tok, grad_mid, vec, mid_sums, up_sums, blocks, other)


def quick_shards(*arguments):
    return quick_step(*arguments)


def quick_step(
    tokens, timesteps, starts, cotangent, ln1_gain, ln1_bias, w_qkv, bias_query,
    bias_value, w_out, bias_out, ln2_gain, ln2_bias, w_up, bias_up, w_down,
    bias_down, time_table,
):
    x, z, y, core = spot()
    chip = x * 8 + z * 2 + y
    sequence = ((lax.axis_index("dp") >> 1) << 1) | x

    def chip_half(shard):
        rows = join(core, shard, trade(shard, CORE), 0)
        return lax.dynamic_slice_in_dim(rows, core * (shard.shape[1] // 2), shard.shape[1] // 2, 1)

    qkv_own = gather_direct(gather_z(chip_half(w_qkv)))
    qkv_other = trade(qkv_own, CORE)
    tokens_here = swap_in(tokens[0])
    rest = gather_z(jnp.concatenate([chip_half(w_up), chip_half(w_out)], axis=1))
    up_a = grow(grow(rest[:, :, :UP_A], Y), X)
    up_b = grow(grow(rest[:, :, UP_A:], X), Y)
    up_pieces = (up_a, up_b, trade(up_a, CORE), trade(up_b, CORE))
    cot = swap_in(cotangent[0])
    rest = gather_z_two(w_down)
    down_a = grow(grow(rest[:, :, :384], Y), X)
    down_b = grow(grow(rest[:, :, 384:], X), Y)
    down_pieces = (down_a, down_b, trade(down_a, CORE), trade(down_b, CORE))

    row = jnp.concatenate([timesteps, starts[0], jnp.zeros((5,), jnp.int32)])
    notes = exchange(jnp.broadcast_to(row, (DEVICES, 8)))
    times = jnp.broadcast_to(notes[:16, 0].reshape(8, 2).T[:, :, None], (2, 8, 2)).reshape(DEVICES)
    levels = jnp.arange(TSTEPS, dtype=jnp.int32)
    rows_of = dense((times[:, None] == levels[None, :]).astype(LOW), time_table).astype(LOW)
    vectors = (ln1_gain, ln1_bias, bias_query, bias_value, bias_out, ln2_gain, ln2_bias, bias_down)
    shared = jnp.concatenate(vectors + (bias_up,)).reshape(1, 12, 24)
    owned = jnp.concatenate(
        [jnp.broadcast_to(shared, (DEVICES, 12, 24)), rows_of[:, None], jnp.zeros((DEVICES, 3, 24), LOW)],
        axis=1,
    )
    owned = exchange(owned)
    up_bias = owned[:, 8:12].reshape(1, FF).astype(F32)
    own_starts = lax.dynamic_slice_in_dim(notes, sequence, 1, 0)[0, 1:3]
    scalars = jnp.concatenate([jnp.stack([chip, core, sequence]).astype(jnp.int32), own_starts])

    vec, normed_one, query, kv = project(scalars, tokens_here, owned, qkv_own, qkv_other)
    kv_other = trade(kv, CORE)
    parts = [attend(scalars, query, kv, kv_other, part) for part in range(PAIRS // PART)]
    heads_out = jnp.concatenate([part[0] for part in parts], axis=1)
    lse = jnp.concatenate([part[1] for part in parts], axis=0)
    mid, normed_two, act, slope = mlp_up(
        scalars, heads_out, tokens_here, vec, up_bias, up_pieces
    )

    away, keep = down_grad(scalars, act, cot)
    got = trade(away, CORE).reshape(16, 96, D)
    keep = keep.reshape(16, 96, D)
    fours = jnp.concatenate(
        [scatter_two(keep[:, :48], got[:, :48], True),
         scatter_two(keep[:, 48:], got[:, 48:], False)],
        axis=1,
    )
    grad_down = scatter_z_two(fours)

    out, grad_up_low, up_sums, grad_mid, grad_attn, grad_heads, mid_sums = mlp_mid(
        scalars, act, slope, mid, cot, vec, down_pieces, up_pieces
    )
    block_out = swap_out(out)
    away, keep = weight_grad(
        scalars, 5, ((normed_two, grad_up_low, 0, 4), (heads_out, grad_attn, 4, 1))
    )
    got = trade(away, CORE)
    fours = jnp.concatenate(
        [scatter_two(keep[:, :UP_A], got[:, :UP_A], True),
         scatter_two(keep[:, UP_A:], got[:, UP_A:], False)],
        axis=2,
    )
    keep, got = settle(scatter_z_two(fours), core)
    grad_up = join(core, keep[:, :1536], got[:, :1536], 1)
    grad_out_w = join(core, keep[:, 1536:], got[:, 1536:], 1)

    dq, own, other = attend_back(scalars, query, grad_heads, lse, kv, kv_other)
    both = add_low(own, trade(other, CORE))
    joined = jnp.concatenate([dq, both[0], both[1]], axis=1)
    away, keep = weight_grad(scalars, 3, ((normed_one, joined, 0, 3),))
    fours = scatter_direct(keep, trade(away, CORE))
    grad_qkv = join(core, *settle(scatter_z(fours), core), 1)
    grad_start, payload = project_back(
        scalars, joined, tokens_here, grad_mid, vec, mid_sums, up_sums.reshape(DEVICES, 4, 24),
        qkv_own, qkv_other,
    )
    grad_tokens = swap_out(grad_start)
    final = exchange(payload)
    summed = jnp.sum(final[:, :12], axis=0)
    hit = (times[None, :] == levels[:, None]).astype(F32)
    grad_table = jnp.dot(hit, final[:, 12], precision=lax.Precision.HIGHEST)
    return (
        block_out[None],
        grad_tokens[None],
        summed[0],
        summed[1],
        grad_qkv,
        summed[2],
        summed[3],
        grad_out_w,
        summed[4],
        summed[5],
        summed[6],
        grad_up,
        summed[8:].reshape(96),
        grad_down,
        summed[7],
        grad_table,
    )


def solution(mesh):
    quick = mesh.shape["seq"] == 2 and mesh.shape["dp"] == 16
    return jax.shard_map(
        quick_shards if quick else shards,
        mesh=mesh,
        in_specs=(
            P("dp", "seq", None),
            P("dp"),
            P("dp", None),
            P("dp", "seq", None),
            P(("seq", "dp")),
            P(("seq", "dp")),
            P(("seq", "dp"), None),
            P(("seq", "dp")),
            P(("seq", "dp")),
            P(("seq", "dp"), None),
            P(("seq", "dp")),
            P(("seq", "dp")),
            P(("seq", "dp")),
            P(("seq", "dp"), None),
            P(("seq", "dp")),
            P(("seq", "dp"), None),
            P(("seq", "dp")),
            P(None, ("seq", "dp")),
        ),
        out_specs=(
            P("dp", "seq", None),
            P("dp", "seq", None),
            P(("seq", "dp")),
            P(("seq", "dp")),
            P(("seq", "dp"), None),
            P(("seq", "dp")),
            P(("seq", "dp")),
            P(("seq", "dp"), None),
            P(("seq", "dp")),
            P(("seq", "dp")),
            P(("seq", "dp")),
            P(("seq", "dp"), None),
            P(("seq", "dp")),
            P(("seq", "dp"), None),
            P(("seq", "dp")),
            P(None, ("seq", "dp")),
        ),
        check_vma=False,
    )
```

```python
import jax
import jax.numpy as jnp
from jax import lax
from jax.experimental import pallas as pl
from jax.experimental.pallas import tpu as pltpu
from jax.sharding import PartitionSpec as P


D = 768
HEADS = 12
HD = 64
TSTEPS = 1000
PIC = 256
NPIC = 2


epsilon = 1e-05


def layer_norm(values, gain, shift):
    average = jnp.mean(values, axis=-1, keepdims=True)
    centred = values - average
    spread = jnp.mean(centred * centred, axis=-1, keepdims=True)
    return centred * lax.rsqrt(spread + epsilon) * gain + shift


def piece_label(starts, places):
    inside = (places[None, None, :] >= starts[:, :, None]) & (
        places[None, None, :] < starts[:, :, None] + PIC
    )
    number = jnp.arange(1, NPIC + 1, dtype=jnp.int32)
    return jnp.sum(inside.astype(jnp.int32) * number[None, :, None], axis=1)


def visible_mask(starts, query_pos, key_pos):
    label_query = piece_label(starts, query_pos)
    label_key = piece_label(starts, key_pos)
    causal = query_pos[:, None] >= key_pos[None, :]
    return causal[None] | (label_query[:, :, None] == label_key[:, None, :]) & (
        label_query[:, :, None] > 0
    )


def dense(left, right):
    return jnp.dot(left, right, preferred_element_type=jnp.float32)


def dense_left(left, right):
    return lax.dot_general(
        left, right, (((0,), (0,)), ((), ())), preferred_element_type=jnp.float32
    )


def dense_right(left, right):
    return lax.dot_general(
        left, right, (((1,), (1,)), ((), ())), preferred_element_type=jnp.float32
    )


def head_slice(array, index):
    return lax.dynamic_slice_in_dim(array, index * HD, HD, 2)


def merge_heads(stacked):
    head_count, seq_count, row_count, head_size = stacked.shape
    return jnp.transpose(stacked, (1, 2, 0, 3)).reshape(
        seq_count, row_count, head_count * head_size
    )


def shards(
    tokens,
    timesteps,
    starts,
    cotangent,
    ln1_gain,
    ln1_bias,
    w_qkv,
    bias_query,
    bias_value,
    w_out,
    bias_out,
    ln2_gain,
    ln2_bias,
    w_up,
    bias_up,
    w_down,
    bias_down,
    time_table,
):
    gathered = (
        lax.all_gather(ln1_gain, ("seq", "dp"), axis=0, tiled=True),
        lax.all_gather(ln1_bias, ("seq", "dp"), axis=0, tiled=True),
        lax.all_gather(w_qkv, ("seq", "dp"), axis=0, tiled=True),
        lax.all_gather(bias_query, ("seq", "dp"), axis=0, tiled=True),
        lax.all_gather(bias_value, ("seq", "dp"), axis=0, tiled=True),
        lax.all_gather(w_out, ("seq", "dp"), axis=0, tiled=True),
        lax.all_gather(bias_out, ("seq", "dp"), axis=0, tiled=True),
        lax.all_gather(ln2_gain, ("seq", "dp"), axis=0, tiled=True),
        lax.all_gather(ln2_bias, ("seq", "dp"), axis=0, tiled=True),
        lax.all_gather(w_up, ("seq", "dp"), axis=0, tiled=True),
        lax.all_gather(bias_up, ("seq", "dp"), axis=0, tiled=True),
        lax.all_gather(w_down, ("seq", "dp"), axis=0, tiled=True),
        lax.all_gather(bias_down, ("seq", "dp"), axis=0, tiled=True),
        lax.all_gather(time_table, ("seq", "dp"), axis=1, tiled=True),
    )
    (
        gain_one,
        shift_one,
        qkv_full,
        query_shift,
        value_shift,
        out_full,
        out_shift,
        gain_two,
        shift_two,
        up_full,
        up_shift,
        down_full,
        down_shift,
        table_full,
    ) = gathered
    seq_count, row_count, model_width = tokens.shape
    flat_rows = seq_count * row_count
    scale = HD ** (-0.5)
    levels = jnp.arange(TSTEPS, dtype=jnp.int32)
    onehot = timesteps[:, None] == levels[None, :]
    embed = dense(onehot.astype(jnp.bfloat16), table_full)
    start_sum = (tokens.astype(jnp.float32) + embed[:, None, :]).reshape(flat_rows, model_width)
    norm_one, pull_one = jax.vjp(
        layer_norm, start_sum, gain_one.astype(jnp.float32), shift_one.astype(jnp.float32)
    )
    normed_one = norm_one.astype(jnp.bfloat16)
    joined = dense(normed_one, qkv_full)
    query = (
        (joined[:, :D] + query_shift.astype(jnp.float32))
        .astype(jnp.bfloat16)
        .reshape(seq_count, row_count, D)
    )
    keys = joined[:, D : 2 * D].astype(jnp.bfloat16).reshape(seq_count, row_count, D)
    values = (
        (joined[:, 2 * D :] + value_shift.astype(jnp.float32))
        .astype(jnp.bfloat16)
        .reshape(seq_count, row_count, D)
    )
    key_all, value_all = (
        lax.all_gather(keys, "seq", axis=1, tiled=True),
        lax.all_gather(values, "seq", axis=1, tiled=True),
    )
    full_len = key_all.shape[1]
    query_pos = lax.axis_index("seq") * row_count + jnp.arange(row_count, dtype=jnp.int32)
    every_pos = jnp.arange(full_len, dtype=jnp.int32)
    allowed = visible_mask(starts, query_pos, every_pos)

    def head_forward(index):
        query_head = head_slice(query, index)
        key_head = head_slice(key_all, index)
        value_head = head_slice(value_all, index)
        scores = scale * jnp.einsum(
            "sre,ske->srk", query_head, key_head, preferred_element_type=jnp.float32
        )
        scores = jnp.where(allowed, scores, -1e30)
        top = jnp.max(scores, axis=-1, keepdims=True)
        expo = jnp.exp(scores - top)
        total = jnp.sum(expo, axis=-1, keepdims=True)
        probs = expo / total
        result = jnp.einsum(
            "srk,ske->sre",
            probs.astype(jnp.bfloat16),
            value_head,
            preferred_element_type=jnp.float32,
        )
        return (result, top[..., 0] + jnp.log(total[..., 0]))

    head_out, log_total = lax.map(head_forward, jnp.arange(HEADS, dtype=jnp.int32))
    heads_out = merge_heads(head_out).astype(jnp.bfloat16).reshape(flat_rows, D)
    mid = start_sum + dense(heads_out, out_full) + out_shift.astype(jnp.float32)
    norm_two, pull_two = jax.vjp(
        layer_norm, mid, gain_two.astype(jnp.float32), shift_two.astype(jnp.float32)
    )
    normed_two = norm_two.astype(jnp.bfloat16)
    up_pre = dense(normed_two, up_full) + up_shift.astype(jnp.float32)
    act_value, pull_act = jax.vjp(jax.nn.gelu, up_pre)
    act = act_value.astype(jnp.bfloat16)
    block_out = (mid + dense(act, down_full) + down_shift.astype(jnp.float32)).astype(jnp.bfloat16)
    qkv_back, out_back, up_back, down_back = (
        lax.all_gather(w_qkv, ("seq", "dp"), axis=0, tiled=True),
        lax.all_gather(w_out, ("seq", "dp"), axis=0, tiled=True),
        lax.all_gather(w_up, ("seq", "dp"), axis=0, tiled=True),
        lax.all_gather(w_down, ("seq", "dp"), axis=0, tiled=True),
    )
    grad_mlp = cotangent.reshape(flat_rows, D)
    grad_down = dense_left(act, grad_mlp)
    grad_down_shift = jnp.sum(grad_mlp.astype(jnp.float32), axis=0)
    grad_act = dense_right(grad_mlp, down_back)
    (grad_up_pre,) = pull_act(grad_act)
    grad_up_low = grad_up_pre.astype(jnp.bfloat16)
    grad_up = dense_left(normed_two, grad_up_low)
    grad_up_shift = jnp.sum(grad_up_low.astype(jnp.float32), axis=0)
    grad_norm_two = dense_right(grad_up_low, up_back)
    grad_mid_norm, grad_gain_two, grad_shift_two = pull_two(grad_norm_two)
    grad_mid = cotangent.reshape(flat_rows, D).astype(jnp.float32) + grad_mid_norm
    grad_attn = grad_mid.astype(jnp.bfloat16)
    grad_out_w = dense_left(heads_out, grad_attn)
    grad_out_shift = jnp.sum(grad_attn.astype(jnp.float32), axis=0)
    grad_heads = (
        dense_right(grad_attn, out_back).astype(jnp.bfloat16).reshape(seq_count, row_count, D)
    )
    key_back, value_back = (
        lax.all_gather(keys, "seq", axis=1, tiled=True),
        lax.all_gather(values, "seq", axis=1, tiled=True),
    )

    def query_side(index, log_head):
        query_head = head_slice(query, index)
        key_head = head_slice(key_back, index)
        value_head = head_slice(value_back, index)
        grad_head = head_slice(grad_heads, index)
        scores = scale * jnp.einsum(
            "sre,ske->srk", query_head, key_head, preferred_element_type=jnp.float32
        )
        scores = jnp.where(allowed, scores, -1e30)
        probs = jnp.exp(scores - log_head[..., None])
        grad_probs = jnp.einsum(
            "sre,ske->srk", grad_head, value_head, preferred_element_type=jnp.float32
        )
        delta = jnp.sum(probs * grad_probs, axis=-1, keepdims=True)
        grad_scores = (probs * (grad_probs - delta)).astype(jnp.bfloat16)
        grad_query_head = scale * jnp.einsum(
            "srk,ske->sre", grad_scores, key_head, preferred_element_type=jnp.float32
        )
        return (probs, grad_scores, delta[..., 0], grad_query_head)

    def query_only(inputs):
        index, log_head = inputs
        _, _, delta, grad_query_head = query_side(index, log_head)
        return (grad_query_head, delta)

    grad_query_heads, delta_heads = lax.map(
        query_only, (jnp.arange(HEADS, dtype=jnp.int32), log_total)
    )
    query_every, grad_every, log_every, delta_every = (
        lax.all_gather(query, "seq", axis=1, tiled=True),
        lax.all_gather(grad_heads, "seq", axis=1, tiled=True),
        lax.all_gather(log_total.astype(jnp.bfloat16), "seq", axis=2, tiled=True).astype(
            log_total.dtype
        ),
        lax.all_gather(delta_heads.astype(jnp.bfloat16), "seq", axis=2, tiled=True).astype(
            delta_heads.dtype
        ),
    )
    key_allowed = visible_mask(starts, every_pos, query_pos)

    def key_side(inputs):
        index, log_head, delta_head = inputs
        query_head = head_slice(query_every, index)
        grad_head = head_slice(grad_every, index)
        key_head = head_slice(keys, index)
        value_head = head_slice(values, index)
        scores = scale * jnp.einsum(
            "sqe,ske->sqk", query_head, key_head, preferred_element_type=jnp.float32
        )
        scores = jnp.where(key_allowed, scores, -1e30)
        probs = jnp.exp(scores - log_head[..., None])
        grad_probs = jnp.einsum(
            "sqe,ske->sqk", grad_head, value_head, preferred_element_type=jnp.float32
        )
        grad_scores = (probs * (grad_probs - delta_head[..., None])).astype(jnp.bfloat16)
        grad_key_head = scale * jnp.einsum(
            "sqk,sqe->ske", grad_scores, query_head, preferred_element_type=jnp.float32
        )
        grad_value_head = jnp.einsum(
            "sqk,sqe->ske",
            probs.astype(jnp.bfloat16),
            grad_head,
            preferred_element_type=jnp.float32,
        )
        return (grad_key_head, grad_value_head)

    grad_key_heads, grad_value_heads = lax.map(
        key_side, (jnp.arange(HEADS, dtype=jnp.int32), log_every, delta_every)
    )
    grad_key_own = merge_heads(grad_key_heads)
    grad_value_own = merge_heads(grad_value_heads)
    grad_query_low = merge_heads(grad_query_heads).astype(jnp.bfloat16).reshape(flat_rows, D)
    grad_key_low = grad_key_own.astype(jnp.bfloat16).reshape(flat_rows, D)
    grad_value_low = grad_value_own.astype(jnp.bfloat16).reshape(flat_rows, D)
    grad_joined = jnp.concatenate([grad_query_low, grad_key_low, grad_value_low], axis=1)
    grad_qkv = dense_left(normed_one, grad_joined)
    grad_query_shift = jnp.sum(grad_query_low.astype(jnp.float32), axis=0)
    grad_value_shift = jnp.sum(grad_value_low.astype(jnp.float32), axis=0)
    grad_norm_one = dense_right(grad_joined, qkv_back)
    grad_start_norm, grad_gain_one, grad_shift_one = pull_one(grad_norm_one)
    grad_start = grad_mid + grad_start_norm
    grad_tokens = grad_start.astype(jnp.bfloat16).reshape(seq_count, row_count, D)
    seq_sums = jnp.sum(grad_start.reshape(seq_count, row_count, D), axis=1)
    every_sums, every_times = (
        lax.all_gather(seq_sums, ("seq", "dp"), axis=0, tiled=True),
        lax.all_gather(timesteps, ("seq", "dp"), axis=0, tiled=True),
    )
    own_width = D // lax.axis_size(("seq", "dp"))
    own_sums = lax.dynamic_slice_in_dim(
        every_sums, lax.axis_index(("seq", "dp")) * own_width, own_width, 1
    )
    every_onehot = (every_times[None, :] == levels[:, None]).astype(jnp.float32)
    grad_table = jnp.dot(every_onehot, own_sums, precision=lax.Precision.HIGHEST)
    summed = (
        lax.psum_scatter(grad_gain_one, ("seq", "dp"), scatter_dimension=0, tiled=True),
        lax.psum_scatter(grad_shift_one, ("seq", "dp"), scatter_dimension=0, tiled=True),
        lax.psum_scatter(grad_qkv, ("seq", "dp"), scatter_dimension=0, tiled=True),
        lax.psum_scatter(grad_query_shift, ("seq", "dp"), scatter_dimension=0, tiled=True),
        lax.psum_scatter(grad_value_shift, ("seq", "dp"), scatter_dimension=0, tiled=True),
        lax.psum_scatter(grad_out_w, ("seq", "dp"), scatter_dimension=0, tiled=True),
        lax.psum_scatter(grad_out_shift, ("seq", "dp"), scatter_dimension=0, tiled=True),
        lax.psum_scatter(grad_gain_two, ("seq", "dp"), scatter_dimension=0, tiled=True),
        lax.psum_scatter(grad_shift_two, ("seq", "dp"), scatter_dimension=0, tiled=True),
        lax.psum_scatter(grad_up, ("seq", "dp"), scatter_dimension=0, tiled=True),
        lax.psum_scatter(grad_up_shift, ("seq", "dp"), scatter_dimension=0, tiled=True),
        lax.psum_scatter(grad_down, ("seq", "dp"), scatter_dimension=0, tiled=True),
        lax.psum_scatter(grad_down_shift, ("seq", "dp"), scatter_dimension=0, tiled=True),
    )
    return (
        block_out.reshape(seq_count, row_count, D),
        grad_tokens,
        summed[0],
        summed[1],
        summed[2],
        summed[3],
        summed[4],
        summed[5],
        summed[6],
        summed[7],
        summed[8],
        summed[9],
        summed[10],
        summed[11],
        summed[12],
        grad_table,
    )


AXES = ("seq", "dp")
CORE, Y, Z0, Z1, X = 1, 2, 4, 8, 16
DEVICES = 32
QUARTER = 256
ROWS = 512
FF = 3072
TILE = 768
WIDE = 384
MIB = 2**20
F32 = jnp.float32
LOW = jnp.bfloat16

Z_MASKS = (0, Z0, Z1, Z0 | Z1)
X_LAST = tuple((xy | z) >> 1 for xy in (0, Y, X, X | Y) for z in Z_MASKS)
Y_LAST = tuple((xy | z) >> 1 for xy in (0, X, Y, X | Y) for z in Z_MASKS)


def send(array, pairs):
    return lax.ppermute(array, AXES, pairs)


def trade(array, mask):
    return send(array, [(i, i ^ mask) for i in range(DEVICES)])


def exchange(array):
    return lax.all_to_all(array, AXES, 0, 0, tiled=True)


def join(bit, own, other, axis):
    return jnp.where(
        bit == 0,
        jnp.concatenate([own, other], axis=axis),
        jnp.concatenate([other, own], axis=axis),
    )


def spot():
    x = lax.axis_index("seq")
    dp = lax.axis_index("dp")
    return x, dp >> 2, (dp >> 1) & 1, dp & 1


def hop_pairs(first):
    pairs = []
    for base in range(0, 16, 2):
        if first:
            moves = (((0, 0), (0, 1)), ((0, 1), (1, 0)), ((1, 0), (0, 0)))
        else:
            moves = (((1, 0), (0, 1)), ((1, 1), (1, 0)), ((0, 1), (1, 1)))
        for (sx, sc), (tx, tc) in moves:
            pairs.append((sx * 16 + base + sc, tx * 16 + base + tc))
    return pairs


def corners():
    x, _, _, core = spot()
    return (x == 0) & (core == 0), (x == 1) & (core == 1)


def swap_in(array):
    first, last = corners()
    front, back = array[:QUARTER], array[QUARTER:]
    one = send(jnp.where(first, back, front), hop_pairs(True))
    two = send(jnp.where(last, front, back), hop_pairs(False))
    low = jnp.where(first, front, jnp.where(last, two, one))
    high = jnp.where(first, one, jnp.where(last, back, two))
    return jnp.concatenate([low, high], axis=0)


def swap_out(array):
    first, last = corners()
    low, high = array[:QUARTER], array[QUARTER:]
    back_pairs = lambda which: [(t, s) for s, t in hop_pairs(which)]
    one = send(jnp.where(first, high, low), back_pairs(True))
    two = send(jnp.where(last, low, high), back_pairs(False))
    front = jnp.where(first, low, jnp.where(last, two, one))
    back = jnp.where(first, one, jnp.where(last, high, two))
    return jnp.concatenate([front, back], axis=0)


def gather_z(block):
    got = [trade(block, mask) for mask in Z_MASKS[1:]]
    return jnp.stack([block] + got, axis=0)


def gather_z_two(block):
    return grow(grow(block[None], Z0), Z1)


def grow(blocks, mask):
    return jnp.concatenate([blocks, trade(blocks, mask)], axis=0)


def both_cores(pieces):
    return tuple(pieces) + tuple(trade(p, CORE) for p in pieces)


def add_low(left, right):
    return (left.astype(F32) + right.astype(F32)).astype(LOW)


def scatter_two(keep, got, x_first):
    n = keep.shape[-1]
    cube = lambda array: array.reshape(2, 4, 2, -1, n)
    keep, got = cube(keep), cube(got)
    if x_first:
        away = trade(add_low(keep[1], got[1]), X)
        half = add_low(add_low(keep[0], got[0]), away)
        away = trade(half[:, 1], Y)
        return add_low(half[:, 0], away)
    away = trade(add_low(keep[:, :, 1], got[:, :, 1]), Y)
    half = add_low(add_low(keep[:, :, 0], got[:, :, 0]), away)
    away = trade(half[1], X)
    return add_low(half[0], away)


def scatter_direct(keep, got):
    n = keep.shape[-1]
    cube = lambda array: array.reshape(2, 4, 2, -1, n)
    keep, got = cube(keep), cube(got)
    total = keep[0, :, 0].astype(F32) + got[0, :, 0].astype(F32)
    for mask, a, b in ((Y, 0, 1), (X, 1, 0), (X | Y, 1, 1)):
        away = trade(add_low(keep[a, :, b], got[a, :, b]), mask)
        total = total + away.astype(F32)
    return total.astype(LOW)


def scatter_z(fours):
    total = fours[0].astype(F32)
    for place, mask in enumerate(Z_MASKS[1:], 1):
        total = total + trade(fours[place], mask).astype(F32)
    return total


def scatter_z_two(fours):
    half = add_low(fours[:2], trade(fours[2:], Z1))
    return half[0].astype(F32) + trade(half[1], Z0).astype(F32)


def settle(block, core):
    keep = lax.dynamic_slice_in_dim(block, core * 24, 24, 0)
    away = lax.dynamic_slice_in_dim(block, (1 - core) * 24, 24, 0)
    return keep, trade(away, CORE)


def dot_nt(left, right):
    return lax.dot_general(
        left, right, (((1,), (1,)), ((), ())), preferred_element_type=F32
    )


def dot_nn(left, right):
    return lax.dot_general(
        left, right, (((1,), (0,)), ((), ())), preferred_element_type=F32
    )


def inside_piece(place, start):
    return (place >= start) & (place < start + PIC)


def fill_bias(scalars, low_bias, high_bias):
    core, first, second = scalars[1], scalars[3], scalars[4]

    def fill(ref, chunk, key_start, query_start):
        shape = (QUARTER, QUARTER)
        key = key_start + lax.broadcasted_iota(jnp.int32, shape, 0)
        query = query_start + lax.broadcasted_iota(jnp.int32, shape, 1)
        seen = (
            (key <= query)
            | (inside_piece(key, first) & inside_piece(query, first))
            | (inside_piece(key, second) & inside_piece(query, second))
        )
        ref[pl.ds(chunk * QUARTER, QUARTER), :] = jnp.where(seen, 0.0, -1e30)

    mine, theirs = core * QUARTER, (1 - core) * QUARTER
    fill(low_bias, 0, mine, mine)
    fill(low_bias, 1, theirs, mine)
    half = 2 * QUARTER
    fill(high_bias, 0, mine, half + mine)
    fill(high_bias, 1, half + mine, half + mine)
    fill(high_bias, 2, theirs, half + mine)
    fill(high_bias, 3, half + theirs, half + mine)


def head_lanes(array, head):
    lane = lax.broadcasted_iota(jnp.int32, array.shape, 1)
    return jnp.where((lane >= HD) == (head == 1), array, jnp.zeros_like(array))


def key_sets(own, other):
    high = jnp.concatenate([own[...], other[...]], axis=0)
    low = jnp.concatenate([own[:QUARTER], other[:QUARTER]], axis=0)
    return low, high


def forward_kernel(scalars, q, k_own, k_other, v_own, v_other, out, lse, low_bias, high_bias):
    @pl.when(pl.program_id(0) == 0)
    def _():
        fill_bias(scalars, low_bias, high_bias)

    scale = HD ** (-0.5)
    keys, values = key_sets(k_own, k_other), key_sets(v_own, v_other)
    for part, bias in enumerate((low_bias, high_bias)):
        key, value_t = keys[part], values[part].T
        rows = pl.ds(part * QUARTER, QUARTER)
        query = q[rows, :] * jnp.bfloat16(scale)
        tops = []
        for head in range(2):
            scores = dot_nt(key, head_lanes(query, head)) + bias[...]
            top = jnp.max(scores, axis=0, keepdims=True)
            expo = jnp.exp(scores - top)
            total = jnp.sum(expo, axis=0, keepdims=True)
            mixed = dot_nn(value_t[head * HD : (head + 1) * HD], expo.astype(LOW))
            tops.append(mixed / total)
            lse[0, pl.ds(head, 1), rows] = top + jnp.log(total)
        both = jnp.concatenate(tops, axis=0)
        out[rows, :] = both.T.astype(LOW)


def backward_kernel(
    scalars, q, grad, lse, k_own, k_other, v_own, v_other,
    dq, own, other, low_bias, high_bias,
):
    @pl.when(pl.program_id(0) == 0)
    def _():
        fill_bias(scalars, low_bias, high_bias)

    scale = HD ** (-0.5)
    keys, values = key_sets(k_own, k_other), key_sets(v_own, v_other)
    sums = []
    for part, bias in enumerate((low_bias, high_bias)):
        key, value = keys[part], values[part]
        key_t = key.T
        rows = pl.ds(part * QUARTER, QUARTER)
        query = q[rows, :] * jnp.bfloat16(scale)
        grad_out = grad[rows, :]
        grad_query, grad_key, grad_value = [], 0.0, 0.0
        for head in range(2):
            query_head = head_lanes(query, head)
            grad_head = head_lanes(grad_out, head)
            scores = dot_nt(key, query_head) + bias[...]
            probs = jnp.exp(scores - lse[0, pl.ds(head, 1), rows])
            grad_probs = dot_nt(value, grad_head)
            delta = jnp.sum(probs * grad_probs, axis=0, keepdims=True)
            grad_scores = (probs * (grad_probs - delta)).astype(LOW)
            grad_value += dot_nn(probs.astype(LOW), grad_head)
            grad_key += dot_nn(grad_scores, query_head)
            grad_query.append(
                dot_nn(key_t[head * HD : (head + 1) * HD], grad_scores) * scale
            )
        dq[rows, :] = jnp.concatenate(grad_query, axis=0).T.astype(LOW)
        sums.append((grad_key, grad_value))
    for which in range(2):
        low, high = sums[0][which], sums[1][which]
        own[which, :QUARTER] = (low[:QUARTER] + high[:QUARTER]).astype(LOW)
        own[which, QUARTER:] = high[QUARTER : 2 * QUARTER].astype(LOW)
        other[which, :QUARTER] = (low[QUARTER:] + high[2 * QUARTER : 3 * QUARTER]).astype(LOW)
        other[which, QUARTER:] = high[3 * QUARTER :].astype(LOW)


PAIRS = HEADS // 2


PART = 2


def pair_block(skip=0):
    return pl.BlockSpec((ROWS, 2 * HD), lambda i, s: (0, i + skip))


def lse_block():
    return pl.BlockSpec((1, 2, ROWS), lambda i, s: (i, 0, 0))


def bias_scratch():
    return [
        pltpu.VMEM((2 * QUARTER, QUARTER), F32),
        pltpu.VMEM((4 * QUARTER, QUARTER), F32),
    ]


def cost(flops, size):
    return pl.CostEstimate(flops=flops, bytes_accessed=size, transcendentals=0)


def array(shape, dtype=LOW):
    return jax.ShapeDtypeStruct(shape, dtype)


def attend(scalars, q, kv, kv_other, part):
    skip = part * PART
    block = pair_block(skip)
    value = pair_block(skip + PAIRS)
    return pl.pallas_call(
        forward_kernel,
        grid_spec=pltpu.PrefetchScalarGridSpec(
            num_scalar_prefetch=1,
            grid=(PART,),
            in_specs=[block, block, block, value, value],
            out_specs=[pair_block(), lse_block()],
            scratch_shapes=bias_scratch(),
        ),
        out_shape=[array((ROWS, PART * 2 * HD)), array((PART, 2, ROWS), F32)],
        cost_estimate=cost(10**9, 2 * 10**6),
        compiler_params=pltpu.CompilerParams(vmem_limit_bytes=16 * MIB),
    )(scalars, q, kv, kv_other, kv, kv_other)


def attend_back(scalars, q, grad, lse, kv, kv_other):
    both = pl.BlockSpec((2, ROWS, 2 * HD), lambda i, s: (0, 0, i))
    return pl.pallas_call(
        backward_kernel,
        grid_spec=pltpu.PrefetchScalarGridSpec(
            num_scalar_prefetch=1,
            grid=(PAIRS,),
            in_specs=[pair_block()] * 2
            + [lse_block(), pair_block(), pair_block(), pair_block(PAIRS), pair_block(PAIRS)],
            out_specs=[pair_block(), both, both],
            scratch_shapes=bias_scratch(),
        ),
        out_shape=[array((ROWS, D)), array((2, ROWS, D)), array((2, ROWS, D))],
        cost_estimate=cost(2 * 10**10, 8 * 10**6),
        compiler_params=pltpu.CompilerParams(vmem_limit_bytes=18 * MIB),
        name="attend_back",
    )(scalars, q, grad, lse, kv, kv_other, kv, kv_other)


def fetch(jobs, sems):
    copies = [pltpu.make_async_copy(s, d, sems.at[i]) for i, (s, d) in enumerate(jobs)]
    for copy in copies:
        copy.start()
    return copies


def wait(copies):
    for copy in copies:
        copy.wait()


def placed(pieces, masks):
    return [
        (ref, j, masks[start + j])
        for ref, start in zip(pieces, range(0, 16, 16 // len(pieces)))
        for j in range(16 // len(pieces))
    ]


def column_jobs(scalars, own, other, target, masks, start, width, half, skip=0):
    chip, core = scalars[0], scalars[1]
    jobs = []
    for pieces, side in ((own, core), (other, 1 - core)):
        columns = pl.ds(pl.multiple_of(side * half + skip, 128), width)
        for ref, j, mask in placed(pieces, masks):
            rows = pl.ds(pl.multiple_of((chip ^ mask) * 48, 16), 48)
            jobs.append((ref.at[j, :, pl.ds(start, width)], target.at[rows, columns]))
    return jobs


def qkv_jobs(scalars, pieces, weight):
    return column_jobs(scalars, pieces[:4], pieces[4:], weight, X_LAST, 0, 1152, 1152)


UP_A = 1024


def up_jobs(scalars, pieces, w_up, w_out):
    a, b, a2, b2 = pieces[:2], pieces[2:4], pieces[4:6], pieces[6:]
    jobs = column_jobs(scalars, b, b2, w_out, Y_LAST, 1536 - UP_A, 384, 384)
    jobs += column_jobs(scalars, a, a2, w_up, X_LAST, 0, UP_A, 1536)
    return jobs + column_jobs(scalars, b, b2, w_up, Y_LAST, 0, 1536 - UP_A, 1536, UP_A)


def down_jobs(scalars, pieces, target):
    chip, core = scalars[0], scalars[1]
    jobs = []
    for k, (side, masks, half) in enumerate(
        ((core, X_LAST, 0), (core, Y_LAST, 1), (1 - core, X_LAST, 0), (1 - core, Y_LAST, 1))
    ):
        for ref, j, mask in placed(pieces[2 * k : 2 * k + 2], masks):
            first = pl.multiple_of((chip ^ mask) * 192 + side * 96, 16)
            jobs.append((ref.at[j], target.at[pl.ds(first, 96), pl.ds(half * 384, 384)]))
    return jobs


CHUNK = 128


def by_rows(body):
    @pl.loop(0, ROWS // CHUNK)
    def _(step):
        body(pl.ds(pl.multiple_of(step * CHUNK, CHUNK), CHUNK))


def norm_parts(values):
    average = jnp.mean(values, axis=-1, keepdims=True)
    centred = values - average
    rate = lax.rsqrt(jnp.mean(centred * centred, axis=-1, keepdims=True) + epsilon)
    return centred * rate, rate


def norm_back(grad, normal, rate, gain):
    scaled = grad * gain
    return rate * (
        scaled
        - jnp.mean(scaled, axis=-1, keepdims=True)
        - normal * jnp.mean(scaled * normal, axis=-1, keepdims=True)
    )


def full(shape):
    return pl.BlockSpec(
        shape, lambda i, s: (0,) * len(shape), pipeline_mode=pl.Buffered(1)
    )


def anywhere():
    return pl.BlockSpec(memory_space=pl.ANY)


def spread(shape):
    column = lax.broadcasted_iota(jnp.int32, shape, len(shape) - 1)
    return column, column - column // 24 * 24


def project_kernel(scalars, tok, owned, *refs):
    pieces, (vec, normed, q, kv, weight, sems) = refs[:8], refs[8:]
    step = pl.program_id(0)

    @pl.when(step == 0)
    def _():
        copies = fetch(qkv_jobs(scalars, pieces, weight), sems)
        _, inner = spread((24, D))
        place = (inner == lax.broadcasted_iota(jnp.int32, (24, D), 0)).astype(LOW)
        wide = dot_nn(owned[...].reshape(DEVICES * 16, 24), place).reshape(DEVICES, 16, D)
        column, _ = spread((DEVICES, 16, D))
        mine = column // 24 == lax.broadcasted_iota(jnp.int32, (DEVICES, 16, D), 0)
        vec[...] = jnp.sum(jnp.where(mine, wide, 0.0), axis=0)

        def rows_of(rows):
            normal, _ = norm_parts(tok[rows, :].astype(F32) + vec[12:13, :])
            normed[rows, :] = (normal * vec[0:1, :] + vec[1:2, :]).astype(LOW)

        by_rows(rows_of)
        wait(copies)

    columns = pl.ds(pl.multiple_of(step * D, D), D)
    result = dot_nn(normed[...], weight[:, columns])

    @pl.when(step < 1)
    def _():
        q[...] = (result + vec[2:3, :]).astype(LOW)

    @pl.when(step == 1)
    def _():
        kv[...] = result.astype(LOW)

    @pl.when(step == 2)
    def _():
        kv[...] = (result + vec[3:4, :]).astype(LOW)


def project(scalars, tok, owned, pieces):
    return pl.pallas_call(
        project_kernel,
        grid_spec=pltpu.PrefetchScalarGridSpec(
            num_scalar_prefetch=1,
            grid=(3,),
            in_specs=[full((ROWS, D)), full((DEVICES, 16, 24))] + [anywhere()] * 8,
            out_specs=[
                full((16, D)),
                full((ROWS, D)),
                full((ROWS, D)),
                pl.BlockSpec((ROWS, D), lambda i, s: (0, jnp.maximum(i - 1, 0))),
            ],
            scratch_shapes=[pltpu.VMEM((D, 3 * D), LOW), pltpu.SemaphoreType.DMA((32,))],
        ),
        out_shape=[array((16, D), F32), array((ROWS, D)), array((ROWS, D)), array((ROWS, 2 * D))],
        cost_estimate=cost(2 * 10**9, 8 * 10**6),
        compiler_params=pltpu.CompilerParams(vmem_limit_bytes=18 * MIB),
        name="project",
    )(scalars, tok, owned, *pieces)


GELU = 0.7978845608028654


def mlp_up_kernel(scalars, heads, tok, vec, up_bias, *refs):
    pieces, (mid, normed, act, slope, w_up, w_out, sems) = refs[:8], refs[8:]
    step = pl.program_id(0)

    @pl.when(step == 0)
    def _():
        copies = fetch(up_jobs(scalars, pieces, w_up, w_out), sems)
        wait(copies[:32])
        mid[...] = dot_nn(heads[...], w_out[...])

        def rows_of(rows):
            total = tok[rows, :].astype(F32) + vec[12:13, :] + mid[rows, :] + vec[4:5, :]
            mid[rows, :] = total
            normal, _ = norm_parts(total)
            normed[rows, :] = (normal * vec[5:6, :] + vec[6:7, :]).astype(LOW)

        by_rows(rows_of)
        wait(copies[32:])

    columns = pl.ds(pl.multiple_of(step * TILE, TILE), TILE)
    v = dot_nn(normed[...], w_up[:, columns]) + up_bias[...]
    square = v * v
    inner = jnp.tanh(GELU * v * (1 + 0.044715 * square))
    half = 0.5 * (1 + inner)
    act[...] = (v * half).astype(LOW)
    slope[...] = (
        half + 0.5 * GELU * v * (1 - inner * inner) * (1 + 3 * 0.044715 * square)
    ).astype(LOW)


def mlp_up(scalars, heads, tok, vec, up_bias, pieces):
    tile = pl.BlockSpec((ROWS, TILE), lambda i, s: (0, i))
    return pl.pallas_call(
        mlp_up_kernel,
        grid_spec=pltpu.PrefetchScalarGridSpec(
            num_scalar_prefetch=1,
            grid=(FF // TILE,),
            in_specs=[
                full((ROWS, D)), full((ROWS, D)), full((16, D)),
                pl.BlockSpec((1, TILE), lambda i, s: (0, i)),
            ] + [anywhere()] * 8,
            out_specs=[full((ROWS, D)), full((ROWS, D)), tile, tile],
            scratch_shapes=[
                pltpu.VMEM((D, FF), LOW), pltpu.VMEM((D, D), LOW), pltpu.SemaphoreType.DMA((96,)),
            ],
        ),
        out_shape=[array((ROWS, D), F32), array((ROWS, D)), array((ROWS, FF)), array((ROWS, FF))],
        cost_estimate=cost(4 * 10**9, 16 * 10**6),
        compiler_params=pltpu.CompilerParams(vmem_limit_bytes=20 * MIB),
        name="mlp_up",
    )(scalars, heads, tok, vec, up_bias, *pieces)


def down_grad_kernel(scalars, act, cot, send, keep):
    chip, core = scalars[0], scalars[1]
    result = lax.dot_general(
        act[...], cot[...], (((0,), (0,)), ((), ())), preferred_element_type=F32
    )
    for index in range(2):
        place = (pl.program_id(0) * 2 + index) ^ chip
        rows = pl.ds(pl.multiple_of(place * 96, 16), 96)
        first = result[index * 192 : index * 192 + 96].astype(LOW)
        second = result[index * 192 + 96 : index * 192 + 192].astype(LOW)
        keep[rows, :] = jnp.where(core == 0, first, second)
        send[rows, :] = jnp.where(core == 0, second, first)


def down_grad(scalars, act, cot):
    return pl.pallas_call(
        down_grad_kernel,
        grid_spec=pltpu.PrefetchScalarGridSpec(
            num_scalar_prefetch=1,
            grid=(8,),
            in_specs=[pl.BlockSpec((ROWS, WIDE), lambda i, s: (0, i)), full((ROWS, D))],
            out_specs=[full((FF // 2, D))] * 2,
        ),
        out_shape=[array((FF // 2, D))] * 2,
        cost_estimate=cost(3 * 10**9, 9 * 10**6),
        compiler_params=pltpu.CompilerParams(vmem_limit_bytes=16 * MIB),
        name="down_grad",
    )(scalars, act, cot)


TILES = FF // TILE


def mlp_mid_kernel(scalars, act, slope, mid, cot, vec, *refs):
    down_pieces, up_pieces, refs = refs[:8], refs[8:16], refs[16:]
    out, grad_up, bias_sum, grad_mid, grad_attn, grad_heads, sums = refs[:7]
    w_down, w_up, w_out, held, total, down_sems, up_sems = refs[7:]
    step = pl.program_id(0)
    down = lambda: [
        pltpu.make_async_copy(s, d, down_sems.at[i])
        for i, (s, d) in enumerate(down_jobs(scalars, down_pieces, w_down))
    ]
    up = lambda: [
        pltpu.make_async_copy(s, d, up_sems.at[i])
        for i, (s, d) in enumerate(up_jobs(scalars, up_pieces, w_up, w_out))
    ]

    @pl.when(step == 0)
    def _():
        copies = down()
        for copy in copies + up():
            copy.start()
        total[...] = mid[...] + vec[7:8, :]
        wait(copies)

    @pl.when(step < TILES)
    def _():
        rows = pl.ds(pl.multiple_of(step * TILE, TILE), TILE)
        part = w_down[rows, :]
        total[...] += dot_nn(act[...], part)
        grad = (dot_nt(cot[...], part) * slope[...].astype(F32)).astype(LOW)
        grad_up[...] = grad
        held[step] = grad
        bias_sum[...] = jnp.sum(grad.astype(F32), axis=0, keepdims=True)

    @pl.when(step == TILES)
    def _():
        out[...] = total[...].astype(LOW)
        total[...] = jnp.zeros_like(total)
        wait(up())

    @pl.when(step >= TILES)
    def _():
        local = step - TILES
        columns = pl.ds(pl.multiple_of(local * TILE, TILE), TILE)
        total[...] += dot_nt(held[local], w_up[:, columns])

    @pl.when(step == 2 * TILES - 1)
    def _():
        sums[...] = jnp.zeros_like(sums)

        def rows_of(rows):
            normal, rate = norm_parts(mid[rows, :])
            grad = total[rows, :]
            outer = cot[rows, :].astype(F32)
            back = outer + norm_back(grad, normal, rate, vec[5:6, :])
            grad_mid[rows, :] = back
            low = back.astype(LOW)
            grad_attn[rows, :] = low
            sums[0:1, :] += jnp.sum(grad * normal, axis=0, keepdims=True)
            sums[1:2, :] += jnp.sum(grad, axis=0, keepdims=True)
            sums[2:3, :] += jnp.sum(low.astype(F32), axis=0, keepdims=True)
            sums[3:4, :] += jnp.sum(outer, axis=0, keepdims=True)

        by_rows(rows_of)
        grad_heads[...] = dot_nt(grad_attn[...], w_out[...]).astype(LOW)


def mlp_mid(scalars, act, slope, mid, cot, vec, down_pieces, up_pieces):
    index = lambda i, s: (0, jnp.minimum(i, TILES - 1))
    tile = pl.BlockSpec((ROWS, TILE), index)
    return pl.pallas_call(
        mlp_mid_kernel,
        grid_spec=pltpu.PrefetchScalarGridSpec(
            num_scalar_prefetch=1,
            grid=(2 * TILES,),
            in_specs=[tile, tile, full((ROWS, D)), full((ROWS, D)), full((16, D))]
            + [anywhere()] * 16,
            out_specs=[full((ROWS, D)), tile, pl.BlockSpec((1, TILE), index)]
            + [full((ROWS, D))] * 3
            + [full((8, D))],
            scratch_shapes=[
                pltpu.VMEM((FF, D), LOW), pltpu.VMEM((D, FF), LOW), pltpu.VMEM((D, D), LOW),
                pltpu.VMEM((TILES, ROWS, TILE), LOW), pltpu.VMEM((ROWS, D), F32),
                pltpu.SemaphoreType.DMA((64,)), pltpu.SemaphoreType.DMA((96,)),
            ],
        ),
        out_shape=[
            array((ROWS, D)), array((ROWS, FF)), array((1, FF), F32), array((ROWS, D), F32),
            array((ROWS, D)), array((ROWS, D)), array((8, D), F32),
        ],
        cost_estimate=cost(10**10, 30 * 10**6),
        compiler_params=pltpu.CompilerParams(vmem_limit_bytes=31 * MIB),
        name="mlp_mid",
    )(scalars, act, slope, mid, cot, vec, *down_pieces, *up_pieces)


def place_rows(result, target, chip):
    for index in range(16):
        rows = pl.ds(pl.multiple_of((index ^ chip) * 48, 16), 48)
        target[rows, :] = result[index * 48 : index * 48 + 48].astype(LOW)


def weight_grad_kernel(tiles, lefts, scalars, *refs):
    left_refs, right_refs = refs[: len(lefts)], refs[len(lefts) : 2 * len(lefts)]
    send, keep = refs[2 * len(lefts) : 2 * len(lefts) + 2]
    flipped = refs[2 * len(lefts) + 2 :]
    step = pl.program_id(0)
    chip = scalars[0]

    @pl.when(step == 0)
    def _():
        for left, flip in zip(left_refs, flipped):
            flip[...] = left[...].T

    local = jnp.where(step < tiles, step, step - tiles)
    for which, (first, last) in enumerate(lefts):

        @pl.when((local >= first) & (local < last))
        def _(which=which):
            result = dot_nn(flipped[which][...], right_refs[which][...])

            @pl.when(step < tiles)
            def _():
                place_rows(result, send, chip)

            @pl.when(step >= tiles)
            def _():
                place_rows(result, keep, chip)


def weight_grad(scalars, tiles, parts):
    def right_block(first, count):
        def index(i, s):
            local = jnp.clip(jnp.where(i < tiles, i, i - tiles) - first, 0, count - 1)
            side = jnp.where(i < tiles, 1 - s[1], s[1])
            return (0, side * count + local)

        return pl.BlockSpec((ROWS, WIDE), index)

    lefts = tuple((first, first + count) for _, _, first, count in parts)
    return pl.pallas_call(
        lambda *refs: weight_grad_kernel(tiles, lefts, *refs),
        grid_spec=pltpu.PrefetchScalarGridSpec(
            num_scalar_prefetch=1,
            grid=(2 * tiles,),
            in_specs=[full((ROWS, D))] * len(parts)
            + [right_block(first, count) for _, _, first, count in parts],
            out_specs=[
                pl.BlockSpec((D, WIDE), lambda i, s: (0, jnp.minimum(i, tiles - 1))),
                pl.BlockSpec((D, WIDE), lambda i, s: (0, jnp.maximum(i - tiles, 0))),
            ],
            scratch_shapes=[pltpu.VMEM((D, ROWS), LOW)] * len(parts),
        ),
        out_shape=[array((D, tiles * WIDE))] * 2,
        cost_estimate=cost(tiles * 6 * 10**8, 10 * 10**6),
        compiler_params=pltpu.CompilerParams(vmem_limit_bytes=18 * MIB),
    )(scalars, *[p[0] for p in parts], *[p[1] for p in parts])


def project_back_kernel(scalars, joined, tok, grad_mid, vec, mid_sums, up_sums, *refs):
    pieces, (out, payload, weight, total, sums, column_sums, sems) = refs[:8], refs[8:]
    step = pl.program_id(0)

    @pl.when(step == 0)
    def _():
        copies = fetch(qkv_jobs(scalars, pieces, weight), sems)
        total[...] = jnp.zeros_like(total)
        wait(copies)

    columns = pl.ds(pl.multiple_of(step * D, D), D)
    total[...] += dot_nt(joined[...], weight[:, columns])
    column_sums[:, columns] = jnp.sum(joined[...].astype(F32), axis=0, keepdims=True)

    @pl.when(step == 2)
    def _():
        sums[...] = jnp.zeros_like(sums)

        def rows_of(rows):
            normal, rate = norm_parts(tok[rows, :].astype(F32) + vec[12:13, :])
            grad = total[rows, :]
            back = grad_mid[rows, :] + norm_back(grad, normal, rate, vec[0:1, :])
            out[rows, :] = back.astype(LOW)
            sums[0:1, :] += jnp.sum(grad * normal, axis=0, keepdims=True)
            sums[1:2, :] += jnp.sum(grad, axis=0, keepdims=True)
            sums[12:13, :] += jnp.sum(back, axis=0, keepdims=True)

        by_rows(rows_of)
        sums[2:3, :] = column_sums[:, :D]
        sums[3:4, :] = column_sums[:, 2 * D :]
        sums[4:5, :] = mid_sums[2:3, :]
        sums[5:7, :] = mid_sums[0:2, :]
        sums[7:8, :] = mid_sums[3:4, :]
        _, inner = spread((24, D))
        place = (inner == lax.broadcasted_iota(jnp.int32, (24, D), 0)).astype(F32)
        column, _ = spread((DEVICES, 16, D))
        mine = column // 24 == lax.broadcasted_iota(jnp.int32, (DEVICES, 16, D), 0)
        wide = jnp.where(mine, sums[...][None], 0.0).reshape(DEVICES * 16, D)
        narrow = lax.dot_general(
            wide, place, (((1,), (1,)), ((), ())),
            precision=lax.Precision.HIGHEST, preferred_element_type=F32,
        )
        payload[...] = narrow.reshape(DEVICES, 16, 24)
        column = lax.broadcasted_iota(jnp.int32, (DEVICES * 4, FF), 1)
        mine = column // 24 == lax.broadcasted_iota(jnp.int32, (DEVICES * 4, FF), 0)
        inner = lax.broadcasted_iota(jnp.int32, (24, FF), 1)
        inner = inner - inner // 24 * 24
        place = (inner == lax.broadcasted_iota(jnp.int32, (24, FF), 0)).astype(F32)
        narrow = lax.dot_general(
            jnp.where(mine, up_sums[...], 0.0), place, (((1,), (1,)), ((), ())),
            precision=lax.Precision.HIGHEST, preferred_element_type=F32,
        )
        payload[:, 8:12, :] = narrow.reshape(DEVICES, 4, 24)


def project_back(scalars, joined, tok, grad_mid, vec, mid_sums, up_sums, pieces):
    return pl.pallas_call(
        project_back_kernel,
        grid_spec=pltpu.PrefetchScalarGridSpec(
            num_scalar_prefetch=1,
            grid=(3,),
            in_specs=[
                pl.BlockSpec((ROWS, D), lambda i, s: (0, i)),
                full((ROWS, D)), full((ROWS, D)), full((16, D)), full((8, D)),
                full((1, FF)),
            ] + [anywhere()] * 8,
            out_specs=[full((ROWS, D)), full((DEVICES, 16, 24))],
            scratch_shapes=[
                pltpu.VMEM((D, 3 * D), LOW), pltpu.VMEM((ROWS, D), F32), pltpu.VMEM((16, D), F32),
                pltpu.VMEM((1, 3 * D), F32), pltpu.SemaphoreType.DMA((32,)),
            ],
        ),
        out_shape=[array((ROWS, D)), array((DEVICES, 16, 24), F32)],
        cost_estimate=cost(3 * 10**9, 12 * 10**6),
        compiler_params=pltpu.CompilerParams(vmem_limit_bytes=20 * MIB),
        name="project_back",
    )(scalars, joined, tok, grad_mid, vec, mid_sums, up_sums, *pieces)


def quick_shards(*arguments):
    return quick_step(*arguments)


def quick_step(
    tokens, timesteps, starts, cotangent, ln1_gain, ln1_bias, w_qkv, bias_query,
    bias_value, w_out, bias_out, ln2_gain, ln2_bias, w_up, bias_up, w_down,
    bias_down, time_table,
):
    x, z, y, core = spot()
    chip = x * 8 + z * 2 + y
    sequence = ((lax.axis_index("dp") >> 1) << 1) | x

    def half_of(rows):
        half = rows.shape[1] // 2
        return lax.dynamic_slice_in_dim(rows, core * half, half, 1)

    fours = gather_z(half_of(join(core, w_qkv, trade(w_qkv, CORE), 0)))
    qkv_pieces = both_cores([fours] + [trade(fours, m) for m in (Y, X, X | Y)])
    tokens_here = swap_in(tokens[0])
    up_shard, out_shard = trade(w_up, CORE), trade(w_out, CORE)
    rest = jnp.concatenate(
        [half_of(join(core, w_up, up_shard, 0)), half_of(join(core, w_out, out_shard, 0))],
        axis=1,
    )
    rest = gather_z(rest)
    up_a = grow(rest[:, :, :UP_A], Y)
    up_b = grow(rest[:, :, UP_A:], X)
    up_pieces = both_cores([up_a, trade(up_a, X), up_b, trade(up_b, Y)])
    cot = swap_in(cotangent[0])
    rest = gather_z_two(w_down)
    down_a = grow(rest[:, :, :384], Y)
    down_b = grow(rest[:, :, 384:], X)
    down_pieces = both_cores([down_a, trade(down_a, X), down_b, trade(down_b, Y)])

    row = jnp.concatenate([timesteps, starts[0], jnp.zeros((5,), jnp.int32)])
    notes = exchange(jnp.broadcast_to(row, (DEVICES, 8)))
    times = jnp.broadcast_to(notes[:16, 0].reshape(8, 2).T[:, :, None], (2, 8, 2)).reshape(DEVICES)
    levels = jnp.arange(TSTEPS, dtype=jnp.int32)
    rows_of = dense((times[:, None] == levels[None, :]).astype(LOW), time_table).astype(LOW)
    vectors = (ln1_gain, ln1_bias, bias_query, bias_value, bias_out, ln2_gain, ln2_bias, bias_down)
    shared = jnp.concatenate(vectors + (bias_up,)).reshape(1, 12, 24)
    owned = jnp.concatenate(
        [jnp.broadcast_to(shared, (DEVICES, 12, 24)), rows_of[:, None], jnp.zeros((DEVICES, 3, 24), LOW)],
        axis=1,
    )
    owned = exchange(owned)
    up_bias = owned[:, 8:12].reshape(1, FF).astype(F32)
    own_starts = lax.dynamic_slice_in_dim(notes, sequence, 1, 0)[0, 1:3]
    scalars = jnp.concatenate([jnp.stack([chip, core, sequence]).astype(jnp.int32), own_starts])

    vec, normed_one, query, kv = project(scalars, tokens_here, owned, qkv_pieces)
    kv_other = trade(kv, CORE)
    parts = [attend(scalars, query, kv, kv_other, part) for part in range(PAIRS // PART)]
    heads_out = jnp.concatenate([part[0] for part in parts], axis=1)
    lse = jnp.concatenate([part[1] for part in parts], axis=0)
    mid, normed_two, act, slope = mlp_up(
        scalars, heads_out, tokens_here, vec, up_bias, up_pieces
    )

    away, keep = down_grad(scalars, act, cot)
    got = trade(away, CORE).reshape(16, 96, D)
    keep = keep.reshape(16, 96, D)
    fours = jnp.concatenate(
        [scatter_two(keep[:, :48], got[:, :48], True),
         scatter_two(keep[:, 48:], got[:, 48:], False)],
        axis=1,
    )
    grad_down = scatter_z_two(fours)

    out, grad_up_low, up_sums, grad_mid, grad_attn, grad_heads, mid_sums = mlp_mid(
        scalars, act, slope, mid, cot, vec, down_pieces, up_pieces
    )
    block_out = swap_out(out)
    away, keep = weight_grad(
        scalars, 5, ((normed_two, grad_up_low, 0, 4), (heads_out, grad_attn, 4, 1))
    )
    got = trade(away, CORE)
    fours = jnp.concatenate(
        [scatter_two(keep[:, :UP_A], got[:, :UP_A], True),
         scatter_two(keep[:, UP_A:], got[:, UP_A:], False)],
        axis=2,
    )
    keep, got = settle(scatter_z_two(fours), core)
    grad_up = join(core, keep[:, :1536], got[:, :1536], 1)
    grad_out_w = join(core, keep[:, 1536:], got[:, 1536:], 1)

    dq, own, other = attend_back(scalars, query, grad_heads, lse, kv, kv_other)
    both = add_low(own, trade(other, CORE))
    joined = jnp.concatenate([dq, both[0], both[1]], axis=1)
    away, keep = weight_grad(scalars, 3, ((normed_one, joined, 0, 3),))
    fours = scatter_direct(keep, trade(away, CORE))
    grad_qkv = join(core, *settle(scatter_z(fours), core), 1)
    grad_start, payload = project_back(
        scalars, joined, tokens_here, grad_mid, vec, mid_sums, up_sums,
        qkv_pieces,
    )
    grad_tokens = swap_out(grad_start)
    final = exchange(payload)
    summed = jnp.sum(final[:, :12], axis=0)
    hit = (times[None, :] == levels[:, None]).astype(F32)
    grad_table = jnp.dot(hit, final[:, 12], precision=lax.Precision.HIGHEST)
    return (
        block_out[None],
        grad_tokens[None],
        summed[0],
        summed[1],
        grad_qkv,
        summed[2],
        summed[3],
        grad_out_w,
        summed[4],
        summed[5],
        summed[6],
        grad_up,
        summed[8:].reshape(96),
        grad_down,
        summed[7],
        grad_table,
    )


def solution(mesh):
    quick = mesh.shape["seq"] == 2 and mesh.shape["dp"] == 16
    return jax.shard_map(
        quick_shards if quick else shards,
        mesh=mesh,
        in_specs=(
            P("dp", "seq", None),
            P("dp"),
            P("dp", None),
            P("dp", "seq", None),
            P(("seq", "dp")),
            P(("seq", "dp")),
            P(("seq", "dp"), None),
            P(("seq", "dp")),
            P(("seq", "dp")),
            P(("seq", "dp"), None),
            P(("seq", "dp")),
            P(("seq", "dp")),
            P(("seq", "dp")),
            P(("seq", "dp"), None),
            P(("seq", "dp")),
            P(("seq", "dp"), None),
            P(("seq", "dp")),
            P(None, ("seq", "dp")),
        ),
        out_specs=(
            P("dp", "seq", None),
            P("dp", "seq", None),
            P(("seq", "dp")),
            P(("seq", "dp")),
            P(("seq", "dp"), None),
            P(("seq", "dp")),
            P(("seq", "dp")),
            P(("seq", "dp"), None),
            P(("seq", "dp")),
            P(("seq", "dp")),
            P(("seq", "dp")),
            P(("seq", "dp"), None),
            P(("seq", "dp")),
            P(("seq", "dp"), None),
            P(("seq", "dp")),
            P(None, ("seq", "dp")),
        ),
        check_vma=False,
    )
```

```python
import jax
import jax.numpy as jnp
from jax import lax
from jax.experimental import pallas as pl
from jax.experimental.pallas import tpu as pltpu
from jax.sharding import PartitionSpec as P


D = 768
HEADS = 12
HD = 64
TSTEPS = 1000
PIC = 256
NPIC = 2


epsilon = 1e-05


def layer_norm(values, gain, shift):
    average = jnp.mean(values, axis=-1, keepdims=True)
    centred = values - average
    spread = jnp.mean(centred * centred, axis=-1, keepdims=True)
    return centred * lax.rsqrt(spread + epsilon) * gain + shift


def piece_label(starts, places):
    inside = (places[None, None, :] >= starts[:, :, None]) & (
        places[None, None, :] < starts[:, :, None] + PIC
    )
    number = jnp.arange(1, NPIC + 1, dtype=jnp.int32)
    return jnp.sum(inside.astype(jnp.int32) * number[None, :, None], axis=1)


def visible_mask(starts, query_pos, key_pos):
    label_query = piece_label(starts, query_pos)
    label_key = piece_label(starts, key_pos)
    causal = query_pos[:, None] >= key_pos[None, :]
    return causal[None] | (label_query[:, :, None] == label_key[:, None, :]) & (
        label_query[:, :, None] > 0
    )


def dense(left, right):
    return jnp.dot(left, right, preferred_element_type=jnp.float32)


def dense_left(left, right):
    return lax.dot_general(
        left, right, (((0,), (0,)), ((), ())), preferred_element_type=jnp.float32
    )


def dense_right(left, right):
    return lax.dot_general(
        left, right, (((1,), (1,)), ((), ())), preferred_element_type=jnp.float32
    )


def head_slice(array, index):
    return lax.dynamic_slice_in_dim(array, index * HD, HD, 2)


def merge_heads(stacked):
    head_count, seq_count, row_count, head_size = stacked.shape
    return jnp.transpose(stacked, (1, 2, 0, 3)).reshape(
        seq_count, row_count, head_count * head_size
    )


def shards(
    tokens,
    timesteps,
    starts,
    cotangent,
    ln1_gain,
    ln1_bias,
    w_qkv,
    bias_query,
    bias_value,
    w_out,
    bias_out,
    ln2_gain,
    ln2_bias,
    w_up,
    bias_up,
    w_down,
    bias_down,
    time_table,
):
    gathered = (
        lax.all_gather(ln1_gain, AXES, axis=0, tiled=True),
        lax.all_gather(ln1_bias, AXES, axis=0, tiled=True),
        lax.all_gather(w_qkv, AXES, axis=0, tiled=True),
        lax.all_gather(bias_query, AXES, axis=0, tiled=True),
        lax.all_gather(bias_value, AXES, axis=0, tiled=True),
        lax.all_gather(w_out, AXES, axis=0, tiled=True),
        lax.all_gather(bias_out, AXES, axis=0, tiled=True),
        lax.all_gather(ln2_gain, AXES, axis=0, tiled=True),
        lax.all_gather(ln2_bias, AXES, axis=0, tiled=True),
        lax.all_gather(w_up, AXES, axis=0, tiled=True),
        lax.all_gather(bias_up, AXES, axis=0, tiled=True),
        lax.all_gather(w_down, AXES, axis=0, tiled=True),
        lax.all_gather(bias_down, AXES, axis=0, tiled=True),
        lax.all_gather(time_table, AXES, axis=1, tiled=True),
    )
    (
        gain_one,
        shift_one,
        qkv_full,
        query_shift,
        value_shift,
        out_full,
        out_shift,
        gain_two,
        shift_two,
        up_full,
        up_shift,
        down_full,
        down_shift,
        table_full,
    ) = gathered
    seq_count, row_count, model_width = tokens.shape
    flat_rows = seq_count * row_count
    scale = HD ** (-0.5)
    levels = jnp.arange(TSTEPS, dtype=jnp.int32)
    onehot = timesteps[:, None] == levels[None, :]
    embed = dense(onehot.astype(jnp.bfloat16), table_full)
    start_sum = (tokens.astype(jnp.float32) + embed[:, None, :]).reshape(flat_rows, model_width)
    norm_one, pull_one = jax.vjp(
        layer_norm, start_sum, gain_one.astype(jnp.float32), shift_one.astype(jnp.float32)
    )
    normed_one = norm_one.astype(jnp.bfloat16)
    joined = dense(normed_one, qkv_full)
    query = (
        (joined[:, :D] + query_shift.astype(jnp.float32))
        .astype(jnp.bfloat16)
        .reshape(seq_count, row_count, D)
    )
    keys = joined[:, D : 2 * D].astype(jnp.bfloat16).reshape(seq_count, row_count, D)
    values = (
        (joined[:, 2 * D :] + value_shift.astype(jnp.float32))
        .astype(jnp.bfloat16)
        .reshape(seq_count, row_count, D)
    )
    key_all, value_all = (
        lax.all_gather(keys, "seq", axis=1, tiled=True),
        lax.all_gather(values, "seq", axis=1, tiled=True),
    )
    full_len = key_all.shape[1]
    query_pos = lax.axis_index("seq") * row_count + jnp.arange(row_count, dtype=jnp.int32)
    every_pos = jnp.arange(full_len, dtype=jnp.int32)
    allowed = visible_mask(starts, query_pos, every_pos)

    def head_forward(index):
        query_head = head_slice(query, index)
        key_head = head_slice(key_all, index)
        value_head = head_slice(value_all, index)
        scores = scale * jnp.einsum(
            "sre,ske->srk", query_head, key_head, preferred_element_type=jnp.float32
        )
        scores = jnp.where(allowed, scores, -1e30)
        top = jnp.max(scores, axis=-1, keepdims=True)
        expo = jnp.exp(scores - top)
        total = jnp.sum(expo, axis=-1, keepdims=True)
        probs = expo / total
        result = jnp.einsum(
            "srk,ske->sre",
            probs.astype(jnp.bfloat16),
            value_head,
            preferred_element_type=jnp.float32,
        )
        return (result, top[..., 0] + jnp.log(total[..., 0]))

    head_out, log_total = lax.map(head_forward, jnp.arange(HEADS, dtype=jnp.int32))
    heads_out = merge_heads(head_out).astype(jnp.bfloat16).reshape(flat_rows, D)
    mid = start_sum + dense(heads_out, out_full) + out_shift.astype(jnp.float32)
    norm_two, pull_two = jax.vjp(
        layer_norm, mid, gain_two.astype(jnp.float32), shift_two.astype(jnp.float32)
    )
    normed_two = norm_two.astype(jnp.bfloat16)
    up_pre = dense(normed_two, up_full) + up_shift.astype(jnp.float32)
    act_value, pull_act = jax.vjp(jax.nn.gelu, up_pre)
    act = act_value.astype(jnp.bfloat16)
    block_out = (mid + dense(act, down_full) + down_shift.astype(jnp.float32)).astype(jnp.bfloat16)
    qkv_back, out_back, up_back, down_back = (
        lax.all_gather(w_qkv, AXES, axis=0, tiled=True),
        lax.all_gather(w_out, AXES, axis=0, tiled=True),
        lax.all_gather(w_up, AXES, axis=0, tiled=True),
        lax.all_gather(w_down, AXES, axis=0, tiled=True),
    )
    grad_mlp = cotangent.reshape(flat_rows, D)
    grad_down = dense_left(act, grad_mlp)
    grad_down_shift = jnp.sum(grad_mlp.astype(jnp.float32), axis=0)
    grad_act = dense_right(grad_mlp, down_back)
    (grad_up_pre,) = pull_act(grad_act)
    grad_up_low = grad_up_pre.astype(jnp.bfloat16)
    grad_up = dense_left(normed_two, grad_up_low)
    grad_up_shift = jnp.sum(grad_up_low.astype(jnp.float32), axis=0)
    grad_norm_two = dense_right(grad_up_low, up_back)
    grad_mid_norm, grad_gain_two, grad_shift_two = pull_two(grad_norm_two)
    grad_mid = cotangent.reshape(flat_rows, D).astype(jnp.float32) + grad_mid_norm
    grad_attn = grad_mid.astype(jnp.bfloat16)
    grad_out_w = dense_left(heads_out, grad_attn)
    grad_out_shift = jnp.sum(grad_attn.astype(jnp.float32), axis=0)
    grad_heads = (
        dense_right(grad_attn, out_back).astype(jnp.bfloat16).reshape(seq_count, row_count, D)
    )
    key_back, value_back = (
        lax.all_gather(keys, "seq", axis=1, tiled=True),
        lax.all_gather(values, "seq", axis=1, tiled=True),
    )

    def query_side(index, log_head):
        query_head = head_slice(query, index)
        key_head = head_slice(key_back, index)
        value_head = head_slice(value_back, index)
        grad_head = head_slice(grad_heads, index)
        scores = scale * jnp.einsum(
            "sre,ske->srk", query_head, key_head, preferred_element_type=jnp.float32
        )
        scores = jnp.where(allowed, scores, -1e30)
        probs = jnp.exp(scores - log_head[..., None])
        grad_probs = jnp.einsum(
            "sre,ske->srk", grad_head, value_head, preferred_element_type=jnp.float32
        )
        delta = jnp.sum(probs * grad_probs, axis=-1, keepdims=True)
        grad_scores = (probs * (grad_probs - delta)).astype(jnp.bfloat16)
        grad_query_head = scale * jnp.einsum(
            "srk,ske->sre", grad_scores, key_head, preferred_element_type=jnp.float32
        )
        return (probs, grad_scores, delta[..., 0], grad_query_head)

    def query_only(inputs):
        index, log_head = inputs
        _, _, delta, grad_query_head = query_side(index, log_head)
        return (grad_query_head, delta)

    grad_query_heads, delta_heads = lax.map(
        query_only, (jnp.arange(HEADS, dtype=jnp.int32), log_total)
    )
    query_every, grad_every, log_every, delta_every = (
        lax.all_gather(query, "seq", axis=1, tiled=True),
        lax.all_gather(grad_heads, "seq", axis=1, tiled=True),
        lax.all_gather(log_total.astype(jnp.bfloat16), "seq", axis=2, tiled=True).astype(
            log_total.dtype
        ),
        lax.all_gather(delta_heads.astype(jnp.bfloat16), "seq", axis=2, tiled=True).astype(
            delta_heads.dtype
        ),
    )
    key_allowed = visible_mask(starts, every_pos, query_pos)

    def key_side(inputs):
        index, log_head, delta_head = inputs
        query_head = head_slice(query_every, index)
        grad_head = head_slice(grad_every, index)
        key_head = head_slice(keys, index)
        value_head = head_slice(values, index)
        scores = scale * jnp.einsum(
            "sqe,ske->sqk", query_head, key_head, preferred_element_type=jnp.float32
        )
        scores = jnp.where(key_allowed, scores, -1e30)
        probs = jnp.exp(scores - log_head[..., None])
        grad_probs = jnp.einsum(
            "sqe,ske->sqk", grad_head, value_head, preferred_element_type=jnp.float32
        )
        grad_scores = (probs * (grad_probs - delta_head[..., None])).astype(jnp.bfloat16)
        grad_key_head = scale * jnp.einsum(
            "sqk,sqe->ske", grad_scores, query_head, preferred_element_type=jnp.float32
        )
        grad_value_head = jnp.einsum(
            "sqk,sqe->ske",
            probs.astype(jnp.bfloat16),
            grad_head,
            preferred_element_type=jnp.float32,
        )
        return (grad_key_head, grad_value_head)

    grad_key_heads, grad_value_heads = lax.map(
        key_side, (jnp.arange(HEADS, dtype=jnp.int32), log_every, delta_every)
    )
    grad_key_own = merge_heads(grad_key_heads)
    grad_value_own = merge_heads(grad_value_heads)
    grad_query_low = merge_heads(grad_query_heads).astype(jnp.bfloat16).reshape(flat_rows, D)
    grad_key_low = grad_key_own.astype(jnp.bfloat16).reshape(flat_rows, D)
    grad_value_low = grad_value_own.astype(jnp.bfloat16).reshape(flat_rows, D)
    grad_joined = jnp.concatenate([grad_query_low, grad_key_low, grad_value_low], axis=1)
    grad_qkv = dense_left(normed_one, grad_joined)
    grad_query_shift = jnp.sum(grad_query_low.astype(jnp.float32), axis=0)
    grad_value_shift = jnp.sum(grad_value_low.astype(jnp.float32), axis=0)
    grad_norm_one = dense_right(grad_joined, qkv_back)
    grad_start_norm, grad_gain_one, grad_shift_one = pull_one(grad_norm_one)
    grad_start = grad_mid + grad_start_norm
    grad_tokens = grad_start.astype(jnp.bfloat16).reshape(seq_count, row_count, D)
    seq_sums = jnp.sum(grad_start.reshape(seq_count, row_count, D), axis=1)
    every_sums, every_times = (
        lax.all_gather(seq_sums, AXES, axis=0, tiled=True),
        lax.all_gather(timesteps, AXES, axis=0, tiled=True),
    )
    own_width = D // lax.axis_size(AXES)
    own_sums = lax.dynamic_slice_in_dim(
        every_sums, lax.axis_index(AXES) * own_width, own_width, 1
    )
    every_onehot = (every_times[None, :] == levels[:, None]).astype(jnp.float32)
    grad_table = jnp.dot(every_onehot, own_sums, precision=lax.Precision.HIGHEST)
    summed = (
        lax.psum_scatter(grad_gain_one, AXES, scatter_dimension=0, tiled=True),
        lax.psum_scatter(grad_shift_one, AXES, scatter_dimension=0, tiled=True),
        lax.psum_scatter(grad_qkv, AXES, scatter_dimension=0, tiled=True),
        lax.psum_scatter(grad_query_shift, AXES, scatter_dimension=0, tiled=True),
        lax.psum_scatter(grad_value_shift, AXES, scatter_dimension=0, tiled=True),
        lax.psum_scatter(grad_out_w, AXES, scatter_dimension=0, tiled=True),
        lax.psum_scatter(grad_out_shift, AXES, scatter_dimension=0, tiled=True),
        lax.psum_scatter(grad_gain_two, AXES, scatter_dimension=0, tiled=True),
        lax.psum_scatter(grad_shift_two, AXES, scatter_dimension=0, tiled=True),
        lax.psum_scatter(grad_up, AXES, scatter_dimension=0, tiled=True),
        lax.psum_scatter(grad_up_shift, AXES, scatter_dimension=0, tiled=True),
        lax.psum_scatter(grad_down, AXES, scatter_dimension=0, tiled=True),
        lax.psum_scatter(grad_down_shift, AXES, scatter_dimension=0, tiled=True),
    )
    return (
        block_out.reshape(seq_count, row_count, D),
        grad_tokens,
        summed[0],
        summed[1],
        summed[2],
        summed[3],
        summed[4],
        summed[5],
        summed[6],
        summed[7],
        summed[8],
        summed[9],
        summed[10],
        summed[11],
        summed[12],
        grad_table,
    )


AXES = ("seq", "dp")
CORE, Y, Z0, Z1, X = 1, 2, 4, 8, 16
DEVICES = 32
QUARTER = 256
ROWS = 512
FF = 3072
TILE = 768
WIDE = 384
MIB = 2**20
F32 = jnp.float32
LOW = jnp.bfloat16

Z_MASKS = (0, Z0, Z1, Z0 | Z1)
FAR_FIRST = (0, Z1, Z0, Z0 | Z1)


def chip_masks(middle, last, z_masks):
    return tuple((xy | z) >> 1 for xy in (0, middle, last, X | Y) for z in z_masks)


X_LAST, Y_LAST = chip_masks(Y, X, Z_MASKS), chip_masks(X, Y, Z_MASKS)
DOWN_X_LAST, DOWN_Y_LAST = chip_masks(Y, X, FAR_FIRST), chip_masks(X, Y, FAR_FIRST)


def send(array, pairs):
    return lax.ppermute(array, AXES, pairs)


def trade(array, mask):
    return send(array, [(i, i ^ mask) for i in range(DEVICES)])


def exchange(array):
    return lax.all_to_all(array, AXES, 0, 0, tiled=True)


def join(bit, own, other, axis):
    return jnp.where(
        bit == 0,
        jnp.concatenate([own, other], axis=axis),
        jnp.concatenate([other, own], axis=axis),
    )


def spot():
    x = lax.axis_index("seq")
    dp = lax.axis_index("dp")
    return x, dp >> 2, (dp >> 1) & 1, dp & 1


def hop_pairs(first):
    pairs = []
    for base in range(0, 16, 2):
        if first:
            moves = (((0, 0), (0, 1)), ((0, 1), (1, 0)), ((1, 0), (0, 0)))
        else:
            moves = (((1, 0), (0, 1)), ((1, 1), (1, 0)), ((0, 1), (1, 1)))
        for (sx, sc), (tx, tc) in moves:
            pairs.append((sx * 16 + base + sc, tx * 16 + base + tc))
    return pairs


def corners():
    x, _, _, core = spot()
    return (x == 0) & (core == 0), (x == 1) & (core == 1)


def swap_in(array):
    first, last = corners()
    front, back = array[:QUARTER], array[QUARTER:]
    one = send(jnp.where(first, back, front), hop_pairs(True))
    two = send(jnp.where(last, front, back), hop_pairs(False))
    low = jnp.where(first, front, jnp.where(last, two, one))
    high = jnp.where(first, one, jnp.where(last, back, two))
    return jnp.concatenate([low, high], axis=0)


def swap_out(array):
    first, last = corners()
    low, high = array[:QUARTER], array[QUARTER:]
    back_pairs = lambda which: [(t, s) for s, t in hop_pairs(which)]
    one = send(jnp.where(first, high, low), back_pairs(True))
    two = send(jnp.where(last, low, high), back_pairs(False))
    front = jnp.where(first, low, jnp.where(last, two, one))
    back = jnp.where(first, one, jnp.where(last, high, two))
    return jnp.concatenate([front, back], axis=0)


def gather_z(block):
    got = [trade(block, mask) for mask in Z_MASKS[1:]]
    return jnp.stack([block] + got, axis=0)


def grow(blocks, mask):
    return jnp.concatenate([blocks, trade(blocks, mask)], axis=0)


def both_cores(pieces):
    return tuple(pieces) + tuple(trade(p, CORE) for p in pieces)


def add_low(left, right):
    return (left.astype(F32) + right.astype(F32)).astype(LOW)


def scatter_two(keep, got, x_first):
    n = keep.shape[-1]
    keep, got = (array.reshape(2, 4, 2, -1, n) for array in (keep, got))
    if x_first:
        away = trade(add_low(keep[1], got[1]), X)
        part = lambda y: add_low(add_low(keep[0, :, y], got[0, :, y]), away[:, y])
    else:
        away = trade(add_low(keep[:, :, 1], got[:, :, 1]), Y)
        part = lambda x: add_low(add_low(keep[x, :, 0], got[x, :, 0]), away[x])
    last = trade(part(1), Y if x_first else X)
    return add_low(part(0), last)


def scatter_direct(keep, got):
    n = keep.shape[-1]
    cube = lambda array: array.reshape(2, 4, 2, -1, n)
    keep, got = cube(keep), cube(got)
    total = keep[0, :, 0].astype(F32) + got[0, :, 0].astype(F32)
    for mask, a, b in ((Y, 0, 1), (X, 1, 0), (X | Y, 1, 1)):
        away = trade(add_low(keep[a, :, b], got[a, :, b]), mask)
        total = total + away.astype(F32)
    return total.astype(LOW)


def scatter_z(fours):
    total = fours[0].astype(F32)
    for place, mask in enumerate(Z_MASKS[1:], 1):
        total = total + trade(fours[place], mask).astype(F32)
    return total


def scatter_z_two(fours):
    fours = fours.reshape((2, 2) + fours.shape[1:])
    away = trade(fours[:, 1], Z0)
    got = trade(add_low(fours[1, 0], away[1]), Z1)
    return add_low(fours[0, 0], away[0]).astype(F32) + got.astype(F32)


def settle(block, core):
    keep = lax.dynamic_slice_in_dim(block, core * 24, 24, 0)
    away = lax.dynamic_slice_in_dim(block, (1 - core) * 24, 24, 0)
    return keep, trade(away, CORE)


def dot_nt(left, right):
    return lax.dot_general(
        left, right, (((1,), (1,)), ((), ())), preferred_element_type=F32
    )


def dot_nn(left, right):
    return lax.dot_general(
        left, right, (((1,), (0,)), ((), ())), preferred_element_type=F32
    )


def inside_piece(place, start):
    return (place >= start) & (place < start + PIC)


def fill_bias(scalars, low_bias, high_bias):
    core, first, second = scalars[1], scalars[3], scalars[4]

    def fill(ref, chunk, key_start, query_start):
        shape = (QUARTER, QUARTER)
        key = key_start + lax.broadcasted_iota(jnp.int32, shape, 0)
        query = query_start + lax.broadcasted_iota(jnp.int32, shape, 1)
        seen = (
            (key <= query)
            | (inside_piece(key, first) & inside_piece(query, first))
            | (inside_piece(key, second) & inside_piece(query, second))
        )
        ref[pl.ds(chunk * QUARTER, QUARTER), :] = jnp.where(seen, 0.0, -1e30)

    mine, theirs = core * QUARTER, (1 - core) * QUARTER
    fill(low_bias, 0, mine, mine)
    fill(low_bias, 1, theirs, mine)
    half = 2 * QUARTER
    fill(high_bias, 0, mine, half + mine)
    fill(high_bias, 1, half + mine, half + mine)
    fill(high_bias, 2, theirs, half + mine)
    fill(high_bias, 3, half + theirs, half + mine)


def head_lanes(array, head):
    lane = lax.broadcasted_iota(jnp.int32, array.shape, 1)
    return jnp.where((lane >= HD) == (head == 1), array, jnp.zeros_like(array))


def key_sets(own, other):
    high = jnp.concatenate([own[...], other[...]], axis=0)
    low = jnp.concatenate([own[:QUARTER], other[:QUARTER]], axis=0)
    return low, high


def forward_kernel(scalars, q, k_own, k_other, v_own, v_other, out, lse, low_bias, high_bias):
    @pl.when(pl.program_id(0) == 0)
    def _():
        fill_bias(scalars, low_bias, high_bias)

    scale = HD ** (-0.5)
    keys, values = key_sets(k_own, k_other), key_sets(v_own, v_other)
    for part, bias in enumerate((low_bias, high_bias)):
        key, value_t = keys[part], values[part].T
        rows = pl.ds(part * QUARTER, QUARTER)
        query = q[rows, :] * jnp.bfloat16(scale)
        tops = []
        for head in range(2):
            scores = dot_nt(key, head_lanes(query, head)) + bias[...]
            top = jnp.max(scores, axis=0, keepdims=True)
            expo = jnp.exp(scores - top)
            total = jnp.sum(expo, axis=0, keepdims=True)
            mixed = dot_nn(value_t[head * HD : (head + 1) * HD], expo.astype(LOW))
            tops.append(mixed / total)
            lse[0, pl.ds(head, 1), rows] = top + jnp.log(total)
        both = jnp.concatenate(tops, axis=0)
        out[rows, :] = both.T.astype(LOW)


def backward_kernel(
    scalars, q, grad, lse, k_own, k_other, v_own, v_other,
    dq, own, other, low_bias, high_bias,
):
    @pl.when(pl.program_id(0) == 0)
    def _():
        fill_bias(scalars, low_bias, high_bias)

    scale = HD ** (-0.5)
    keys, values = key_sets(k_own, k_other), key_sets(v_own, v_other)
    sums = []
    for part, bias in enumerate((low_bias, high_bias)):
        key, value = keys[part], values[part]
        key_t = key.T
        rows = pl.ds(part * QUARTER, QUARTER)
        query = q[rows, :] * jnp.bfloat16(scale)
        grad_out = grad[rows, :]
        grad_query, grad_key, grad_value = [], 0.0, 0.0
        for head in range(2):
            query_head = head_lanes(query, head)
            grad_head = head_lanes(grad_out, head)
            scores = dot_nt(key, query_head) + bias[...]
            probs = jnp.exp(scores - lse[0, pl.ds(head, 1), rows])
            grad_probs = dot_nt(value, grad_head)
            delta = jnp.sum(probs * grad_probs, axis=0, keepdims=True)
            grad_scores = (probs * (grad_probs - delta)).astype(LOW)
            grad_value += dot_nn(probs.astype(LOW), grad_head)
            grad_key += dot_nn(grad_scores, query_head)
            grad_query.append(
                dot_nn(key_t[head * HD : (head + 1) * HD], grad_scores) * scale
            )
        dq[rows, :] = jnp.concatenate(grad_query, axis=0).T.astype(LOW)
        sums.append((grad_key, grad_value))
    for which in range(2):
        low, high = sums[0][which], sums[1][which]
        own[which, :QUARTER] = (low[:QUARTER] + high[:QUARTER]).astype(LOW)
        own[which, QUARTER:] = high[QUARTER : 2 * QUARTER].astype(LOW)
        other[which, :QUARTER] = (low[QUARTER:] + high[2 * QUARTER : 3 * QUARTER]).astype(LOW)
        other[which, QUARTER:] = high[3 * QUARTER :].astype(LOW)


PAIRS = HEADS // 2


PART = 3


def pair_block(skip=0):
    return pl.BlockSpec((ROWS, 2 * HD), lambda i, s: (0, i + skip))


def lse_block():
    return pl.BlockSpec((1, 2, ROWS), lambda i, s: (i, 0, 0))


def bias_scratch():
    return [
        pltpu.VMEM((2 * QUARTER, QUARTER), F32),
        pltpu.VMEM((4 * QUARTER, QUARTER), F32),
    ]


def cost(flops, size):
    return pl.CostEstimate(flops=flops, bytes_accessed=size, transcendentals=0)


def array(shape, dtype=LOW):
    return jax.ShapeDtypeStruct(shape, dtype)


def attend(scalars, q, kv, kv_other, part):
    skip = part * PART
    block = pair_block(skip)
    value = pair_block(skip + PAIRS)
    return pl.pallas_call(
        forward_kernel,
        grid_spec=pltpu.PrefetchScalarGridSpec(
            num_scalar_prefetch=1,
            grid=(PART,),
            in_specs=[block, block, block, value, value],
            out_specs=[pair_block(), lse_block()],
            scratch_shapes=bias_scratch(),
        ),
        out_shape=[array((ROWS, PART * 2 * HD)), array((PART, 2, ROWS), F32)],
        cost_estimate=cost(10**9, 2 * 10**6),
        compiler_params=pltpu.CompilerParams(vmem_limit_bytes=16 * MIB),
    )(scalars, q, kv, kv_other, kv, kv_other)


def attend_back(scalars, q, grad, lse, kv, kv_other):
    both = pl.BlockSpec((2, ROWS, 2 * HD), lambda i, s: (0, 0, i))
    return pl.pallas_call(
        backward_kernel,
        grid_spec=pltpu.PrefetchScalarGridSpec(
            num_scalar_prefetch=1,
            grid=(PAIRS,),
            in_specs=[pair_block()] * 2
            + [lse_block(), pair_block(), pair_block(), pair_block(PAIRS), pair_block(PAIRS)],
            out_specs=[pair_block(), both, both],
            scratch_shapes=bias_scratch(),
        ),
        out_shape=[array((ROWS, D)), array((2, ROWS, D)), array((2, ROWS, D))],
        cost_estimate=cost(2 * 10**10, 8 * 10**6),
        compiler_params=pltpu.CompilerParams(vmem_limit_bytes=18 * MIB),
        name="attend_back",
    )(scalars, q, grad, lse, kv, kv_other, kv, kv_other)


def fetch(jobs, sems):
    copies = [pltpu.make_async_copy(s, d, sems.at[i]) for i, (s, d) in enumerate(jobs)]
    for copy in copies:
        copy.start()
    return copies


def wait(copies):
    for copy in copies:
        copy.wait()


def placed(pieces, masks):
    return [
        (ref, j, masks[start + j])
        for ref, start in zip(pieces, range(0, 16, 16 // len(pieces)))
        for j in range(16 // len(pieces))
    ]


def column_jobs(scalars, own, other, target, masks, start, width, half, skip=0):
    chip, core = scalars[0], scalars[1]
    jobs = []
    for pieces, side in ((own, core), (other, 1 - core)):
        columns = pl.ds(pl.multiple_of(side * half + skip, 128), width)
        for ref, j, mask in placed(pieces, masks):
            rows = pl.ds(pl.multiple_of((chip ^ mask) * 48, 16), 48)
            jobs.append((ref.at[j, :, pl.ds(start, width)], target.at[rows, columns]))
    return jobs


def qkv_jobs(scalars, pieces, weight):
    return column_jobs(scalars, pieces[:4], pieces[4:], weight, X_LAST, 0, 1152, 1152)


UP_A = 1024


def up_jobs(scalars, pieces, w_up, w_out):
    a, b, a2, b2 = pieces[:2], pieces[2:4], pieces[4:6], pieces[6:]
    jobs = column_jobs(scalars, b, b2, w_out, Y_LAST, 1536 - UP_A, 384, 384)
    jobs += column_jobs(scalars, a, a2, w_up, X_LAST, 0, UP_A, 1536)
    return jobs + column_jobs(scalars, b, b2, w_up, Y_LAST, 0, 1536 - UP_A, 1536, UP_A)


def down_jobs(scalars, pieces, target):
    chip, core = scalars[0], scalars[1]
    jobs = []
    for k, (side, masks, half) in enumerate(
        (
            (core, DOWN_X_LAST, 0), (core, DOWN_Y_LAST, 1),
            (1 - core, DOWN_X_LAST, 0), (1 - core, DOWN_Y_LAST, 1),
        )
    ):
        for ref, j, mask in placed(pieces[2 * k : 2 * k + 2], masks):
            first = pl.multiple_of((chip ^ mask) * 192 + side * 96, 16)
            jobs.append((ref.at[j], target.at[pl.ds(first, 96), pl.ds(half * 384, 384)]))
    return jobs


CHUNK = 128


def by_rows(body):
    @pl.loop(0, ROWS // CHUNK)
    def _(step):
        body(pl.ds(pl.multiple_of(step * CHUNK, CHUNK), CHUNK))


def norm_parts(values):
    average = jnp.mean(values, axis=-1, keepdims=True)
    centred = values - average
    rate = lax.rsqrt(jnp.mean(centred * centred, axis=-1, keepdims=True) + epsilon)
    return centred * rate, rate


def norm_back(grad, normal, rate, gain):
    scaled = grad * gain
    return rate * (
        scaled
        - jnp.mean(scaled, axis=-1, keepdims=True)
        - normal * jnp.mean(scaled * normal, axis=-1, keepdims=True)
    )


def full(shape):
    return pl.BlockSpec(
        shape, lambda i, s: (0,) * len(shape), pipeline_mode=pl.Buffered(1)
    )


def anywhere():
    return pl.BlockSpec(memory_space=pl.ANY)


def spread(shape):
    column = lax.broadcasted_iota(jnp.int32, shape, len(shape) - 1)
    return column, column - column // 24 * 24


def project_kernel(scalars, tok, owned, *refs):
    pieces, (vec, normed, q, kv, weight, sems) = refs[:8], refs[8:]
    step = pl.program_id(0)

    @pl.when(step == 0)
    def _():
        copies = fetch(qkv_jobs(scalars, pieces, weight), sems)
        _, inner = spread((24, D))
        place = (inner == lax.broadcasted_iota(jnp.int32, (24, D), 0)).astype(LOW)
        wide = dot_nn(owned[...].reshape(DEVICES * 16, 24), place).reshape(DEVICES, 16, D)
        column, _ = spread((DEVICES, 16, D))
        mine = column // 24 == lax.broadcasted_iota(jnp.int32, (DEVICES, 16, D), 0)
        vec[...] = jnp.sum(jnp.where(mine, wide, 0.0), axis=0)

        def rows_of(rows):
            normal, _ = norm_parts(tok[rows, :].astype(F32) + vec[12:13, :])
            normed[rows, :] = (normal * vec[0:1, :] + vec[1:2, :]).astype(LOW)

        by_rows(rows_of)
        wait(copies)

    columns = pl.ds(pl.multiple_of(step * D, D), D)
    result = dot_nn(normed[...], weight[:, columns])

    @pl.when(step < 1)
    def _():
        q[...] = (result + vec[2:3, :]).astype(LOW)

    @pl.when(step == 1)
    def _():
        kv[...] = result.astype(LOW)

    @pl.when(step == 2)
    def _():
        kv[...] = (result + vec[3:4, :]).astype(LOW)


def project(scalars, tok, owned, pieces):
    return pl.pallas_call(
        project_kernel,
        grid_spec=pltpu.PrefetchScalarGridSpec(
            num_scalar_prefetch=1,
            grid=(3,),
            in_specs=[full((ROWS, D)), full((DEVICES, 16, 24))] + [anywhere()] * 8,
            out_specs=[
                full((16, D)),
                full((ROWS, D)),
                full((ROWS, D)),
                pl.BlockSpec((ROWS, D), lambda i, s: (0, jnp.maximum(i - 1, 0))),
            ],
            scratch_shapes=[pltpu.VMEM((D, 3 * D), LOW), pltpu.SemaphoreType.DMA((32,))],
        ),
        out_shape=[array((16, D), F32), array((ROWS, D)), array((ROWS, D)), array((ROWS, 2 * D))],
        cost_estimate=cost(2 * 10**9, 8 * 10**6),
        compiler_params=pltpu.CompilerParams(vmem_limit_bytes=18 * MIB),
        name="project",
    )(scalars, tok, owned, *pieces)


GELU = 0.7978845608028654


def mlp_up_kernel(scalars, heads, tok, vec, up_bias, *refs):
    pieces, (mid, normed, act, slope, w_up, w_out, sems) = refs[:8], refs[8:]
    step = pl.program_id(0)

    @pl.when(step == 0)
    def _():
        copies = fetch(up_jobs(scalars, pieces, w_up, w_out), sems)
        wait(copies[:32])
        mid[...] = dot_nn(heads[...], w_out[...])

        def rows_of(rows):
            total = tok[rows, :].astype(F32) + vec[12:13, :] + mid[rows, :] + vec[4:5, :]
            mid[rows, :] = total
            normal, _ = norm_parts(total)
            normed[rows, :] = (normal * vec[5:6, :] + vec[6:7, :]).astype(LOW)

        by_rows(rows_of)
        wait(copies[32:])

    columns = pl.ds(pl.multiple_of(step * TILE, TILE), TILE)
    v = dot_nn(normed[...], w_up[:, columns]) + up_bias[...]
    square = v * v
    inner = jnp.tanh(GELU * v * (1 + 0.044715 * square))
    half = 0.5 * (1 + inner)
    act[...] = (v * half).astype(LOW)
    slope[...] = (
        half + 0.5 * GELU * v * (1 - inner * inner) * (1 + 3 * 0.044715 * square)
    ).astype(LOW)


def mlp_up(scalars, heads, tok, vec, up_bias, pieces):
    tile = pl.BlockSpec((ROWS, TILE), lambda i, s: (0, i))
    return pl.pallas_call(
        mlp_up_kernel,
        grid_spec=pltpu.PrefetchScalarGridSpec(
            num_scalar_prefetch=1,
            grid=(FF // TILE,),
            in_specs=[
                full((ROWS, D)), full((ROWS, D)), full((16, D)),
                pl.BlockSpec((1, TILE), lambda i, s: (0, i)),
            ] + [anywhere()] * 8,
            out_specs=[full((ROWS, D)), full((ROWS, D)), tile, tile],
            scratch_shapes=[
                pltpu.VMEM((D, FF), LOW), pltpu.VMEM((D, D), LOW), pltpu.SemaphoreType.DMA((96,)),
            ],
        ),
        out_shape=[array((ROWS, D), F32), array((ROWS, D)), array((ROWS, FF)), array((ROWS, FF))],
        cost_estimate=cost(4 * 10**9, 16 * 10**6),
        compiler_params=pltpu.CompilerParams(vmem_limit_bytes=20 * MIB),
        name="mlp_up",
    )(scalars, heads, tok, vec, up_bias, *pieces)


def down_grad_kernel(scalars, act, cot, send, keep):
    chip, core = scalars[0], scalars[1]
    result = lax.dot_general(
        act[...], cot[...], (((0,), (0,)), ((), ())), preferred_element_type=F32
    )
    for index in range(2):
        place = (pl.program_id(0) * 2 + index) ^ chip
        rows = pl.ds(pl.multiple_of(place * 96, 16), 96)
        first = result[index * 192 : index * 192 + 96].astype(LOW)
        second = result[index * 192 + 96 : index * 192 + 192].astype(LOW)
        keep[rows, :] = jnp.where(core == 0, first, second)
        send[rows, :] = jnp.where(core == 0, second, first)


def down_grad(scalars, act, cot):
    return pl.pallas_call(
        down_grad_kernel,
        grid_spec=pltpu.PrefetchScalarGridSpec(
            num_scalar_prefetch=1,
            grid=(8,),
            in_specs=[pl.BlockSpec((ROWS, WIDE), lambda i, s: (0, i)), full((ROWS, D))],
            out_specs=[full((FF // 2, D))] * 2,
        ),
        out_shape=[array((FF // 2, D))] * 2,
        cost_estimate=cost(3 * 10**9, 9 * 10**6),
        compiler_params=pltpu.CompilerParams(vmem_limit_bytes=16 * MIB),
        name="down_grad",
    )(scalars, act, cot)


TILES = FF // TILE


def mlp_mid_kernel(scalars, act, slope, mid, cot, vec, *refs):
    down_pieces, up_pieces, refs = refs[:8], refs[8:16], refs[16:]
    out, grad_up, bias_sum, grad_mid, grad_attn, grad_heads, sums = refs[:7]
    w_down, w_up, w_out, held, total, down_sems, up_sems = refs[7:]
    step = pl.program_id(0)
    down = lambda: [
        pltpu.make_async_copy(s, d, down_sems.at[i])
        for i, (s, d) in enumerate(down_jobs(scalars, down_pieces, w_down))
    ]
    up = lambda: [
        pltpu.make_async_copy(s, d, up_sems.at[i])
        for i, (s, d) in enumerate(up_jobs(scalars, up_pieces, w_up, w_out))
    ]

    @pl.when(step == 0)
    def _():
        copies = down()
        for copy in copies + up():
            copy.start()
        total[...] = mid[...] + vec[7:8, :]
        wait(copies)

    @pl.when(step < TILES)
    def _():
        rows = pl.ds(pl.multiple_of(step * TILE, TILE), TILE)
        part = w_down[rows, :]
        total[...] += dot_nn(act[...], part)
        grad = (dot_nt(cot[...], part) * slope[...].astype(F32)).astype(LOW)
        grad_up[...] = grad
        held[step] = grad
        bias_sum[...] = jnp.sum(grad.astype(F32), axis=0, keepdims=True)

    @pl.when(step == TILES)
    def _():
        out[...] = total[...].astype(LOW)
        total[...] = jnp.zeros_like(total)
        wait(up())

    @pl.when(step >= TILES)
    def _():
        local = step - TILES
        columns = pl.ds(pl.multiple_of(local * TILE, TILE), TILE)
        total[...] += dot_nt(held[local], w_up[:, columns])

    @pl.when(step == 2 * TILES - 1)
    def _():
        sums[...] = jnp.zeros_like(sums)

        def rows_of(rows):
            normal, rate = norm_parts(mid[rows, :])
            grad = total[rows, :]
            outer = cot[rows, :].astype(F32)
            back = outer + norm_back(grad, normal, rate, vec[5:6, :])
            grad_mid[rows, :] = back
            low = back.astype(LOW)
            grad_attn[rows, :] = low
            sums[0:1, :] += jnp.sum(grad * normal, axis=0, keepdims=True)
            sums[1:2, :] += jnp.sum(grad, axis=0, keepdims=True)
            sums[2:3, :] += jnp.sum(low.astype(F32), axis=0, keepdims=True)
            sums[3:4, :] += jnp.sum(outer, axis=0, keepdims=True)

        by_rows(rows_of)
        grad_heads[...] = dot_nt(grad_attn[...], w_out[...]).astype(LOW)


def mlp_mid(scalars, act, slope, mid, cot, vec, down_pieces, up_pieces):
    index = lambda i, s: (0, jnp.minimum(i, TILES - 1))
    tile = pl.BlockSpec((ROWS, TILE), index)
    return pl.pallas_call(
        mlp_mid_kernel,
        grid_spec=pltpu.PrefetchScalarGridSpec(
            num_scalar_prefetch=1,
            grid=(2 * TILES,),
            in_specs=[tile, tile, full((ROWS, D)), full((ROWS, D)), full((16, D))]
            + [anywhere()] * 16,
            out_specs=[full((ROWS, D)), tile, pl.BlockSpec((1, TILE), index)]
            + [full((ROWS, D))] * 3
            + [full((8, D))],
            scratch_shapes=[
                pltpu.VMEM((FF, D), LOW), pltpu.VMEM((D, FF), LOW), pltpu.VMEM((D, D), LOW),
                pltpu.VMEM((TILES, ROWS, TILE), LOW), pltpu.VMEM((ROWS, D), F32),
                pltpu.SemaphoreType.DMA((64,)), pltpu.SemaphoreType.DMA((96,)),
            ],
        ),
        out_shape=[
            array((ROWS, D)), array((ROWS, FF)), array((1, FF), F32), array((ROWS, D), F32),
            array((ROWS, D)), array((ROWS, D)), array((8, D), F32),
        ],
        cost_estimate=cost(10**10, 30 * 10**6),
        compiler_params=pltpu.CompilerParams(vmem_limit_bytes=31 * MIB),
        name="mlp_mid",
    )(scalars, act, slope, mid, cot, vec, *down_pieces, *up_pieces)


def place_rows(result, target, chip):
    for index in range(16):
        rows = pl.ds(pl.multiple_of((index ^ chip) * 48, 16), 48)
        target[rows, :] = result[index * 48 : index * 48 + 48].astype(LOW)


def weight_grad_kernel(tiles, lefts, scalars, *refs):
    left_refs, right_refs = refs[: len(lefts)], refs[len(lefts) : 2 * len(lefts)]
    send, keep = refs[2 * len(lefts) : 2 * len(lefts) + 2]
    flipped = refs[2 * len(lefts) + 2 :]
    step = pl.program_id(0)
    chip = scalars[0]

    @pl.when(step == 0)
    def _():
        for left, flip in zip(left_refs, flipped):
            flip[...] = left[...].T

    local = jnp.where(step < tiles, step, step - tiles)
    for which, (first, last) in enumerate(lefts):

        @pl.when((local >= first) & (local < last))
        def _(which=which):
            result = dot_nn(flipped[which][...], right_refs[which][...])

            @pl.when(step < tiles)
            def _():
                place_rows(result, send, chip)

            @pl.when(step >= tiles)
            def _():
                place_rows(result, keep, chip)


def weight_grad(scalars, tiles, parts):
    def right_block(first, count):
        def index(i, s):
            local = jnp.clip(jnp.where(i < tiles, i, i - tiles) - first, 0, count - 1)
            side = jnp.where(i < tiles, 1 - s[1], s[1])
            return (0, side * count + local)

        return pl.BlockSpec((ROWS, WIDE), index)

    lefts = tuple((first, first + count) for _, _, first, count in parts)
    return pl.pallas_call(
        lambda *refs: weight_grad_kernel(tiles, lefts, *refs),
        grid_spec=pltpu.PrefetchScalarGridSpec(
            num_scalar_prefetch=1,
            grid=(2 * tiles,),
            in_specs=[full((ROWS, D))] * len(parts)
            + [right_block(first, count) for _, _, first, count in parts],
            out_specs=[
                pl.BlockSpec((D, WIDE), lambda i, s: (0, jnp.minimum(i, tiles - 1))),
                pl.BlockSpec((D, WIDE), lambda i, s: (0, jnp.maximum(i - tiles, 0))),
            ],
            scratch_shapes=[pltpu.VMEM((D, ROWS), LOW)] * len(parts),
        ),
        out_shape=[array((D, tiles * WIDE))] * 2,
        cost_estimate=cost(tiles * 6 * 10**8, 10 * 10**6),
        compiler_params=pltpu.CompilerParams(vmem_limit_bytes=18 * MIB),
    )(scalars, *[p[0] for p in parts], *[p[1] for p in parts])


def project_back_kernel(scalars, joined, tok, grad_mid, vec, mid_sums, up_sums, *refs):
    pieces, (out, payload, weight, total, sums, column_sums, sems) = refs[:8], refs[8:]
    step = pl.program_id(0)

    @pl.when(step == 0)
    def _():
        copies = fetch(qkv_jobs(scalars, pieces, weight), sems)
        total[...] = jnp.zeros_like(total)
        wait(copies)

    columns = pl.ds(pl.multiple_of(step * D, D), D)
    total[...] += dot_nt(joined[...], weight[:, columns])
    column_sums[:, columns] = jnp.sum(joined[...].astype(F32), axis=0, keepdims=True)

    @pl.when(step == 2)
    def _():
        sums[...] = jnp.zeros_like(sums)

        def rows_of(rows):
            normal, rate = norm_parts(tok[rows, :].astype(F32) + vec[12:13, :])
            grad = total[rows, :]
            back = grad_mid[rows, :] + norm_back(grad, normal, rate, vec[0:1, :])
            out[rows, :] = back.astype(LOW)
            sums[0:1, :] += jnp.sum(grad * normal, axis=0, keepdims=True)
            sums[1:2, :] += jnp.sum(grad, axis=0, keepdims=True)
            sums[12:13, :] += jnp.sum(back, axis=0, keepdims=True)

        by_rows(rows_of)
        sums[2:3, :] = column_sums[:, :D]
        sums[3:4, :] = column_sums[:, 2 * D :]
        sums[4:5, :] = mid_sums[2:3, :]
        sums[5:7, :] = mid_sums[0:2, :]
        sums[7:8, :] = mid_sums[3:4, :]
        _, inner = spread((24, D))
        place = (inner == lax.broadcasted_iota(jnp.int32, (24, D), 0)).astype(F32)
        column, _ = spread((DEVICES, 16, D))
        mine = column // 24 == lax.broadcasted_iota(jnp.int32, (DEVICES, 16, D), 0)
        wide = jnp.where(mine, sums[...][None], 0.0).reshape(DEVICES * 16, D)
        narrow = lax.dot_general(
            wide, place, (((1,), (1,)), ((), ())),
            precision=lax.Precision.HIGHEST, preferred_element_type=F32,
        )
        payload[...] = narrow.reshape(DEVICES, 16, 24)
        column = lax.broadcasted_iota(jnp.int32, (DEVICES * 4, FF), 1)
        mine = column // 24 == lax.broadcasted_iota(jnp.int32, (DEVICES * 4, FF), 0)
        inner = lax.broadcasted_iota(jnp.int32, (24, FF), 1)
        inner = inner - inner // 24 * 24
        place = (inner == lax.broadcasted_iota(jnp.int32, (24, FF), 0)).astype(F32)
        narrow = lax.dot_general(
            jnp.where(mine, up_sums[...], 0.0), place, (((1,), (1,)), ((), ())),
            precision=lax.Precision.HIGHEST, preferred_element_type=F32,
        )
        payload[:, 8:12, :] = narrow.reshape(DEVICES, 4, 24)


def project_back(scalars, joined, tok, grad_mid, vec, mid_sums, up_sums, pieces):
    return pl.pallas_call(
        project_back_kernel,
        grid_spec=pltpu.PrefetchScalarGridSpec(
            num_scalar_prefetch=1,
            grid=(3,),
            in_specs=[
                pl.BlockSpec((ROWS, D), lambda i, s: (0, i)),
                full((ROWS, D)), full((ROWS, D)), full((16, D)), full((8, D)),
                full((1, FF)),
            ] + [anywhere()] * 8,
            out_specs=[full((ROWS, D)), full((DEVICES, 16, 24))],
            scratch_shapes=[
                pltpu.VMEM((D, 3 * D), LOW), pltpu.VMEM((ROWS, D), F32), pltpu.VMEM((16, D), F32),
                pltpu.VMEM((1, 3 * D), F32), pltpu.SemaphoreType.DMA((32,)),
            ],
        ),
        out_shape=[array((ROWS, D)), array((DEVICES, 16, 24), F32)],
        cost_estimate=cost(3 * 10**9, 12 * 10**6),
        compiler_params=pltpu.CompilerParams(vmem_limit_bytes=20 * MIB),
        name="project_back",
    )(scalars, joined, tok, grad_mid, vec, mid_sums, up_sums, *pieces)


def quick_shards(*arguments):
    return quick_step(*arguments)


def quick_step(
    tokens, timesteps, starts, cotangent, ln1_gain, ln1_bias, w_qkv, bias_query,
    bias_value, w_out, bias_out, ln2_gain, ln2_bias, w_up, bias_up, w_down,
    bias_down, time_table,
):
    x, z, y, core = spot()
    chip = x * 8 + z * 2 + y
    sequence = ((lax.axis_index("dp") >> 1) << 1) | x

    def half_of(rows):
        half = rows.shape[1] // 2
        return lax.dynamic_slice_in_dim(rows, core * half, half, 1)

    fours = gather_z(half_of(join(core, w_qkv, trade(w_qkv, CORE), 0)))
    qkv_pieces = both_cores([fours] + [trade(fours, m) for m in (Y, X, X | Y)])
    tokens_here = swap_in(tokens[0])
    up_shard, out_shard = trade(w_up, CORE), trade(w_out, CORE)
    rest = jnp.concatenate(
        [half_of(join(core, w_up, up_shard, 0)), half_of(join(core, w_out, out_shard, 0))],
        axis=1,
    )
    rest = gather_z(rest)
    up_a = grow(rest[:, :, :UP_A], Y)
    up_b = grow(rest[:, :, UP_A:], X)
    up_pieces = both_cores([up_a, trade(up_a, X), up_b, trade(up_b, Y)])
    cot = swap_in(cotangent[0])
    rest = grow(grow(w_down[None], Z1), Z0)
    down_a = grow(rest[:, :, :384], Y)
    down_b = grow(rest[:, :, 384:], X)
    down_pieces = both_cores([down_a, trade(down_a, X), down_b, trade(down_b, Y)])

    row = jnp.concatenate([timesteps, starts[0], jnp.zeros((5,), jnp.int32)])
    notes = exchange(jnp.broadcast_to(row, (DEVICES, 8)))
    times = jnp.broadcast_to(notes[:16, 0].reshape(8, 2).T[:, :, None], (2, 8, 2)).reshape(DEVICES)
    levels = jnp.arange(TSTEPS, dtype=jnp.int32)
    rows_of = dense((times[:, None] == levels[None, :]).astype(LOW), time_table).astype(LOW)
    vectors = (ln1_gain, ln1_bias, bias_query, bias_value, bias_out, ln2_gain, ln2_bias, bias_down)
    shared = jnp.concatenate(vectors + (bias_up,)).reshape(1, 12, 24)
    owned = jnp.concatenate(
        [jnp.broadcast_to(shared, (DEVICES, 12, 24)), rows_of[:, None], jnp.zeros((DEVICES, 3, 24), LOW)],
        axis=1,
    )
    owned = exchange(owned)
    up_bias = owned[:, 8:12].reshape(1, FF).astype(F32)
    own_starts = lax.dynamic_slice_in_dim(notes, sequence, 1, 0)[0, 1:3]
    scalars = jnp.concatenate([jnp.stack([chip, core, sequence]).astype(jnp.int32), own_starts])

    vec, normed_one, query, kv = project(scalars, tokens_here, owned, qkv_pieces)
    kv_other = trade(kv, CORE)
    parts = [attend(scalars, query, kv, kv_other, part) for part in range(PAIRS // PART)]
    heads_out = jnp.concatenate([part[0] for part in parts], axis=1)
    lse = jnp.concatenate([part[1] for part in parts], axis=0)
    mid, normed_two, act, slope = mlp_up(
        scalars, heads_out, tokens_here, vec, up_bias, up_pieces
    )

    away, keep = down_grad(scalars, act, cot)
    got = trade(away, CORE).reshape(16, 96, D)
    keep = keep.reshape(16, 96, D)
    fours = jnp.concatenate(
        [scatter_two(keep[:, :48], got[:, :48], True),
         scatter_two(keep[:, 48:], got[:, 48:], False)],
        axis=1,
    )
    grad_down = scatter_z_two(fours)

    out, grad_up_low, up_sums, grad_mid, grad_attn, grad_heads, mid_sums = mlp_mid(
        scalars, act, slope, mid, cot, vec, down_pieces, up_pieces
    )
    block_out = swap_out(out)
    away, keep = weight_grad(
        scalars, 5, ((normed_two, grad_up_low, 0, 4), (heads_out, grad_attn, 4, 1))
    )
    got = trade(away, CORE)
    fours = jnp.concatenate(
        [scatter_two(keep[:, :UP_A], got[:, :UP_A], True),
         scatter_two(keep[:, UP_A:], got[:, UP_A:], False)],
        axis=2,
    )
    keep, got = settle(scatter_z(fours), core)
    grad_up = join(core, keep[:, :1536], got[:, :1536], 1)
    grad_out_w = join(core, keep[:, 1536:], got[:, 1536:], 1)

    dq, own, other = attend_back(scalars, query, grad_heads, lse, kv, kv_other)
    both = add_low(own, trade(other, CORE))
    joined = jnp.concatenate([dq, both[0], both[1]], axis=1)
    away, keep = weight_grad(scalars, 3, ((normed_one, joined, 0, 3),))
    fours = scatter_direct(keep, trade(away, CORE))
    grad_qkv = join(core, *settle(scatter_z(fours), core), 1)
    grad_start, payload = project_back(
        scalars, joined, tokens_here, grad_mid, vec, mid_sums, up_sums,
        qkv_pieces,
    )
    grad_tokens = swap_out(grad_start)
    final = exchange(payload)
    summed = jnp.sum(final[:, :12], axis=0)
    hit = (times[None, :] == levels[:, None]).astype(F32)
    grad_table = jnp.dot(hit, final[:, 12], precision=lax.Precision.HIGHEST)
    return (
        block_out[None],
        grad_tokens[None],
        summed[0],
        summed[1],
        grad_qkv,
        summed[2],
        summed[3],
        grad_out_w,
        summed[4],
        summed[5],
        summed[6],
        grad_up,
        summed[8:].reshape(96),
        grad_down,
        summed[7],
        grad_table,
    )


def solution(mesh):
    quick = mesh.shape["seq"] == 2 and mesh.shape["dp"] == 16
    return jax.shard_map(
        quick_shards if quick else shards,
        mesh=mesh,
        in_specs=(
            P("dp", "seq", None),
            P("dp"),
            P("dp", None),
            P("dp", "seq", None),
            P(AXES),
            P(AXES),
            P(AXES, None),
            P(AXES),
            P(AXES),
            P(AXES, None),
            P(AXES),
            P(AXES),
            P(AXES),
            P(AXES, None),
            P(AXES),
            P(AXES, None),
            P(AXES),
            P(None, AXES),
        ),
        out_specs=(
            P("dp", "seq", None),
            P("dp", "seq", None),
            P(AXES),
            P(AXES),
            P(AXES, None),
            P(AXES),
            P(AXES),
            P(AXES, None),
            P(AXES),
            P(AXES),
            P(AXES),
            P(AXES, None),
            P(AXES),
            P(AXES, None),
            P(AXES),
            P(None, AXES),
        ),
        check_vma=False,
    )
```

```python
import jax
import jax.numpy as jnp
from jax import lax
from jax.experimental import pallas as pl
from jax.experimental.pallas import tpu as pltpu
from jax.sharding import PartitionSpec as P


D = 768
HEADS = 12
HD = 64
TSTEPS = 1000
PIC = 256
NPIC = 2


epsilon = 1e-05


def layer_norm(values, gain, shift):
    average = jnp.mean(values, axis=-1, keepdims=True)
    centred = values - average
    spread = jnp.mean(centred * centred, axis=-1, keepdims=True)
    return centred * lax.rsqrt(spread + epsilon) * gain + shift


def piece_label(starts, places):
    inside = (places[None, None, :] >= starts[:, :, None]) & (
        places[None, None, :] < starts[:, :, None] + PIC
    )
    number = jnp.arange(1, NPIC + 1, dtype=jnp.int32)
    return jnp.sum(inside.astype(jnp.int32) * number[None, :, None], axis=1)


def visible_mask(starts, query_pos, key_pos):
    label_query = piece_label(starts, query_pos)
    label_key = piece_label(starts, key_pos)
    causal = query_pos[:, None] >= key_pos[None, :]
    return causal[None] | (label_query[:, :, None] == label_key[:, None, :]) & (
        label_query[:, :, None] > 0
    )


def dense(left, right):
    return jnp.dot(left, right, preferred_element_type=jnp.float32)


def dense_left(left, right):
    return lax.dot_general(
        left, right, (((0,), (0,)), ((), ())), preferred_element_type=jnp.float32
    )


def dense_right(left, right):
    return lax.dot_general(
        left, right, (((1,), (1,)), ((), ())), preferred_element_type=jnp.float32
    )


def head_slice(array, index):
    return lax.dynamic_slice_in_dim(array, index * HD, HD, 2)


def merge_heads(stacked):
    head_count, seq_count, row_count, head_size = stacked.shape
    return jnp.transpose(stacked, (1, 2, 0, 3)).reshape(
        seq_count, row_count, head_count * head_size
    )


def shards(
    tokens,
    timesteps,
    starts,
    cotangent,
    ln1_gain,
    ln1_bias,
    w_qkv,
    bias_query,
    bias_value,
    w_out,
    bias_out,
    ln2_gain,
    ln2_bias,
    w_up,
    bias_up,
    w_down,
    bias_down,
    time_table,
):
    gathered = (
        lax.all_gather(ln1_gain, AXES, axis=0, tiled=True),
        lax.all_gather(ln1_bias, AXES, axis=0, tiled=True),
        lax.all_gather(w_qkv, AXES, axis=0, tiled=True),
        lax.all_gather(bias_query, AXES, axis=0, tiled=True),
        lax.all_gather(bias_value, AXES, axis=0, tiled=True),
        lax.all_gather(w_out, AXES, axis=0, tiled=True),
        lax.all_gather(bias_out, AXES, axis=0, tiled=True),
        lax.all_gather(ln2_gain, AXES, axis=0, tiled=True),
        lax.all_gather(ln2_bias, AXES, axis=0, tiled=True),
        lax.all_gather(w_up, AXES, axis=0, tiled=True),
        lax.all_gather(bias_up, AXES, axis=0, tiled=True),
        lax.all_gather(w_down, AXES, axis=0, tiled=True),
        lax.all_gather(bias_down, AXES, axis=0, tiled=True),
        lax.all_gather(time_table, AXES, axis=1, tiled=True),
    )
    (
        gain_one,
        shift_one,
        qkv_full,
        query_shift,
        value_shift,
        out_full,
        out_shift,
        gain_two,
        shift_two,
        up_full,
        up_shift,
        down_full,
        down_shift,
        table_full,
    ) = gathered
    seq_count, row_count, model_width = tokens.shape
    flat_rows = seq_count * row_count
    scale = HD ** (-0.5)
    levels = jnp.arange(TSTEPS, dtype=jnp.int32)
    onehot = timesteps[:, None] == levels[None, :]
    embed = dense(onehot.astype(jnp.bfloat16), table_full)
    start_sum = (tokens.astype(jnp.float32) + embed[:, None, :]).reshape(flat_rows, model_width)
    norm_one, pull_one = jax.vjp(
        layer_norm, start_sum, gain_one.astype(jnp.float32), shift_one.astype(jnp.float32)
    )
    normed_one = norm_one.astype(jnp.bfloat16)
    joined = dense(normed_one, qkv_full)
    query = (
        (joined[:, :D] + query_shift.astype(jnp.float32))
        .astype(jnp.bfloat16)
        .reshape(seq_count, row_count, D)
    )
    keys = joined[:, D : 2 * D].astype(jnp.bfloat16).reshape(seq_count, row_count, D)
    values = (
        (joined[:, 2 * D :] + value_shift.astype(jnp.float32))
        .astype(jnp.bfloat16)
        .reshape(seq_count, row_count, D)
    )
    key_all, value_all = (
        lax.all_gather(keys, "seq", axis=1, tiled=True),
        lax.all_gather(values, "seq", axis=1, tiled=True),
    )
    full_len = key_all.shape[1]
    query_pos = lax.axis_index("seq") * row_count + jnp.arange(row_count, dtype=jnp.int32)
    every_pos = jnp.arange(full_len, dtype=jnp.int32)
    allowed = visible_mask(starts, query_pos, every_pos)

    def head_forward(index):
        query_head = head_slice(query, index)
        key_head = head_slice(key_all, index)
        value_head = head_slice(value_all, index)
        scores = scale * jnp.einsum(
            "sre,ske->srk", query_head, key_head, preferred_element_type=jnp.float32
        )
        scores = jnp.where(allowed, scores, -1e30)
        top = jnp.max(scores, axis=-1, keepdims=True)
        expo = jnp.exp(scores - top)
        total = jnp.sum(expo, axis=-1, keepdims=True)
        probs = expo / total
        result = jnp.einsum(
            "srk,ske->sre",
            probs.astype(jnp.bfloat16),
            value_head,
            preferred_element_type=jnp.float32,
        )
        return (result, top[..., 0] + jnp.log(total[..., 0]))

    head_out, log_total = lax.map(head_forward, jnp.arange(HEADS, dtype=jnp.int32))
    heads_out = merge_heads(head_out).astype(jnp.bfloat16).reshape(flat_rows, D)
    mid = start_sum + dense(heads_out, out_full) + out_shift.astype(jnp.float32)
    norm_two, pull_two = jax.vjp(
        layer_norm, mid, gain_two.astype(jnp.float32), shift_two.astype(jnp.float32)
    )
    normed_two = norm_two.astype(jnp.bfloat16)
    up_pre = dense(normed_two, up_full) + up_shift.astype(jnp.float32)
    act_value, pull_act = jax.vjp(jax.nn.gelu, up_pre)
    act = act_value.astype(jnp.bfloat16)
    block_out = (mid + dense(act, down_full) + down_shift.astype(jnp.float32)).astype(jnp.bfloat16)
    qkv_back, out_back, up_back, down_back = (
        lax.all_gather(w_qkv, AXES, axis=0, tiled=True),
        lax.all_gather(w_out, AXES, axis=0, tiled=True),
        lax.all_gather(w_up, AXES, axis=0, tiled=True),
        lax.all_gather(w_down, AXES, axis=0, tiled=True),
    )
    grad_mlp = cotangent.reshape(flat_rows, D)
    grad_down = dense_left(act, grad_mlp)
    grad_down_shift = jnp.sum(grad_mlp.astype(jnp.float32), axis=0)
    grad_act = dense_right(grad_mlp, down_back)
    (grad_up_pre,) = pull_act(grad_act)
    grad_up_low = grad_up_pre.astype(jnp.bfloat16)
    grad_up = dense_left(normed_two, grad_up_low)
    grad_up_shift = jnp.sum(grad_up_low.astype(jnp.float32), axis=0)
    grad_norm_two = dense_right(grad_up_low, up_back)
    grad_mid_norm, grad_gain_two, grad_shift_two = pull_two(grad_norm_two)
    grad_mid = cotangent.reshape(flat_rows, D).astype(jnp.float32) + grad_mid_norm
    grad_attn = grad_mid.astype(jnp.bfloat16)
    grad_out_w = dense_left(heads_out, grad_attn)
    grad_out_shift = jnp.sum(grad_attn.astype(jnp.float32), axis=0)
    grad_heads = (
        dense_right(grad_attn, out_back).astype(jnp.bfloat16).reshape(seq_count, row_count, D)
    )
    key_back, value_back = (
        lax.all_gather(keys, "seq", axis=1, tiled=True),
        lax.all_gather(values, "seq", axis=1, tiled=True),
    )

    def query_side(index, log_head):
        query_head = head_slice(query, index)
        key_head = head_slice(key_back, index)
        value_head = head_slice(value_back, index)
        grad_head = head_slice(grad_heads, index)
        scores = scale * jnp.einsum(
            "sre,ske->srk", query_head, key_head, preferred_element_type=jnp.float32
        )
        scores = jnp.where(allowed, scores, -1e30)
        probs = jnp.exp(scores - log_head[..., None])
        grad_probs = jnp.einsum(
            "sre,ske->srk", grad_head, value_head, preferred_element_type=jnp.float32
        )
        delta = jnp.sum(probs * grad_probs, axis=-1, keepdims=True)
        grad_scores = (probs * (grad_probs - delta)).astype(jnp.bfloat16)
        grad_query_head = scale * jnp.einsum(
            "srk,ske->sre", grad_scores, key_head, preferred_element_type=jnp.float32
        )
        return (probs, grad_scores, delta[..., 0], grad_query_head)

    def query_only(inputs):
        index, log_head = inputs
        _, _, delta, grad_query_head = query_side(index, log_head)
        return (grad_query_head, delta)

    grad_query_heads, delta_heads = lax.map(
        query_only, (jnp.arange(HEADS, dtype=jnp.int32), log_total)
    )
    query_every, grad_every, log_every, delta_every = (
        lax.all_gather(query, "seq", axis=1, tiled=True),
        lax.all_gather(grad_heads, "seq", axis=1, tiled=True),
        lax.all_gather(log_total.astype(jnp.bfloat16), "seq", axis=2, tiled=True).astype(
            log_total.dtype
        ),
        lax.all_gather(delta_heads.astype(jnp.bfloat16), "seq", axis=2, tiled=True).astype(
            delta_heads.dtype
        ),
    )
    key_allowed = visible_mask(starts, every_pos, query_pos)

    def key_side(inputs):
        index, log_head, delta_head = inputs
        query_head = head_slice(query_every, index)
        grad_head = head_slice(grad_every, index)
        key_head = head_slice(keys, index)
        value_head = head_slice(values, index)
        scores = scale * jnp.einsum(
            "sqe,ske->sqk", query_head, key_head, preferred_element_type=jnp.float32
        )
        scores = jnp.where(key_allowed, scores, -1e30)
        probs = jnp.exp(scores - log_head[..., None])
        grad_probs = jnp.einsum(
            "sqe,ske->sqk", grad_head, value_head, preferred_element_type=jnp.float32
        )
        grad_scores = (probs * (grad_probs - delta_head[..., None])).astype(jnp.bfloat16)
        grad_key_head = scale * jnp.einsum(
            "sqk,sqe->ske", grad_scores, query_head, preferred_element_type=jnp.float32
        )
        grad_value_head = jnp.einsum(
            "sqk,sqe->ske",
            probs.astype(jnp.bfloat16),
            grad_head,
            preferred_element_type=jnp.float32,
        )
        return (grad_key_head, grad_value_head)

    grad_key_heads, grad_value_heads = lax.map(
        key_side, (jnp.arange(HEADS, dtype=jnp.int32), log_every, delta_every)
    )
    grad_key_own = merge_heads(grad_key_heads)
    grad_value_own = merge_heads(grad_value_heads)
    grad_query_low = merge_heads(grad_query_heads).astype(jnp.bfloat16).reshape(flat_rows, D)
    grad_key_low = grad_key_own.astype(jnp.bfloat16).reshape(flat_rows, D)
    grad_value_low = grad_value_own.astype(jnp.bfloat16).reshape(flat_rows, D)
    grad_joined = jnp.concatenate([grad_query_low, grad_key_low, grad_value_low], axis=1)
    grad_qkv = dense_left(normed_one, grad_joined)
    grad_query_shift = jnp.sum(grad_query_low.astype(jnp.float32), axis=0)
    grad_value_shift = jnp.sum(grad_value_low.astype(jnp.float32), axis=0)
    grad_norm_one = dense_right(grad_joined, qkv_back)
    grad_start_norm, grad_gain_one, grad_shift_one = pull_one(grad_norm_one)
    grad_start = grad_mid + grad_start_norm
    grad_tokens = grad_start.astype(jnp.bfloat16).reshape(seq_count, row_count, D)
    seq_sums = jnp.sum(grad_start.reshape(seq_count, row_count, D), axis=1)
    every_sums, every_times = (
        lax.all_gather(seq_sums, AXES, axis=0, tiled=True),
        lax.all_gather(timesteps, AXES, axis=0, tiled=True),
    )
    own_width = D // lax.axis_size(AXES)
    own_sums = lax.dynamic_slice_in_dim(
        every_sums, lax.axis_index(AXES) * own_width, own_width, 1
    )
    every_onehot = (every_times[None, :] == levels[:, None]).astype(jnp.float32)
    grad_table = jnp.dot(every_onehot, own_sums, precision=lax.Precision.HIGHEST)
    summed = (
        lax.psum_scatter(grad_gain_one, AXES, scatter_dimension=0, tiled=True),
        lax.psum_scatter(grad_shift_one, AXES, scatter_dimension=0, tiled=True),
        lax.psum_scatter(grad_qkv, AXES, scatter_dimension=0, tiled=True),
        lax.psum_scatter(grad_query_shift, AXES, scatter_dimension=0, tiled=True),
        lax.psum_scatter(grad_value_shift, AXES, scatter_dimension=0, tiled=True),
        lax.psum_scatter(grad_out_w, AXES, scatter_dimension=0, tiled=True),
        lax.psum_scatter(grad_out_shift, AXES, scatter_dimension=0, tiled=True),
        lax.psum_scatter(grad_gain_two, AXES, scatter_dimension=0, tiled=True),
        lax.psum_scatter(grad_shift_two, AXES, scatter_dimension=0, tiled=True),
        lax.psum_scatter(grad_up, AXES, scatter_dimension=0, tiled=True),
        lax.psum_scatter(grad_up_shift, AXES, scatter_dimension=0, tiled=True),
        lax.psum_scatter(grad_down, AXES, scatter_dimension=0, tiled=True),
        lax.psum_scatter(grad_down_shift, AXES, scatter_dimension=0, tiled=True),
    )
    return (
        block_out.reshape(seq_count, row_count, D),
        grad_tokens,
        summed[0],
        summed[1],
        summed[2],
        summed[3],
        summed[4],
        summed[5],
        summed[6],
        summed[7],
        summed[8],
        summed[9],
        summed[10],
        summed[11],
        summed[12],
        grad_table,
    )


AXES = ("seq", "dp")
CORE, Y, Z0, Z1, X = 1, 2, 4, 8, 16
DEVICES = 32
QUARTER = 256
ROWS = 512
FF = 3072
TILE = 768
WIDE = 384
MIB = 2**20
F32 = jnp.float32
LOW = jnp.bfloat16

Z_MASKS = (0, Z0, Z1, Z0 | Z1)
FAR_FIRST = (0, Z1, Z0, Z0 | Z1)


def chip_masks(middle, last, z_masks):
    return tuple((xy | z) >> 1 for xy in (0, middle, last, X | Y) for z in z_masks)


X_LAST, Y_LAST = chip_masks(Y, X, Z_MASKS), chip_masks(X, Y, Z_MASKS)
DOWN_X_LAST, DOWN_Y_LAST = chip_masks(Y, X, FAR_FIRST), chip_masks(X, Y, FAR_FIRST)


def send(array, pairs):
    return lax.ppermute(array, AXES, pairs)


def trade(array, mask):
    return send(array, [(i, i ^ mask) for i in range(DEVICES)])


def exchange(array):
    return lax.all_to_all(array, AXES, 0, 0, tiled=True)


def join(bit, own, other, axis):
    return jnp.where(
        bit == 0,
        jnp.concatenate([own, other], axis=axis),
        jnp.concatenate([other, own], axis=axis),
    )


def spot():
    x = lax.axis_index("seq")
    dp = lax.axis_index("dp")
    return x, dp >> 2, (dp >> 1) & 1, dp & 1


def hop_pairs(first):
    pairs = []
    for base in range(0, 16, 2):
        if first:
            moves = (((0, 0), (0, 1)), ((0, 1), (1, 0)), ((1, 0), (0, 0)))
        else:
            moves = (((1, 0), (0, 1)), ((1, 1), (1, 0)), ((0, 1), (1, 1)))
        for (sx, sc), (tx, tc) in moves:
            pairs.append((sx * 16 + base + sc, tx * 16 + base + tc))
    return pairs


def corners():
    x, _, _, core = spot()
    return (x == 0) & (core == 0), (x == 1) & (core == 1)


def swap_in(array):
    first, last = corners()
    front, back = array[:QUARTER], array[QUARTER:]
    one = send(jnp.where(first, back, front), hop_pairs(True))
    two = send(jnp.where(last, front, back), hop_pairs(False))
    low = jnp.where(first, front, jnp.where(last, two, one))
    high = jnp.where(first, one, jnp.where(last, back, two))
    return jnp.concatenate([low, high], axis=0)


def swap_out(array):
    first, last = corners()
    low, high = array[:QUARTER], array[QUARTER:]
    back_pairs = lambda which: [(t, s) for s, t in hop_pairs(which)]
    one = send(jnp.where(first, high, low), back_pairs(True))
    two = send(jnp.where(last, low, high), back_pairs(False))
    front = jnp.where(first, low, jnp.where(last, two, one))
    back = jnp.where(first, one, jnp.where(last, high, two))
    return jnp.concatenate([front, back], axis=0)


def gather_z(block):
    got = [trade(block, mask) for mask in Z_MASKS[1:]]
    return jnp.stack([block] + got, axis=0)


def grow(blocks, mask):
    return jnp.concatenate([blocks, trade(blocks, mask)], axis=0)


def both_cores(pieces):
    return tuple(pieces) + tuple(trade(p, CORE) for p in pieces)


def add_low(left, right):
    return (left.astype(F32) + right.astype(F32)).astype(LOW)


def scatter_two(keep, got, x_first):
    n = keep.shape[-1]
    keep, got = (array.reshape(2, 4, 2, -1, n) for array in (keep, got))
    if x_first:
        away = trade(add_low(keep[1], got[1]), X)
        part = lambda y: add_low(add_low(keep[0, :, y], got[0, :, y]), away[:, y])
    else:
        away = trade(add_low(keep[:, :, 1], got[:, :, 1]), Y)
        part = lambda x: add_low(add_low(keep[x, :, 0], got[x, :, 0]), away[x])
    last = trade(part(1), Y if x_first else X)
    return add_low(part(0), last)


def scatter_direct(keep, got):
    n = keep.shape[-1]
    cube = lambda array: array.reshape(2, 4, 2, -1, n)
    keep, got = cube(keep), cube(got)
    total = keep[0, :, 0].astype(F32) + got[0, :, 0].astype(F32)
    for mask, a, b in ((Y, 0, 1), (X, 1, 0), (X | Y, 1, 1)):
        away = trade(add_low(keep[a, :, b], got[a, :, b]), mask)
        total = total + away.astype(F32)
    return total.astype(LOW)


def scatter_z(fours):
    total = fours[0].astype(F32)
    for place, mask in enumerate(Z_MASKS[1:], 1):
        total = total + trade(fours[place], mask).astype(F32)
    return total


def scatter_z_two(fours):
    fours = fours.reshape((2, 2) + fours.shape[1:])
    away = trade(fours[:, 1], Z0)
    got = trade(add_low(fours[1, 0], away[1]), Z1)
    return add_low(fours[0, 0], away[0]).astype(F32) + got.astype(F32)


def settle(block, core):
    keep = lax.dynamic_slice_in_dim(block, core * 24, 24, 0)
    away = lax.dynamic_slice_in_dim(block, (1 - core) * 24, 24, 0)
    return keep, trade(away, CORE)


def dot_nt(left, right):
    return lax.dot_general(
        left, right, (((1,), (1,)), ((), ())), preferred_element_type=F32
    )


def dot_nn(left, right):
    return lax.dot_general(
        left, right, (((1,), (0,)), ((), ())), preferred_element_type=F32
    )


def inside_piece(place, start):
    return (place >= start) & (place < start + PIC)


def fill_bias(scalars, low_bias, high_bias):
    core, first, second = scalars[1], scalars[3], scalars[4]

    def fill(ref, chunk, key_start, query_start):
        shape = (QUARTER, QUARTER)
        key = key_start + lax.broadcasted_iota(jnp.int32, shape, 0)
        query = query_start + lax.broadcasted_iota(jnp.int32, shape, 1)
        seen = (
            (key <= query)
            | (inside_piece(key, first) & inside_piece(query, first))
            | (inside_piece(key, second) & inside_piece(query, second))
        )
        ref[pl.ds(chunk * QUARTER, QUARTER), :] = jnp.where(seen, 0.0, -1e30)

    mine, theirs = core * QUARTER, (1 - core) * QUARTER
    fill(low_bias, 0, mine, mine)
    fill(low_bias, 1, theirs, mine)
    half = 2 * QUARTER
    fill(high_bias, 0, mine, half + mine)
    fill(high_bias, 1, half + mine, half + mine)
    fill(high_bias, 2, theirs, half + mine)
    fill(high_bias, 3, half + theirs, half + mine)


def head_lanes(array, head):
    lane = lax.broadcasted_iota(jnp.int32, array.shape, 1)
    return jnp.where((lane >= HD) == (head == 1), array, jnp.zeros_like(array))


def key_sets(own, other):
    high = jnp.concatenate([own[...], other[...]], axis=0)
    low = jnp.concatenate([own[:QUARTER], other[:QUARTER]], axis=0)
    return low, high


def masked(scores, bias, part):
    if part == 0:
        return scores + bias[...]
    chunks = [scores[k * QUARTER : (k + 1) * QUARTER] for k in range(4)]
    for k in (1, 3):
        chunks[k] = chunks[k] + bias[k * QUARTER : (k + 1) * QUARTER]
    return jnp.concatenate(chunks, axis=0)


def forward_kernel(scalars, q, k_own, k_other, v_own, v_other, out, lse, low_bias, high_bias):
    @pl.when(pl.program_id(0) == 0)
    def _():
        fill_bias(scalars, low_bias, high_bias)

    scale = HD ** (-0.5)
    keys, values = key_sets(k_own, k_other), key_sets(v_own, v_other)
    for part, bias in enumerate((low_bias, high_bias)):
        key, value_t = keys[part], values[part].T
        rows = pl.ds(part * QUARTER, QUARTER)
        query = q[rows, :] * jnp.bfloat16(scale)
        tops = []
        for head in range(2):
            scores = masked(dot_nt(key, head_lanes(query, head)), bias, part)
            top = jnp.max(scores, axis=0, keepdims=True)
            expo = jnp.exp(scores - top)
            total = jnp.sum(expo, axis=0, keepdims=True)
            mixed = dot_nn(value_t[head * HD : (head + 1) * HD], expo.astype(LOW))
            tops.append(mixed / total)
            lse[0, pl.ds(head, 1), rows] = top + jnp.log(total)
        both = jnp.concatenate(tops, axis=0)
        out[rows, :] = both.T.astype(LOW)


def backward_kernel(
    scalars, q, grad, lse, k_own, k_other, v_own, v_other,
    dq, own, other, low_bias, high_bias,
):
    @pl.when(pl.program_id(0) == 0)
    def _():
        fill_bias(scalars, low_bias, high_bias)

    scale = HD ** (-0.5)
    keys, values = key_sets(k_own, k_other), key_sets(v_own, v_other)
    sums = []
    for part, bias in enumerate((low_bias, high_bias)):
        key, value = keys[part], values[part]
        key_t = key.T
        rows = pl.ds(part * QUARTER, QUARTER)
        query = q[rows, :] * jnp.bfloat16(scale)
        grad_out = grad[rows, :]
        grad_query, grad_key, grad_value = [], 0.0, 0.0
        for head in range(2):
            query_head = head_lanes(query, head)
            grad_head = head_lanes(grad_out, head)
            scores = masked(dot_nt(key, query_head), bias, part)
            probs = jnp.exp(scores - lse[0, pl.ds(head, 1), rows])
            grad_probs = dot_nt(value, grad_head)
            delta = jnp.sum(probs * grad_probs, axis=0, keepdims=True)
            grad_scores = (probs * (grad_probs - delta)).astype(LOW)
            grad_value += dot_nn(probs.astype(LOW), grad_head)
            grad_key += dot_nn(grad_scores, query_head)
            grad_query.append(
                dot_nn(key_t[head * HD : (head + 1) * HD], grad_scores) * scale
            )
        dq[rows, :] = jnp.concatenate(grad_query, axis=0).T.astype(LOW)
        sums.append((grad_key, grad_value))
    for which in range(2):
        low, high = sums[0][which], sums[1][which]
        own[which, :QUARTER] = (low[:QUARTER] + high[:QUARTER]).astype(LOW)
        own[which, QUARTER:] = high[QUARTER : 2 * QUARTER].astype(LOW)
        other[which, :QUARTER] = (low[QUARTER:] + high[2 * QUARTER : 3 * QUARTER]).astype(LOW)
        other[which, QUARTER:] = high[3 * QUARTER :].astype(LOW)


PAIRS = HEADS // 2


PART = 3


def pair_block(skip=0):
    return pl.BlockSpec((ROWS, 2 * HD), lambda i, s: (0, i + skip))


def lse_block():
    return pl.BlockSpec((1, 2, ROWS), lambda i, s: (i, 0, 0))


def bias_scratch():
    return [
        pltpu.VMEM((2 * QUARTER, QUARTER), F32),
        pltpu.VMEM((4 * QUARTER, QUARTER), F32),
    ]


def cost(flops, size):
    return pl.CostEstimate(flops=flops, bytes_accessed=size, transcendentals=0)


def array(shape, dtype=LOW):
    return jax.ShapeDtypeStruct(shape, dtype)


def attend(scalars, q, kv, kv_other, part):
    skip = part * PART
    block = pair_block(skip)
    value = pair_block(skip + PAIRS)
    return pl.pallas_call(
        forward_kernel,
        grid_spec=pltpu.PrefetchScalarGridSpec(
            num_scalar_prefetch=1,
            grid=(PART,),
            in_specs=[block, block, block, value, value],
            out_specs=[pair_block(), lse_block()],
            scratch_shapes=bias_scratch(),
        ),
        out_shape=[array((ROWS, PART * 2 * HD)), array((PART, 2, ROWS), F32)],
        cost_estimate=cost(10**9, 2 * 10**6),
        compiler_params=pltpu.CompilerParams(vmem_limit_bytes=16 * MIB),
    )(scalars, q, kv, kv_other, kv, kv_other)


def attend_back(scalars, q, grad, lse, kv, kv_other):
    both = pl.BlockSpec((2, ROWS, 2 * HD), lambda i, s: (0, 0, i))
    return pl.pallas_call(
        backward_kernel,
        grid_spec=pltpu.PrefetchScalarGridSpec(
            num_scalar_prefetch=1,
            grid=(PAIRS,),
            in_specs=[pair_block()] * 2
            + [lse_block(), pair_block(), pair_block(), pair_block(PAIRS), pair_block(PAIRS)],
            out_specs=[pair_block(), both, both],
            scratch_shapes=bias_scratch(),
        ),
        out_shape=[array((ROWS, D)), array((2, ROWS, D)), array((2, ROWS, D))],
        cost_estimate=cost(2 * 10**10, 8 * 10**6),
        compiler_params=pltpu.CompilerParams(vmem_limit_bytes=18 * MIB),
        name="attend_back",
    )(scalars, q, grad, lse, kv, kv_other, kv, kv_other)


def fetch(jobs, sems):
    copies = [pltpu.make_async_copy(s, d, sems.at[i]) for i, (s, d) in enumerate(jobs)]
    for copy in copies:
        copy.start()
    return copies


def wait(copies):
    for copy in copies:
        copy.wait()


def placed(pieces, masks):
    return [
        (ref, j, masks[start + j])
        for ref, start in zip(pieces, range(0, 16, 16 // len(pieces)))
        for j in range(16 // len(pieces))
    ]


def column_jobs(scalars, own, other, target, masks, start, width, half, skip=0):
    chip, core = scalars[0], scalars[1]
    jobs = []
    for pieces, side in ((own, core), (other, 1 - core)):
        columns = pl.ds(pl.multiple_of(side * half + skip, 128), width)
        for ref, j, mask in placed(pieces, masks):
            rows = pl.ds(pl.multiple_of((chip ^ mask) * 48, 16), 48)
            jobs.append((ref.at[j, :, pl.ds(start, width)], target.at[rows, columns]))
    return jobs


def qkv_jobs(scalars, pieces, weight):
    return column_jobs(scalars, pieces[:4], pieces[4:], weight, X_LAST, 0, 1152, 1152)


UP_A = 1024


def up_jobs(scalars, pieces, w_up, w_out):
    a, b, a2, b2 = pieces[:2], pieces[2:4], pieces[4:6], pieces[6:]
    jobs = column_jobs(scalars, b, b2, w_out, Y_LAST, 1536 - UP_A, 384, 384)
    jobs += column_jobs(scalars, a, a2, w_up, X_LAST, 0, UP_A, 1536)
    return jobs + column_jobs(scalars, b, b2, w_up, Y_LAST, 0, 1536 - UP_A, 1536, UP_A)


def down_jobs(scalars, pieces, target):
    chip, core = scalars[0], scalars[1]
    jobs = []
    for k, (side, masks, half) in enumerate(
        (
            (core, DOWN_X_LAST, 0), (core, DOWN_Y_LAST, 1),
            (1 - core, DOWN_X_LAST, 0), (1 - core, DOWN_Y_LAST, 1),
        )
    ):
        for ref, j, mask in placed(pieces[2 * k : 2 * k + 2], masks):
            first = pl.multiple_of((chip ^ mask) * 192 + side * 96, 16)
            jobs.append((ref.at[j], target.at[pl.ds(first, 96), pl.ds(half * 384, 384)]))
    return jobs


CHUNK = 128


def by_rows(body):
    @pl.loop(0, ROWS // CHUNK)
    def _(step):
        body(pl.ds(pl.multiple_of(step * CHUNK, CHUNK), CHUNK))


def norm_parts(values):
    average = jnp.mean(values, axis=-1, keepdims=True)
    centred = values - average
    rate = lax.rsqrt(jnp.mean(centred * centred, axis=-1, keepdims=True) + epsilon)
    return centred * rate, rate


def norm_back(grad, normal, rate, gain):
    scaled = grad * gain
    return rate * (
        scaled
        - jnp.mean(scaled, axis=-1, keepdims=True)
        - normal * jnp.mean(scaled * normal, axis=-1, keepdims=True)
    )


def full(shape):
    return pl.BlockSpec(
        shape, lambda i, s: (0,) * len(shape), pipeline_mode=pl.Buffered(1)
    )


def anywhere():
    return pl.BlockSpec(memory_space=pl.ANY)


def spread(shape):
    column = lax.broadcasted_iota(jnp.int32, shape, len(shape) - 1)
    return column, column - column // 24 * 24


def project_kernel(scalars, tok, owned, *refs):
    pieces, (vec, normed, q, kv, weight, sems) = refs[:8], refs[8:]
    step = pl.program_id(0)

    @pl.when(step == 0)
    def _():
        copies = fetch(qkv_jobs(scalars, pieces, weight), sems)
        _, inner = spread((24, D))
        place = (inner == lax.broadcasted_iota(jnp.int32, (24, D), 0)).astype(LOW)
        wide = dot_nn(owned[...].reshape(DEVICES * 16, 24), place).reshape(DEVICES, 16, D)
        column, _ = spread((DEVICES, 16, D))
        mine = column // 24 == lax.broadcasted_iota(jnp.int32, (DEVICES, 16, D), 0)
        vec[...] = jnp.sum(jnp.where(mine, wide, 0.0), axis=0)

        def rows_of(rows):
            normal, _ = norm_parts(tok[rows, :].astype(F32) + vec[12:13, :])
            normed[rows, :] = (normal * vec[0:1, :] + vec[1:2, :]).astype(LOW)

        by_rows(rows_of)
        wait(copies)

    columns = pl.ds(pl.multiple_of(step * D, D), D)
    result = dot_nn(normed[...], weight[:, columns])

    @pl.when(step < 1)
    def _():
        q[...] = (result + vec[2:3, :]).astype(LOW)

    @pl.when(step == 1)
    def _():
        kv[...] = result.astype(LOW)

    @pl.when(step == 2)
    def _():
        kv[...] = (result + vec[3:4, :]).astype(LOW)


def project(scalars, tok, owned, pieces):
    return pl.pallas_call(
        project_kernel,
        grid_spec=pltpu.PrefetchScalarGridSpec(
            num_scalar_prefetch=1,
            grid=(3,),
            in_specs=[full((ROWS, D)), full((DEVICES, 16, 24))] + [anywhere()] * 8,
            out_specs=[
                full((16, D)),
                full((ROWS, D)),
                full((ROWS, D)),
                pl.BlockSpec((ROWS, D), lambda i, s: (0, jnp.maximum(i - 1, 0))),
            ],
            scratch_shapes=[pltpu.VMEM((D, 3 * D), LOW), pltpu.SemaphoreType.DMA((32,))],
        ),
        out_shape=[array((16, D), F32), array((ROWS, D)), array((ROWS, D)), array((ROWS, 2 * D))],
        cost_estimate=cost(2 * 10**9, 8 * 10**6),
        compiler_params=pltpu.CompilerParams(vmem_limit_bytes=18 * MIB),
        name="project",
    )(scalars, tok, owned, *pieces)


GELU = 0.7978845608028654


def mlp_up_kernel(scalars, heads, tok, vec, up_bias, *refs):
    pieces, (mid, normed, act, slope, w_up, w_out, sems) = refs[:8], refs[8:]
    step = pl.program_id(0)

    @pl.when(step == 0)
    def _():
        copies = fetch(up_jobs(scalars, pieces, w_up, w_out), sems)
        wait(copies[:32])
        mid[...] = dot_nn(heads[...], w_out[...])

        def rows_of(rows):
            total = tok[rows, :].astype(F32) + vec[12:13, :] + mid[rows, :] + vec[4:5, :]
            mid[rows, :] = total
            normal, _ = norm_parts(total)
            normed[rows, :] = (normal * vec[5:6, :] + vec[6:7, :]).astype(LOW)

        by_rows(rows_of)
        wait(copies[32:])

    columns = pl.ds(pl.multiple_of(step * TILE, TILE), TILE)
    v = dot_nn(normed[...], w_up[:, columns]) + up_bias[...]
    square = v * v
    inner = jnp.tanh(GELU * v * (1 + 0.044715 * square))
    half = 0.5 * (1 + inner)
    act[...] = (v * half).astype(LOW)
    slope[...] = (
        half + 0.5 * GELU * v * (1 - inner * inner) * (1 + 3 * 0.044715 * square)
    ).astype(LOW)


def mlp_up(scalars, heads, tok, vec, up_bias, pieces):
    tile = pl.BlockSpec((ROWS, TILE), lambda i, s: (0, i))
    return pl.pallas_call(
        mlp_up_kernel,
        grid_spec=pltpu.PrefetchScalarGridSpec(
            num_scalar_prefetch=1,
            grid=(FF // TILE,),
            in_specs=[
                full((ROWS, D)), full((ROWS, D)), full((16, D)),
                pl.BlockSpec((1, TILE), lambda i, s: (0, i)),
            ] + [anywhere()] * 8,
            out_specs=[full((ROWS, D)), full((ROWS, D)), tile, tile],
            scratch_shapes=[
                pltpu.VMEM((D, FF), LOW), pltpu.VMEM((D, D), LOW), pltpu.SemaphoreType.DMA((96,)),
            ],
        ),
        out_shape=[array((ROWS, D), F32), array((ROWS, D)), array((ROWS, FF)), array((ROWS, FF))],
        cost_estimate=cost(4 * 10**9, 16 * 10**6),
        compiler_params=pltpu.CompilerParams(vmem_limit_bytes=17 * MIB),
        name="mlp_up",
    )(scalars, heads, tok, vec, up_bias, *pieces)


def down_grad_kernel(scalars, act, cot, send, keep):
    chip, core = scalars[0], scalars[1]
    result = lax.dot_general(
        act[...], cot[...], (((0,), (0,)), ((), ())), preferred_element_type=F32
    )
    for index in range(2):
        place = (pl.program_id(0) * 2 + index) ^ chip
        rows = pl.ds(pl.multiple_of(place * 96, 16), 96)
        first = result[index * 192 : index * 192 + 96].astype(LOW)
        second = result[index * 192 + 96 : index * 192 + 192].astype(LOW)
        keep[rows, :] = jnp.where(core == 0, first, second)
        send[rows, :] = jnp.where(core == 0, second, first)


def down_grad(scalars, act, cot):
    return pl.pallas_call(
        down_grad_kernel,
        grid_spec=pltpu.PrefetchScalarGridSpec(
            num_scalar_prefetch=1,
            grid=(8,),
            in_specs=[pl.BlockSpec((ROWS, WIDE), lambda i, s: (0, i)), full((ROWS, D))],
            out_specs=[full((FF // 2, D))] * 2,
        ),
        out_shape=[array((FF // 2, D))] * 2,
        cost_estimate=cost(3 * 10**9, 9 * 10**6),
        compiler_params=pltpu.CompilerParams(vmem_limit_bytes=16 * MIB),
        name="down_grad",
    )(scalars, act, cot)


TILES = FF // TILE


def mlp_mid_kernel(scalars, act, slope, mid, cot, vec, *refs):
    down_pieces, up_pieces, refs = refs[:8], refs[8:16], refs[16:]
    out, grad_up, bias_sum, grad_mid, grad_attn, grad_heads, sums = refs[:7]
    w_down, w_up, w_out, held, total, down_sems, up_sems = refs[7:]
    step = pl.program_id(0)
    down = lambda: [
        pltpu.make_async_copy(s, d, down_sems.at[i])
        for i, (s, d) in enumerate(down_jobs(scalars, down_pieces, w_down))
    ]
    up = lambda: [
        pltpu.make_async_copy(s, d, up_sems.at[i])
        for i, (s, d) in enumerate(up_jobs(scalars, up_pieces, w_up, w_out))
    ]

    @pl.when(step == 0)
    def _():
        copies = down()
        for copy in copies + up():
            copy.start()
        total[...] = mid[...] + vec[7:8, :]
        wait(copies)

    @pl.when(step < TILES)
    def _():
        rows = pl.ds(pl.multiple_of(step * TILE, TILE), TILE)
        part = w_down[rows, :]
        total[...] += dot_nn(act[...], part)
        grad = (dot_nt(cot[...], part) * slope[...].astype(F32)).astype(LOW)
        grad_up[...] = grad
        held[step] = grad
        bias_sum[...] = jnp.sum(grad.astype(F32), axis=0, keepdims=True)

    @pl.when(step == TILES)
    def _():
        out[...] = total[...].astype(LOW)
        total[...] = jnp.zeros_like(total)
        wait(up())

    @pl.when(step >= TILES)
    def _():
        local = step - TILES
        columns = pl.ds(pl.multiple_of(local * TILE, TILE), TILE)
        total[...] += dot_nt(held[local], w_up[:, columns])

    @pl.when(step == 2 * TILES - 1)
    def _():
        sums[...] = jnp.zeros_like(sums)

        def rows_of(rows):
            normal, rate = norm_parts(mid[rows, :])
            grad = total[rows, :]
            outer = cot[rows, :].astype(F32)
            back = outer + norm_back(grad, normal, rate, vec[5:6, :])
            grad_mid[rows, :] = back
            low = back.astype(LOW)
            grad_attn[rows, :] = low
            sums[0:1, :] += jnp.sum(grad * normal, axis=0, keepdims=True)
            sums[1:2, :] += jnp.sum(grad, axis=0, keepdims=True)
            sums[2:3, :] += jnp.sum(low.astype(F32), axis=0, keepdims=True)
            sums[3:4, :] += jnp.sum(outer, axis=0, keepdims=True)

        by_rows(rows_of)
        grad_heads[...] = dot_nt(grad_attn[...], w_out[...]).astype(LOW)


def mlp_mid(scalars, act, slope, mid, cot, vec, down_pieces, up_pieces):
    index = lambda i, s: (0, jnp.minimum(i, TILES - 1))
    tile = pl.BlockSpec((ROWS, TILE), index)
    return pl.pallas_call(
        mlp_mid_kernel,
        grid_spec=pltpu.PrefetchScalarGridSpec(
            num_scalar_prefetch=1,
            grid=(2 * TILES,),
            in_specs=[tile, tile, full((ROWS, D)), full((ROWS, D)), full((16, D))]
            + [anywhere()] * 16,
            out_specs=[full((ROWS, D)), tile, pl.BlockSpec((1, TILE), index)]
            + [full((ROWS, D))] * 3
            + [full((8, D))],
            scratch_shapes=[
                pltpu.VMEM((FF, D), LOW), pltpu.VMEM((D, FF), LOW), pltpu.VMEM((D, D), LOW),
                pltpu.VMEM((TILES, ROWS, TILE), LOW), pltpu.VMEM((ROWS, D), F32),
                pltpu.SemaphoreType.DMA((64,)), pltpu.SemaphoreType.DMA((96,)),
            ],
        ),
        out_shape=[
            array((ROWS, D)), array((ROWS, FF)), array((1, FF), F32), array((ROWS, D), F32),
            array((ROWS, D)), array((ROWS, D)), array((8, D), F32),
        ],
        cost_estimate=cost(10**10, 30 * 10**6),
        compiler_params=pltpu.CompilerParams(vmem_limit_bytes=29 * MIB),
        name="mlp_mid",
    )(scalars, act, slope, mid, cot, vec, *down_pieces, *up_pieces)


def place_rows(result, target, chip):
    for index in range(16):
        rows = pl.ds(pl.multiple_of((index ^ chip) * 48, 16), 48)
        target[rows, :] = result[index * 48 : index * 48 + 48].astype(LOW)


def weight_grad_kernel(tiles, lefts, scalars, *refs):
    left_refs, right_refs = refs[: len(lefts)], refs[len(lefts) : 2 * len(lefts)]
    send, keep = refs[2 * len(lefts) : 2 * len(lefts) + 2]
    flipped = refs[2 * len(lefts) + 2 :]
    step = pl.program_id(0)
    chip = scalars[0]

    @pl.when(step == 0)
    def _():
        for left, flip in zip(left_refs, flipped):
            flip[...] = left[...].T

    local = jnp.where(step < tiles, step, step - tiles)
    for which, (first, last) in enumerate(lefts):

        @pl.when((local >= first) & (local < last))
        def _(which=which):
            result = dot_nn(flipped[which][...], right_refs[which][...])

            @pl.when(step < tiles)
            def _():
                place_rows(result, send, chip)

            @pl.when(step >= tiles)
            def _():
                place_rows(result, keep, chip)


def weight_grad(scalars, tiles, parts):
    def right_block(first, count):
        def index(i, s):
            local = jnp.clip(jnp.where(i < tiles, i, i - tiles) - first, 0, count - 1)
            side = jnp.where(i < tiles, 1 - s[1], s[1])
            return (0, side * count + local)

        return pl.BlockSpec((ROWS, WIDE), index)

    lefts = tuple((first, first + count) for _, _, first, count in parts)
    return pl.pallas_call(
        lambda *refs: weight_grad_kernel(tiles, lefts, *refs),
        grid_spec=pltpu.PrefetchScalarGridSpec(
            num_scalar_prefetch=1,
            grid=(2 * tiles,),
            in_specs=[full((ROWS, D))] * len(parts)
            + [right_block(first, count) for _, _, first, count in parts],
            out_specs=[
                pl.BlockSpec((D, WIDE), lambda i, s: (0, jnp.minimum(i, tiles - 1))),
                pl.BlockSpec((D, WIDE), lambda i, s: (0, jnp.maximum(i - tiles, 0))),
            ],
            scratch_shapes=[pltpu.VMEM((D, ROWS), LOW)] * len(parts),
        ),
        out_shape=[array((D, tiles * WIDE))] * 2,
        cost_estimate=cost(tiles * 6 * 10**8, 10 * 10**6),
        compiler_params=pltpu.CompilerParams(vmem_limit_bytes=18 * MIB),
    )(scalars, *[p[0] for p in parts], *[p[1] for p in parts])


def project_back_kernel(scalars, joined, tok, grad_mid, vec, mid_sums, up_sums, *refs):
    pieces, (out, payload, weight, total, sums, column_sums, sems) = refs[:8], refs[8:]
    step = pl.program_id(0)

    @pl.when(step == 0)
    def _():
        copies = fetch(qkv_jobs(scalars, pieces, weight), sems)
        total[...] = jnp.zeros_like(total)
        wait(copies)

    columns = pl.ds(pl.multiple_of(step * D, D), D)
    total[...] += dot_nt(joined[...], weight[:, columns])
    column_sums[:, columns] = jnp.sum(joined[...].astype(F32), axis=0, keepdims=True)

    @pl.when(step == 2)
    def _():
        sums[...] = jnp.zeros_like(sums)

        def rows_of(rows):
            normal, rate = norm_parts(tok[rows, :].astype(F32) + vec[12:13, :])
            grad = total[rows, :]
            back = grad_mid[rows, :] + norm_back(grad, normal, rate, vec[0:1, :])
            out[rows, :] = back.astype(LOW)
            sums[0:1, :] += jnp.sum(grad * normal, axis=0, keepdims=True)
            sums[1:2, :] += jnp.sum(grad, axis=0, keepdims=True)
            sums[12:13, :] += jnp.sum(back, axis=0, keepdims=True)

        by_rows(rows_of)
        sums[2:3, :] = column_sums[:, :D]
        sums[3:4, :] = column_sums[:, 2 * D :]
        sums[4:5, :] = mid_sums[2:3, :]
        sums[5:7, :] = mid_sums[0:2, :]
        sums[7:8, :] = mid_sums[3:4, :]
        _, inner = spread((24, D))
        place = (inner == lax.broadcasted_iota(jnp.int32, (24, D), 0)).astype(F32)
        column, _ = spread((DEVICES, 16, D))
        mine = column // 24 == lax.broadcasted_iota(jnp.int32, (DEVICES, 16, D), 0)
        wide = jnp.where(mine, sums[...][None], 0.0).reshape(DEVICES * 16, D)
        narrow = lax.dot_general(
            wide, place, (((1,), (1,)), ((), ())),
            precision=lax.Precision.HIGHEST, preferred_element_type=F32,
        )
        payload[...] = narrow.reshape(DEVICES, 16, 24)
        column = lax.broadcasted_iota(jnp.int32, (DEVICES * 4, FF), 1)
        mine = column // 24 == lax.broadcasted_iota(jnp.int32, (DEVICES * 4, FF), 0)
        inner = lax.broadcasted_iota(jnp.int32, (24, FF), 1)
        inner = inner - inner // 24 * 24
        place = (inner == lax.broadcasted_iota(jnp.int32, (24, FF), 0)).astype(F32)
        narrow = lax.dot_general(
            jnp.where(mine, up_sums[...], 0.0), place, (((1,), (1,)), ((), ())),
            precision=lax.Precision.HIGHEST, preferred_element_type=F32,
        )
        payload[:, 8:12, :] = narrow.reshape(DEVICES, 4, 24)


def project_back(scalars, joined, tok, grad_mid, vec, mid_sums, up_sums, pieces):
    return pl.pallas_call(
        project_back_kernel,
        grid_spec=pltpu.PrefetchScalarGridSpec(
            num_scalar_prefetch=1,
            grid=(3,),
            in_specs=[
                pl.BlockSpec((ROWS, D), lambda i, s: (0, i)),
                full((ROWS, D)), full((ROWS, D)), full((16, D)), full((8, D)),
                full((1, FF)),
            ] + [anywhere()] * 8,
            out_specs=[full((ROWS, D)), full((DEVICES, 16, 24))],
            scratch_shapes=[
                pltpu.VMEM((D, 3 * D), LOW), pltpu.VMEM((ROWS, D), F32), pltpu.VMEM((16, D), F32),
                pltpu.VMEM((1, 3 * D), F32), pltpu.SemaphoreType.DMA((32,)),
            ],
        ),
        out_shape=[array((ROWS, D)), array((DEVICES, 16, 24), F32)],
        cost_estimate=cost(3 * 10**9, 12 * 10**6),
        compiler_params=pltpu.CompilerParams(vmem_limit_bytes=20 * MIB),
        name="project_back",
    )(scalars, joined, tok, grad_mid, vec, mid_sums, up_sums, *pieces)


def quick_shards(*arguments):
    return quick_step(*arguments)


def quick_step(
    tokens, timesteps, starts, cotangent, ln1_gain, ln1_bias, w_qkv, bias_query,
    bias_value, w_out, bias_out, ln2_gain, ln2_bias, w_up, bias_up, w_down,
    bias_down, time_table,
):
    x, z, y, core = spot()
    chip = x * 8 + z * 2 + y
    sequence = ((lax.axis_index("dp") >> 1) << 1) | x

    def half_of(rows):
        half = rows.shape[1] // 2
        return lax.dynamic_slice_in_dim(rows, core * half, half, 1)

    fours = gather_z(half_of(join(core, w_qkv, trade(w_qkv, CORE), 0)))
    qkv_pieces = both_cores([fours] + [trade(fours, m) for m in (Y, X, X | Y)])
    tokens_here = swap_in(tokens[0])
    up_shard, out_shard = trade(w_up, CORE), trade(w_out, CORE)
    rest = jnp.concatenate(
        [half_of(join(core, w_up, up_shard, 0)), half_of(join(core, w_out, out_shard, 0))],
        axis=1,
    )
    rest = gather_z(rest)
    up_a = grow(rest[:, :, :UP_A], Y)
    up_b = grow(rest[:, :, UP_A:], X)
    up_pieces = both_cores([up_a, trade(up_a, X), up_b, trade(up_b, Y)])
    cot = swap_in(cotangent[0])
    rest = grow(grow(w_down[None], Z1), Z0)
    down_a = grow(rest[:, :, :384], Y)
    down_b = grow(rest[:, :, 384:], X)
    down_pieces = both_cores([down_a, trade(down_a, X), down_b, trade(down_b, Y)])

    row = jnp.concatenate([timesteps, starts[0], jnp.zeros((5,), jnp.int32)])
    notes = exchange(jnp.broadcast_to(row, (DEVICES, 8)))
    times = jnp.broadcast_to(notes[:16, 0].reshape(8, 2).T[:, :, None], (2, 8, 2)).reshape(DEVICES)
    levels = jnp.arange(TSTEPS, dtype=jnp.int32)
    rows_of = dense((times[:, None] == levels[None, :]).astype(LOW), time_table).astype(LOW)
    vectors = (ln1_gain, ln1_bias, bias_query, bias_value, bias_out, ln2_gain, ln2_bias, bias_down)
    shared = jnp.concatenate(vectors + (bias_up,)).reshape(1, 12, 24)
    owned = jnp.concatenate(
        [jnp.broadcast_to(shared, (DEVICES, 12, 24)), rows_of[:, None], jnp.zeros((DEVICES, 3, 24), LOW)],
        axis=1,
    )
    owned = exchange(owned)
    up_bias = owned[:, 8:12].reshape(1, FF).astype(F32)
    own_starts = lax.dynamic_slice_in_dim(notes, sequence, 1, 0)[0, 1:3]
    scalars = jnp.concatenate([jnp.stack([chip, core, sequence]).astype(jnp.int32), own_starts])

    vec, normed_one, query, kv = project(scalars, tokens_here, owned, qkv_pieces)
    kv_other = trade(kv, CORE)
    parts = [attend(scalars, query, kv, kv_other, part) for part in range(PAIRS // PART)]
    heads_out = jnp.concatenate([part[0] for part in parts], axis=1)
    lse = jnp.concatenate([part[1] for part in parts], axis=0)
    mid, normed_two, act, slope = mlp_up(
        scalars, heads_out, tokens_here, vec, up_bias, up_pieces
    )

    away, keep = down_grad(scalars, act, cot)
    got = trade(away, CORE).reshape(16, 96, D)
    keep = keep.reshape(16, 96, D)
    fours = jnp.concatenate(
        [scatter_two(keep[:, :48], got[:, :48], True),
         scatter_two(keep[:, 48:], got[:, 48:], False)],
        axis=1,
    )
    grad_down = scatter_z_two(fours)

    out, grad_up_low, up_sums, grad_mid, grad_attn, grad_heads, mid_sums = mlp_mid(
        scalars, act, slope, mid, cot, vec, down_pieces, up_pieces
    )
    block_out = swap_out(out)
    away, keep = weight_grad(
        scalars, 5, ((normed_two, grad_up_low, 0, 4), (heads_out, grad_attn, 4, 1))
    )
    got = trade(away, CORE)
    fours = jnp.concatenate(
        [scatter_two(keep[:, :UP_A], got[:, :UP_A], True),
         scatter_two(keep[:, UP_A:], got[:, UP_A:], False)],
        axis=2,
    )
    keep, got = settle(scatter_z(fours), core)
    grad_up = join(core, keep[:, :1536], got[:, :1536], 1)
    grad_out_w = join(core, keep[:, 1536:], got[:, 1536:], 1)

    dq, own, other = attend_back(scalars, query, grad_heads, lse, kv, kv_other)
    both = add_low(own, trade(other, CORE))
    joined = jnp.concatenate([dq, both[0], both[1]], axis=1)
    away, keep = weight_grad(scalars, 3, ((normed_one, joined, 0, 3),))
    fours = scatter_direct(keep, trade(away, CORE))
    grad_qkv = join(core, *settle(scatter_z(fours), core), 1)
    grad_start, payload = project_back(
        scalars, joined, tokens_here, grad_mid, vec, mid_sums, up_sums,
        qkv_pieces,
    )
    grad_tokens = swap_out(grad_start)
    final = exchange(payload)
    summed = jnp.sum(final[:, :12], axis=0)
    hit = (times[None, :] == levels[:, None]).astype(F32)
    grad_table = jnp.dot(hit, final[:, 12], precision=lax.Precision.HIGHEST)
    return (
        block_out[None],
        grad_tokens[None],
        summed[0],
        summed[1],
        grad_qkv,
        summed[2],
        summed[3],
        grad_out_w,
        summed[4],
        summed[5],
        summed[6],
        grad_up,
        summed[8:].reshape(96),
        grad_down,
        summed[7],
        grad_table,
    )


def solution(mesh):
    quick = mesh.shape["seq"] == 2 and mesh.shape["dp"] == 16
    return jax.shard_map(
        quick_shards if quick else shards,
        mesh=mesh,
        in_specs=(
            P("dp", "seq", None),
            P("dp"),
            P("dp", None),
            P("dp", "seq", None),
            P(AXES),
            P(AXES),
            P(AXES, None),
            P(AXES),
            P(AXES),
            P(AXES, None),
            P(AXES),
            P(AXES),
            P(AXES),
            P(AXES, None),
            P(AXES),
            P(AXES, None),
            P(AXES),
            P(None, AXES),
        ),
        out_specs=(
            P("dp", "seq", None),
            P("dp", "seq", None),
            P(AXES),
            P(AXES),
            P(AXES, None),
            P(AXES),
            P(AXES),
            P(AXES, None),
            P(AXES),
            P(AXES),
            P(AXES),
            P(AXES, None),
            P(AXES),
            P(AXES, None),
            P(AXES),
            P(None, AXES),
        ),
        check_vma=False,
    )
```
